256 devices in a mesh: tm: 16 (over z, core), trans: 16 (over y, x).
Axes of the slice: x: 4, y: 4, z: 8, core: 2. Of those that a mesh axis runs over, the one named last changes fastest.
Arguments:
- light_field: float32 [2, 256, 32, 1024], P(None, 'trans', 'tm'), may hold values from -6 to 6
- gas_density: float32 [256, 1024], replicated, may hold values from 0.5 to 2
- phase_x: float32 [256], replicated, may hold values from -3.140625 to 3.140625
- phase_y: float32 [1024], replicated, may hold values from -3.140625 to 3.140625
Outputs:
- light_out: float32 [2, 256, 32, 1024], P(None, 'trans', 'tm')
- electrons: float32 [256, 32, 1024], P('trans', 'tm')
The draws below stay inside these ranges and needn't reach their ends.
All inputs are finite; a program needn't handle non-finite values.
Results may differ from the reference program's by a relative error of at most 0.0003.
Values sent between devices are 32-bit elements; how exact they have to be, the bound alone decides.
A program may use at most 64 MiB of HBM per device.

```python
import math
import jax
import jax.numpy as jnp
from jax import lax

NX = 256
NY = 1024
PHOTONS = 8
STEPS = 2
NT = 32


def shard_levels(key, dims, cuts, smallest, top_value):
    def one(dim, shards_of):
        steps = jax.random.uniform(jax.random.fold_in(jax.random.fold_in(key, 6), dim), (shards_of,), jnp.float32, smallest / len(cuts), top_value / len(cuts))
        return jnp.repeat(jnp.exp(steps), dims[dim] // shards_of).reshape((-1,) + (1,) * (len(dims) - dim - 1))

    gain = one(*cuts[0])
    for cut in cuts[1:]:
        gain = gain * one(*cut)
    return gain


def gaussian(stream_key, shape, deviation, bound, split=(), kind=jnp.bfloat16):
    gain = shard_levels(stream_key, shape, split, -0.22, 0.18) if split else 1.0
    result = jax.random.normal(stream_key, shape, jnp.float32) * deviation * gain
    return jnp.minimum(jnp.maximum(result, -bound), bound).astype(kind)


def setup_inputs(seed: int = 0) -> dict:
    key_of = jax.random.split(jax.random.key(seed), 5)
    return {
        "light_field": gaussian(key_of[0], (2, NX, NT, NY), 1.0, 6.0, ((1, 16), (2, 16)), jnp.float32),
        "gas_density": jnp.clip(jnp.exp(jax.random.uniform(key_of[1], (NX, NY), jnp.float32, math.log(0.5), math.log(2.0))), 0.5, 2.0),
        "phase_x": jnp.clip(jax.random.uniform(key_of[2], (NX,), jnp.float32, -3.140625, 3.140625), -3.140625, 3.140625),
        "phase_y": jnp.clip(jax.random.uniform(key_of[3], (NY,), jnp.float32, -3.140625, 3.140625), -3.140625, 3.140625),
    }


RATE_COEF = 1.8e-8
RECOMB = 0.02
KERR_COEF = 0.3
PLASMA = 4.0


def nonlinear(complex_wave, gas_density):
    intensity = jnp.real(complex_wave) ** 2 + jnp.imag(complex_wave) ** 2
    ion_rate = RATE_COEF * intensity ** PHOTONS
    decays = jnp.exp(-(ion_rate + RECOMB))
    source = (1.0 - decays) * gas_density[:, None, :] * ion_rate / (ion_rate + RECOMB)

    def advance(carried, pieces):
        updated = pieces[0] * carried + pieces[1]
        return updated, updated

    start = jnp.zeros((intensity.shape[0], intensity.shape[2]), dtype=intensity.dtype)
    _, stacked = lax.scan(advance, start, (jnp.moveaxis(decays, 1, 0), jnp.moveaxis(source, 1, 0)))
    electrons = jnp.moveaxis(stacked, 0, 1)
    phase_shift = KERR_COEF * intensity - PLASMA * electrons
    return complex_wave * jnp.exp(1j * phase_shift), electrons


def reference(light_field, gas_density, phase_x, phase_y):
    complex_wave = light_field[0] + 1j * light_field[1]
    electrons = jnp.zeros(light_field.shape[1:], dtype=jnp.float32)
    for turn_index in range(STEPS):
        spectrum = jnp.fft.fft(complex_wave, axis=2) * jnp.exp(1j * phase_y)
        complex_wave = jnp.fft.ifft(spectrum, axis=2)
        spectrum = jnp.fft.fft(complex_wave, axis=0) * jnp.exp(1j * phase_x)[:, None, None]
        complex_wave = jnp.fft.ifft(spectrum, axis=0)
        complex_wave, electrons = nonlinear(complex_wave, gas_density)
    return jnp.stack([jnp.real(complex_wave), jnp.imag(complex_wave)]), electrons
```

```python
import functools
import math

import jax
import jax.numpy as jnp
import numpy as np
from jax import lax
from jax.experimental import pallas as pl
from jax.experimental.pallas import tpu as pltpu
from jax.sharding import PartitionSpec as P

RATE_COEF = 1.8e-08
RECOMB = 0.02
KERR_COEF = 0.3
PLASMA = 4.0

N = 16
LANES = 128
HALF = 64
NX = 256
NY = 1024
RADIX = 8

F32 = jnp.float32
MESH = pl.DeviceIdType.MESH
ROOT_HALF = math.sqrt(0.5)


def tables():
    j = np.arange(NX)
    angle = 2.0 * np.pi * ((j[:, None] * j[None, :]) % NX) / NX
    table_x = np.concatenate([np.cos(angle), np.sin(angle)], axis=1)
    b = np.arange(LANES)
    angle = 2.0 * np.pi * ((b[:, None] * b[None, :]) % LANES) / LANES
    c, s = np.cos(angle), np.sin(angle)
    forward = np.block([[c, -s], [s, c]])
    backward = np.block([[c, s], [-s, c]])
    k = np.arange(RADIX)
    angle = 2.0 * np.pi * (k[:, None] * b[None, :]) / NY
    twist = np.stack([np.cos(angle), np.sin(angle)])
    spread = (b[None, :] % 16 == b[:, None] // RADIX).astype(np.float32)
    return [np.asarray(t, np.float32) for t in (table_x, forward, backward, twist, spread)]


def sincos(x):
    n = jnp.floor(x * (2.0 / math.pi) + 0.5)
    r = x - n * 1.5703125
    r = r - n * 4.837512969970703125e-4
    r = r - n * 7.54978995489188216e-8
    z = r * r
    s = r + r * z * (-1.6666654611e-1 + z * (8.3321608736e-3 + z * -1.9515295891e-4))
    c = 1.0 - 0.5 * z + z * z * (
        4.166664568298827e-2 + z * (-1.388731625493765e-3 + z * 2.443315711809948e-5)
    )
    q = n.astype(jnp.int32)
    odd = (q & 1) == 1
    sin = jnp.where(odd, c, s)
    cos = jnp.where(odd, s, c)
    sin = jnp.where((q & 2) == 2, -sin, sin)
    cos = jnp.where(((q + 1) & 2) == 2, -cos, cos)
    return sin, cos


def dot(a, b):
    return lax.dot_general(
        a,
        b,
        (((1,), (0,)), ((), ())),
        precision=lax.Precision.HIGHEST,
        preferred_element_type=F32,
    )


def cadd(a, b):
    return (a[0] + b[0], a[1] + b[1])


def csub(a, b):
    return (a[0] - b[0], a[1] - b[1])


def radix8(x, sign):
    def turn(v):
        return (-v[1], v[0]) if sign > 0 else (v[1], -v[0])

    def four(p, q, r, s):
        e0, e1, e2, e3 = cadd(p, r), csub(p, r), cadd(q, s), turn(csub(q, s))
        return cadd(e0, e2), cadd(e1, e3), csub(e0, e2), csub(e1, e3)

    e = four(x[0], x[2], x[4], x[6])
    o = four(x[1], x[3], x[5], x[7])
    t1, t3 = turn(o[1]), turn(o[3])
    w1 = ((o[1][0] + t1[0]) * ROOT_HALF, (o[1][1] + t1[1]) * ROOT_HALF)
    w3 = ((t3[0] - o[3][0]) * ROOT_HALF, (t3[1] - o[3][1]) * ROOT_HALF)
    o = (o[0], w1, turn(o[2]), w3)
    return [cadd(e[k], o[k]) for k in range(4)] + [csub(e[k], o[k]) for k in range(4)]


def kernel(
    field_hbm, dens_hbm, phx_hbm, phy_hbm, tx_hbm, wf_hbm, wb_hbm, tw_hbm, sp_hbm,
    out_hbm, ele_hbm,
    field, dens1, dens2, phx, phy, tx, wf, wb, tw, sp,
    stage, bmat, mmat, turns,
    send1, recv1, work, dec, src, inten,
    send2, recv2, send3, recv3, send4, recv4, send5, recv5, send6, recv6,
    out, ele,
    in_sems, send_sem, recv_sem, ein_sem, out_sems,
):
    tm = lax.axis_index("tm")
    trans = lax.axis_index("trans")
    low = lax.broadcasted_iota(jnp.int32, (8, LANES), 1) < HALF

    row0 = pl.multiple_of(trans * N, N)
    col0 = pl.multiple_of((trans // 2) * LANES, LANES)
    loads = [
        pltpu.make_async_copy(a, b, in_sems.at[i])
        for i, (a, b) in enumerate(
            [
                (field_hbm, field),
                (tw_hbm, tw),
                (wf_hbm, wf),
                (phy_hbm, phy),
                (sp_hbm, sp),
                (wb_hbm, wb),
                (phx_hbm, phx),
                (tx_hbm, tx),
                (dens_hbm.at[:, pl.ds(col0, LANES)], dens1),
                (dens_hbm.at[pl.ds(row0, N), :], dens2),
            ]
        )
    ]
    for load in loads:
        load.start()

    barrier = pltpu.get_barrier_semaphore()

    def greet(r, carry):
        pl.semaphore_signal(
            barrier, inc=1, device_id={"trans": lax.rem(trans + r, N)}, device_id_type=MESH
        )
        pl.semaphore_signal(
            barrier, inc=1, device_id={"tm": lax.rem(tm + r, N)}, device_id_type=MESH
        )
        return carry

    lax.fori_loop(1, N, greet, 0)

    def exchange(axis, me, src_ref, dst_ref, phase):
        def one(r, carry):
            peer = lax.rem(me + r, N)
            pltpu.make_async_remote_copy(
                src_ref=src_ref.at[peer],
                dst_ref=dst_ref.at[me],
                send_sem=send_sem.at[phase],
                recv_sem=recv_sem.at[phase],
                device_id={axis: peer},
                device_id_type=MESH,
            ).start()
            return carry

        lax.fori_loop(1, N, one, 0)
        dst_ref[me] = src_ref[me]

    def arrived(dst_ref, phase):
        part = dst_ref.at[pl.ds(0, N - 1)]
        pltpu.make_async_copy(part, part, recv_sem.at[phase]).wait()

    def left(src_ref, phase):
        part = src_ref.at[pl.ds(0, N - 1)]
        pltpu.make_async_copy(part, part, send_sem.at[phase]).wait()

    def spectral():
        freq = dot(stage[...], wf[...])
        for k in range(RADIX):
            rows = slice(32 * k, 32 * k + 32)
            re, im = freq[rows, :LANES], freq[rows, LANES:]
            pr, pi = turns[1, k : k + 1, :], turns[0, k : k + 1, :]
            stage[rows, :LANES] = re * pr - im * pi
            stage[rows, LANES:] = re * pi + im * pr
        stage[...] = dot(stage[...], wb[...])

    def forward(blocks, t, xh):
        for k, (re, im) in enumerate(radix8(blocks, -1)):
            rows = slice(32 * k + 16 * t + 8 * xh, 32 * k + 16 * t + 8 * xh + 8)
            c, s = tw[0, k : k + 1, :], tw[1, k : k + 1, :]
            stage[rows, :LANES] = re * c + im * s
            stage[rows, LANES:] = im * c - re * s

    def back(t, xh):
        parts = []
        for k in range(RADIX):
            rows = slice(32 * k + 16 * t + 8 * xh, 32 * k + 16 * t + 8 * xh + 8)
            re, im = stage[rows, :LANES], stage[rows, LANES:]
            c, s = tw[0, k : k + 1, :], tw[1, k : k + 1, :]
            parts.append((re * c - im * s, im * c + re * s))
        return radix8(parts, 1)

    def swap(v):
        return pltpu.roll(v, HALF, 1)

    loads[0].wait()
    loads[1].wait()
    for xh in range(2):
        for t in range(2):
            forward(
                [
                    tuple(field[c, pl.ds(128 * xh + 2 * a + t, 8, stride=16), :] for c in range(2))
                    for a in range(RADIX)
                ],
                t,
                xh,
            )
    for load in loads[2:6]:
        load.wait()
    lane = lax.broadcasted_iota(jnp.int32, (8, LANES), 1)
    sub = lax.broadcasted_iota(jnp.int32, (8, LANES), 0)
    picked = jnp.concatenate(
        [jnp.where(lane % RADIX == sub, phy[r : r + 1, :], 0.0) for r in range(RADIX)], axis=0
    )
    picked = dot(picked, sp[...])
    phase = jnp.zeros((8, LANES), F32)
    for r in range(RADIX):
        phase = jnp.where(lane // 16 == r, picked[8 * r : 8 * r + 8, :], phase)
    sin, cos = sincos(phase)
    turns[0] = sin * (1.0 / NY)
    turns[1] = cos * (1.0 / NY)
    spectral()
    for xh in range(2):
        rows = slice(8 * xh, 8 * xh + 8)
        first, second = back(0, xh), back(1, xh)
        for a in range(RADIX):
            for c in range(2):
                u, v = first[a][c], second[a][c]
                send1[2 * a, c, rows, :] = jnp.where(low, u, swap(v))
                send1[2 * a + 1, c, rows, :] = jnp.where(low, swap(u), v)

    pl.semaphore_wait(barrier, 2 * (N - 1))
    exchange("trans", trans, send1, recv1, 0)

    for load in loads[6:]:
        load.wait()
    sin, cos = sincos(phx[...])
    sin, cos = sin * (1.0 / NX), cos * (1.0 / NX)
    cx, sx = tx[:, :NX], tx[:, NX:]
    bmat[:NX, :] = cx * cos - sx * sin
    bmat[NX:, :] = cx * sin + sx * cos
    both = dot(bmat[...], tx[...])
    mmat[:NX, :] = both[:NX, :NX] + both[NX:, NX:]
    mmat[NX:, :] = both[NX:, :NX] - both[:NX, NX:]

    def along_x(re, im):
        both = dot(mmat[...], jnp.concatenate([re, im], axis=1))
        return both[:NX, :LANES] - both[NX:, LANES:], both[NX:, :LANES] + both[:NX, LANES:]

    def rates(re, im, dens):
        intensity = re * re + im * im
        power = intensity * intensity
        power = power * power
        power = power * power
        rate = RATE_COEF * power
        lost = rate + RECOMB
        decays = jnp.exp(-lost)
        source = (1.0 - decays) * dens * (rate / lost)
        return intensity, decays, source

    arrived(recv1, 0)
    re, im = along_x(
        recv1[:, 0].reshape(NX, LANES), recv1[:, 1].reshape(NX, LANES)
    )
    work[0] = re
    work[1] = im

    odd_slab = lax.rem(trans, 2) == 1
    for k in range(N):
        gains, adds = [], []
        for xh in range(2):
            rows = slice(16 * k + 8 * xh, 16 * k + 8 * xh + 8)
            dens = dens1[rows, :]
            turned = swap(dens)
            dens = jnp.where(low, jnp.where(odd_slab, turned, dens), jnp.where(odd_slab, dens, turned))
            intensity, decays, source = rates(work[0, rows, :], work[1, rows, :], dens)
            inten[rows, :] = intensity
            dec[rows, :] = decays
            src[rows, :] = source
            gains.append(decays * swap(decays))
            adds.append(decays * swap(source) + source)
        send2[k, 0] = jnp.where(low, gains[0], gains[1])
        send2[k, 1] = jnp.where(low, swap(adds[0]), adds[1])
    exchange("tm", tm, send2, recv2, 1)
    arrived(recv2, 1)

    def scan(from_ref, to_ref):
        entering = jnp.zeros((8, LANES), F32)
        for k in range(N):
            to_ref[k] = entering
            entering = from_ref[k, 0] * entering + from_ref[k, 1]

    scan(recv2, send3)
    exchange("tm", tm, send3, recv3, 2)
    arrived(recv3, 2)
    for k in range(N):
        packed = recv3[k]
        turned = swap(packed)
        for xh in range(2):
            rows = slice(16 * k + 8 * xh, 16 * k + 8 * xh + 8)
            entering = jnp.where(low, packed, turned) if xh == 0 else jnp.where(low, turned, packed)
            decays, source = dec[rows, :], src[rows, :]
            earlier = decays * entering + source
            electrons = decays * jnp.where(low, entering, swap(earlier)) + source
            sin, cos = sincos(KERR_COEF * inten[rows, :] - PLASMA * electrons)
            re, im = work[0, rows, :], work[1, rows, :]
            work[0, rows, :] = re * cos - im * sin
            work[1, rows, :] = re * sin + im * cos

    re, im = along_x(work[0], work[1])
    send4[:, 0] = re.reshape(N, 16, LANES)
    send4[:, 1] = im.reshape(N, 16, LANES)
    exchange("trans", trans, send4, recv4, 3)
    arrived(recv4, 3)

    for xh in range(2):
        rows = slice(8 * xh, 8 * xh + 8)
        pairs = [
            [(recv4[2 * a, c, rows, :], recv4[2 * a + 1, c, rows, :]) for c in range(2)]
            for a in range(RADIX)
        ]
        forward([tuple(jnp.where(low, u, swap(v)) for u, v in pair) for pair in pairs], 0, xh)
        forward([tuple(jnp.where(low, swap(u), v) for u, v in pair) for pair in pairs], 1, xh)
    spectral()
    for xh in range(2):
        rows = slice(8 * xh, 8 * xh + 8)
        blocks = [back(t, xh) for t in range(2)]
        for a in range(RADIX):
            k = 8 * xh + a
            dens = dens2[rows, LANES * a : LANES * (a + 1)]
            got = []
            for t in range(2):
                re, im = blocks[t][a]
                at = slice(16 * k + 8 * t, 16 * k + 8 * t + 8)
                work[0, at, :] = re
                work[1, at, :] = im
                intensity, decays, source = rates(re, im, dens)
                inten[at, :] = intensity
                dec[at, :] = decays
                src[at, :] = source
                got.append((decays, source))
            send5[k, 0] = got[0][0] * got[1][0]
            send5[k, 1] = got[1][0] * got[0][1] + got[1][1]
    exchange("tm", tm, send5, recv5, 4)
    arrived(recv5, 4)
    scan(recv5, send6)
    exchange("tm", tm, send6, recv6, 5)
    arrived(recv6, 5)
    for k in range(N):
        xh, a = divmod(k, RADIX)
        electrons = recv6[k]
        for t in range(2):
            at = slice(16 * k + 8 * t, 16 * k + 8 * t + 8)
            electrons = dec[at, :] * electrons + src[at, :]
            sin, cos = sincos(KERR_COEF * inten[at, :] - PLASMA * electrons)
            re, im = work[0, at, :], work[1, at, :]
            to = pl.ds(128 * xh + 2 * a + t, 8, stride=16)
            out[0, to, :] = re * cos - im * sin
            out[1, to, :] = re * sin + im * cos
            ele[to, :] = electrons

    stores = [
        pltpu.make_async_copy(out, out_hbm, out_sems.at[0]),
        pltpu.make_async_copy(ele, ele_hbm, out_sems.at[1]),
    ]
    for store in stores:
        store.start()
    for phase_index, ref in enumerate((send1, send2, send3, send4, send5, send6)):
        left(ref, phase_index)
    for store in stores:
        store.wait()


def local(light_field, gas_density, phase_x, phase_y):
    consts = tables()
    rows = light_field.reshape(2, 16, 2, RADIX, LANES).transpose(0, 1, 3, 2, 4).reshape(2, NX, LANES)
    vmem = lambda *shape: pltpu.VMEM(shape, F32)
    block = vmem(N, 2, 16, LANES)
    small = vmem(N, 2, 8, LANES)
    tiny = vmem(N, 8, LANES)
    out, ele = pl.pallas_call(
        kernel,
        out_shape=(
            jax.ShapeDtypeStruct((2, NX, LANES), F32),
            jax.ShapeDtypeStruct((NX, LANES), F32),
        ),
        in_specs=[pl.BlockSpec(memory_space=pl.ANY)] * 9,
        out_specs=(pl.BlockSpec(memory_space=pl.ANY),) * 2,
        scratch_shapes=[
            vmem(2, NX, LANES), vmem(NX, LANES), vmem(16, NY), vmem(1, NX), vmem(8, LANES),
            vmem(NX, 2 * NX), vmem(NX, NX), vmem(NX, NX), vmem(2, 8, LANES), vmem(LANES, LANES),
            vmem(NX, NX), vmem(2 * NX, NX), vmem(2 * NX, NX), vmem(2, 8, LANES),
            block, block, vmem(2, NX, LANES), vmem(NX, LANES), vmem(NX, LANES), vmem(NX, LANES),
            small, small, tiny, tiny, block, block, small, small, tiny, tiny,
            vmem(2, NX, LANES), vmem(NX, LANES),
            pltpu.SemaphoreType.DMA((10,)),
            pltpu.SemaphoreType.DMA((6,)),
            pltpu.SemaphoreType.DMA((6,)),
            pltpu.SemaphoreType.DMA((N,)),
            pltpu.SemaphoreType.DMA((2,)),
        ],
        compiler_params=pltpu.CompilerParams(
            collective_id=0, has_side_effects=True, vmem_limit_bytes=32 * 1024 * 1024
        ),
        name="split_step",
    )(rows, gas_density, phase_x.reshape(1, NX), phase_y.reshape(RADIX, LANES), *consts)
    out = out.reshape(2, 16, RADIX, 2, LANES).transpose(0, 1, 3, 2, 4).reshape(2, 16, 2, NY)
    ele = ele.reshape(16, RADIX, 2, LANES).transpose(0, 2, 1, 3).reshape(16, 2, NY)
    return out, ele


def solution(mesh):
    placed = (P(None, "trans", "tm", None), P(), P(), P())
    return jax.shard_map(
        local,
        mesh=mesh,
        in_specs=placed,
        out_specs=(P(None, "trans", "tm", None), P("trans", "tm", None)),
        check_vma=False,
    )
```

```python
import functools
import math

import jax
import jax.numpy as jnp
import numpy as np
from jax import lax
from jax.experimental import pallas as pl
from jax.experimental.pallas import tpu as pltpu
from jax.sharding import PartitionSpec as P

RATE_COEF = 1.8e-08
RECOMB = 0.02
KERR_COEF = 0.3
PLASMA = 4.0

N = 16
LANES = 128
HALF = 64
NX = 256
NY = 1024
RADIX = 8

F32 = jnp.float32
MESH = pl.DeviceIdType.MESH
ROOT_HALF = math.sqrt(0.5)


def tables():
    j = np.arange(NX)
    angle = 2.0 * np.pi * ((j[:, None] * j[None, :]) % NX) / NX
    table_x = np.concatenate([np.cos(angle), np.sin(angle)], axis=1)
    b = np.arange(LANES)
    angle = 2.0 * np.pi * ((b[:, None] * b[None, :]) % LANES) / LANES
    c, s = np.cos(angle), np.sin(angle)
    forward = np.block([[c, -s], [s, c]])
    backward = np.block([[c, s], [-s, c]])
    k = np.arange(RADIX)
    angle = 2.0 * np.pi * (k[:, None] * b[None, :]) / NY
    twist = np.stack([np.cos(angle), np.sin(angle)])
    spread = (b[None, :] % 16 == b[:, None] // RADIX).astype(np.float32)
    return [np.asarray(t, np.float32) for t in (table_x, forward, backward, twist, spread)]


def sincos(x):
    n = jnp.floor(x * (2.0 / math.pi) + 0.5)
    r = x - n * 1.5703125
    r = r - n * 4.837512969970703125e-4
    r = r - n * 7.54978995489188216e-8
    z = r * r
    s = r + r * z * (-1.6666654611e-1 + z * (8.3321608736e-3 + z * -1.9515295891e-4))
    c = 1.0 - 0.5 * z + z * z * (
        4.166664568298827e-2 + z * (-1.388731625493765e-3 + z * 2.443315711809948e-5)
    )
    q = n.astype(jnp.int32)
    odd = (q & 1) == 1
    sin = jnp.where(odd, c, s)
    cos = jnp.where(odd, s, c)
    sin = jnp.where((q & 2) == 2, -sin, sin)
    cos = jnp.where(((q + 1) & 2) == 2, -cos, cos)
    return sin, cos


def dot(a, b):
    return lax.dot_general(
        a,
        b,
        (((1,), (0,)), ((), ())),
        precision=lax.Precision.HIGHEST,
        preferred_element_type=F32,
    )


def cadd(a, b):
    return (a[0] + b[0], a[1] + b[1])


def csub(a, b):
    return (a[0] - b[0], a[1] - b[1])


def radix8(x, sign):
    def turn(v):
        return (-v[1], v[0]) if sign > 0 else (v[1], -v[0])

    def four(p, q, r, s):
        e0, e1, e2, e3 = cadd(p, r), csub(p, r), cadd(q, s), turn(csub(q, s))
        return cadd(e0, e2), cadd(e1, e3), csub(e0, e2), csub(e1, e3)

    e = four(x[0], x[2], x[4], x[6])
    o = four(x[1], x[3], x[5], x[7])
    t1, t3 = turn(o[1]), turn(o[3])
    w1 = ((o[1][0] + t1[0]) * ROOT_HALF, (o[1][1] + t1[1]) * ROOT_HALF)
    w3 = ((t3[0] - o[3][0]) * ROOT_HALF, (t3[1] - o[3][1]) * ROOT_HALF)
    o = (o[0], w1, turn(o[2]), w3)
    return [cadd(e[k], o[k]) for k in range(4)] + [csub(e[k], o[k]) for k in range(4)]


def kernel(
    field_hbm, dens_hbm, phx_hbm, phy_hbm, tx_hbm, wf_hbm, wb_hbm, tw_hbm, sp_hbm,
    out_hbm, ele_hbm,
    field, dens1, dens2, phx, phy, tx, wf, wb, tw, sp,
    stage, bmat, mmat, turns,
    send1, recv1, work, dec, src, inten,
    send2, recv2, send3, recv3, send4, recv4, send5, recv5, send6, recv6,
    out, ele,
    in_sems, send_sem, recv_sem, ein_sem, out_sems,
):
    tm = lax.axis_index("tm")
    trans = lax.axis_index("trans")
    low = lax.broadcasted_iota(jnp.int32, (8, LANES), 1) < HALF

    row0 = pl.multiple_of(trans * N, N)
    col0 = pl.multiple_of((trans // 2) * LANES, LANES)
    loads = [
        pltpu.make_async_copy(a, b, in_sems.at[i])
        for i, (a, b) in enumerate(
            [
                (field_hbm, field),
                (tw_hbm, tw),
                (wf_hbm, wf),
                (phy_hbm, phy),
                (sp_hbm, sp),
                (wb_hbm, wb),
                (phx_hbm, phx),
                (tx_hbm, tx),
                (dens_hbm.at[:, pl.ds(col0, LANES)], dens1),
                (dens_hbm.at[pl.ds(row0, N), :], dens2),
            ]
        )
    ]
    for load in loads:
        load.start()

    barrier = pltpu.get_barrier_semaphore()

    def greet(r, carry):
        pl.semaphore_signal(
            barrier, inc=1, device_id={"trans": lax.rem(trans + r, N)}, device_id_type=MESH
        )
        pl.semaphore_signal(
            barrier, inc=1, device_id={"tm": lax.rem(tm + r, N)}, device_id_type=MESH
        )
        return carry

    lax.fori_loop(1, N, greet, 0)

    def exchange(axis, me, src_ref, dst_ref, phase):
        def one(r, carry):
            peer = lax.rem(me + r, N)
            pltpu.make_async_remote_copy(
                src_ref=src_ref.at[peer],
                dst_ref=dst_ref.at[me],
                send_sem=send_sem.at[phase],
                recv_sem=recv_sem.at[phase],
                device_id={axis: peer},
                device_id_type=MESH,
            ).start()
            return carry

        lax.fori_loop(1, N, one, 0)
        dst_ref[me] = src_ref[me]

    def arrived(dst_ref, phase):
        part = dst_ref.at[pl.ds(0, N - 1)]
        pltpu.make_async_copy(part, part, recv_sem.at[phase]).wait()

    def left(src_ref, phase):
        part = src_ref.at[pl.ds(0, N - 1)]
        pltpu.make_async_copy(part, part, send_sem.at[phase]).wait()

    def spectral():
        freq = dot(stage[...], wf[...])
        for k in range(RADIX):
            rows = slice(32 * k, 32 * k + 32)
            re, im = freq[rows, :LANES], freq[rows, LANES:]
            pr, pi = turns[1, k : k + 1, :], turns[0, k : k + 1, :]
            stage[rows, :LANES] = re * pr - im * pi
            stage[rows, LANES:] = re * pi + im * pr
        stage[...] = dot(stage[...], wb[...])

    def forward(blocks, t, xh):
        for k, (re, im) in enumerate(radix8(blocks, -1)):
            rows = slice(32 * k + 16 * t + 8 * xh, 32 * k + 16 * t + 8 * xh + 8)
            c, s = tw[0, k : k + 1, :], tw[1, k : k + 1, :]
            stage[rows, :LANES] = re * c + im * s
            stage[rows, LANES:] = im * c - re * s

    def back(t, xh):
        parts = []
        for k in range(RADIX):
            rows = slice(32 * k + 16 * t + 8 * xh, 32 * k + 16 * t + 8 * xh + 8)
            re, im = stage[rows, :LANES], stage[rows, LANES:]
            c, s = tw[0, k : k + 1, :], tw[1, k : k + 1, :]
            parts.append((re * c - im * s, im * c + re * s))
        return radix8(parts, 1)

    def swap(v):
        return pltpu.roll(v, HALF, 1)

    loads[0].wait()
    loads[1].wait()
    for xh in range(2):
        for t in range(2):
            forward(
                [
                    tuple(field[c, pl.ds(128 * xh + 2 * a + t, 8, stride=16), :] for c in range(2))
                    for a in range(RADIX)
                ],
                t,
                xh,
            )
    for load in loads[2:6]:
        load.wait()
    lane = lax.broadcasted_iota(jnp.int32, (8, LANES), 1)
    sub = lax.broadcasted_iota(jnp.int32, (8, LANES), 0)
    picked = jnp.concatenate(
        [jnp.where(lane % RADIX == sub, phy[r : r + 1, :], 0.0) for r in range(RADIX)], axis=0
    )
    picked = dot(picked, sp[...])
    phase = jnp.zeros((8, LANES), F32)
    for r in range(RADIX):
        phase = jnp.where(lane // 16 == r, picked[8 * r : 8 * r + 8, :], phase)
    sin, cos = sincos(phase)
    turns[0] = sin * (1.0 / NY)
    turns[1] = cos * (1.0 / NY)
    spectral()
    for xh in range(2):
        rows = slice(8 * xh, 8 * xh + 8)
        first, second = back(0, xh), back(1, xh)
        for a in range(RADIX):
            for c in range(2):
                u, v = first[a][c], second[a][c]
                send1[2 * a, c, rows, :] = jnp.where(low, u, swap(v))
                send1[2 * a + 1, c, rows, :] = jnp.where(low, swap(u), v)

    pl.semaphore_wait(barrier, 2 * (N - 1))
    exchange("trans", trans, send1, recv1, 0)

    for load in loads[6:]:
        load.wait()
    sin, cos = sincos(phx[...])
    sin, cos = sin * (1.0 / NX), cos * (1.0 / NX)
    cx, sx = tx[:, :NX], tx[:, NX:]
    bmat[:NX, :] = cx * cos - sx * sin
    bmat[NX:, :] = cx * sin + sx * cos
    both = dot(bmat[...], tx[...])
    mmat[:NX, :] = both[:NX, :NX] + both[NX:, NX:]
    mmat[NX:, :] = both[NX:, :NX] - both[:NX, NX:]

    def along_x(re, im):
        both = dot(mmat[...], jnp.concatenate([re, im], axis=1))
        return both[:NX, :LANES] - both[NX:, LANES:], both[NX:, :LANES] + both[:NX, LANES:]

    def rates(re, im, dens):
        intensity = re * re + im * im
        power = intensity * intensity
        power = power * power
        power = power * power
        rate = RATE_COEF * power
        lost = rate + RECOMB
        decays = jnp.exp(-lost)
        source = (1.0 - decays) * dens * (rate / lost)
        return intensity, decays, source

    arrived(recv1, 0)
    re, im = along_x(
        recv1[:, 0].reshape(NX, LANES), recv1[:, 1].reshape(NX, LANES)
    )
    work[0] = re
    work[1] = im

    odd_slab = lax.rem(trans, 2) == 1
    for k in range(N):
        gains, adds = [], []
        for xh in range(2):
            rows = slice(16 * k + 8 * xh, 16 * k + 8 * xh + 8)
            dens = dens1[rows, :]
            turned = swap(dens)
            dens = jnp.where(low, jnp.where(odd_slab, turned, dens), jnp.where(odd_slab, dens, turned))
            intensity, decays, source = rates(work[0, rows, :], work[1, rows, :], dens)
            inten[rows, :] = intensity
            dec[rows, :] = decays
            src[rows, :] = source
            gains.append(decays * swap(decays))
            adds.append(decays * swap(source) + source)
        send2[k, 0] = jnp.where(low, gains[0], gains[1])
        send2[k, 1] = jnp.where(low, swap(adds[0]), adds[1])
    exchange("tm", tm, send2, recv2, 1)
    arrived(recv2, 1)

    def scan(from_ref, to_ref):
        entering = jnp.zeros((8, LANES), F32)
        for k in range(N):
            to_ref[k] = entering
            entering = from_ref[k, 0] * entering + from_ref[k, 1]

    scan(recv2, send3)
    exchange("tm", tm, send3, recv3, 2)
    arrived(recv3, 2)
    for k in range(N):
        packed = recv3[k]
        turned = swap(packed)
        for xh in range(2):
            rows = slice(16 * k + 8 * xh, 16 * k + 8 * xh + 8)
            entering = jnp.where(low, packed, turned) if xh == 0 else jnp.where(low, turned, packed)
            decays, source = dec[rows, :], src[rows, :]
            earlier = decays * entering + source
            electrons = decays * jnp.where(low, entering, swap(earlier)) + source
            sin, cos = sincos(KERR_COEF * inten[rows, :] - PLASMA * electrons)
            re, im = work[0, rows, :], work[1, rows, :]
            work[0, rows, :] = re * cos - im * sin
            work[1, rows, :] = re * sin + im * cos

    re, im = along_x(work[0], work[1])
    send4[:, 0] = re.reshape(N, 16, LANES)
    send4[:, 1] = im.reshape(N, 16, LANES)
    exchange("trans", trans, send4, recv4, 3)
    arrived(recv4, 3)

    for xh in range(2):
        rows = slice(8 * xh, 8 * xh + 8)
        pairs = [
            [(recv4[2 * a, c, rows, :], recv4[2 * a + 1, c, rows, :]) for c in range(2)]
            for a in range(RADIX)
        ]
        forward([tuple(jnp.where(low, u, swap(v)) for u, v in pair) for pair in pairs], 0, xh)
        forward([tuple(jnp.where(low, swap(u), v) for u, v in pair) for pair in pairs], 1, xh)
    spectral()
    for xh in range(2):
        rows = slice(8 * xh, 8 * xh + 8)
        blocks = [back(t, xh) for t in range(2)]
        for a in range(RADIX):
            k = 8 * xh + a
            dens = dens2[rows, LANES * a : LANES * (a + 1)]
            got = []
            for t in range(2):
                re, im = blocks[t][a]
                at = slice(16 * k + 8 * t, 16 * k + 8 * t + 8)
                work[0, at, :] = re
                work[1, at, :] = im
                intensity, decays, source = rates(re, im, dens)
                inten[at, :] = intensity
                dec[at, :] = decays
                src[at, :] = source
                got.append((decays, source))
            send5[k, 0] = got[0][0] * got[1][0]
            send5[k, 1] = got[1][0] * got[0][1] + got[1][1]
    exchange("tm", tm, send5, recv5, 4)
    arrived(recv5, 4)
    scan(recv5, send6)
    exchange("tm", tm, send6, recv6, 5)
    arrived(recv6, 5)
    for k in range(N):
        xh, a = divmod(k, RADIX)
        electrons = recv6[k]
        for t in range(2):
            at = slice(16 * k + 8 * t, 16 * k + 8 * t + 8)
            electrons = dec[at, :] * electrons + src[at, :]
            sin, cos = sincos(KERR_COEF * inten[at, :] - PLASMA * electrons)
            re, im = work[0, at, :], work[1, at, :]
            to = pl.ds(128 * xh + 2 * a + t, 8, stride=16)
            out[0, to, :] = re * cos - im * sin
            out[1, to, :] = re * sin + im * cos
            ele[to, :] = electrons

    stores = [
        pltpu.make_async_copy(out, out_hbm, out_sems.at[0]),
        pltpu.make_async_copy(ele, ele_hbm, out_sems.at[1]),
    ]
    for store in stores:
        store.start()
    for phase_index, ref in enumerate((send1, send2, send3, send4, send5, send6)):
        left(ref, phase_index)
    for store in stores:
        store.wait()


def local(light_field, gas_density, phase_x, phase_y):
    consts = tables()
    rows = light_field.reshape(2, 16, 2, RADIX, LANES).transpose(0, 1, 3, 2, 4).reshape(2, NX, LANES)
    vmem = lambda *shape: pltpu.VMEM(shape, F32)
    block = vmem(N, 2, 16, LANES)
    small = vmem(N, 2, 8, LANES)
    tiny = vmem(N, 8, LANES)
    out, ele = pl.pallas_call(
        kernel,
        out_shape=(
            jax.ShapeDtypeStruct((2, NX, LANES), F32),
            jax.ShapeDtypeStruct((NX, LANES), F32),
        ),
        in_specs=[pl.BlockSpec(memory_space=pl.ANY)] * 9,
        out_specs=(pl.BlockSpec(memory_space=pl.ANY),) * 2,
        scratch_shapes=[
            vmem(2, NX, LANES), vmem(NX, LANES), vmem(16, NY), vmem(1, NX), vmem(8, LANES),
            vmem(NX, 2 * NX), vmem(NX, NX), vmem(NX, NX), vmem(2, 8, LANES), vmem(LANES, LANES),
            vmem(NX, NX), vmem(2 * NX, NX), vmem(2 * NX, NX), vmem(2, 8, LANES),
            block, block, vmem(2, NX, LANES), vmem(NX, LANES), vmem(NX, LANES), vmem(NX, LANES),
            small, small, tiny, tiny, block, block, small, small, tiny, tiny,
            vmem(2, NX, LANES), vmem(NX, LANES),
            pltpu.SemaphoreType.DMA((10,)),
            pltpu.SemaphoreType.DMA((6,)),
            pltpu.SemaphoreType.DMA((6,)),
            pltpu.SemaphoreType.DMA((N,)),
            pltpu.SemaphoreType.DMA((2,)),
        ],
        compiler_params=pltpu.CompilerParams(
            collective_id=0, has_side_effects=True, vmem_limit_bytes=60 * 1024 * 1024
        ),
        name="split_step",
    )(rows, gas_density, phase_x.reshape(1, NX), phase_y.reshape(RADIX, LANES), *consts)
    out = out.reshape(2, 16, RADIX, 2, LANES).transpose(0, 1, 3, 2, 4).reshape(2, 16, 2, NY)
    ele = ele.reshape(16, RADIX, 2, LANES).transpose(0, 2, 1, 3).reshape(16, 2, NY)
    return out, ele


def solution(mesh):
    placed = (P(None, "trans", "tm", None), P(), P(), P())
    return jax.shard_map(
        local,
        mesh=mesh,
        in_specs=placed,
        out_specs=(P(None, "trans", "tm", None), P("trans", "tm", None)),
        check_vma=False,
    )
```

```python
import functools
import math

import jax
import jax.numpy as jnp
import numpy as np
from jax import lax
from jax.experimental import pallas as pl
from jax.experimental.pallas import tpu as pltpu
from jax.sharding import PartitionSpec as P

RATE_COEF = 1.8e-08
RECOMB = 0.02
KERR_COEF = 0.3
PLASMA = 4.0

N = 16
LANES = 128
GROUP = 4
TEAM = N * GROUP
NX = 256
NY = 1024
RADIX = 8

F32 = jnp.float32
MESH = pl.DeviceIdType.MESH
ROOT_HALF = math.sqrt(0.5)


def tables():
    j = np.arange(NX)
    angle = 2.0 * np.pi * ((j[:, None] * j[None, :]) % NX) / NX
    table_x = np.concatenate([np.cos(angle), np.sin(angle)], axis=1)
    b = np.arange(LANES)
    angle = 2.0 * np.pi * ((b[:, None] * b[None, :]) % LANES) / LANES
    c, s = np.cos(angle), np.sin(angle)
    forward = np.block([[c, -s], [s, c]])
    backward = np.block([[c, s], [-s, c]])
    k = np.arange(RADIX)
    angle = 2.0 * np.pi * (k[:, None] * b[None, :]) / NY
    twist = np.stack([np.cos(angle), np.sin(angle)])
    spread = (b[None, :] % 16 == b[:, None] // RADIX).astype(np.float32)
    return [np.asarray(t, np.float32) for t in (table_x, forward, backward, twist, spread)]


def sincos(x):
    n = jnp.floor(x * (2.0 / math.pi) + 0.5)
    r = x - n * 1.5703125
    r = r - n * 4.837512969970703125e-4
    r = r - n * 7.54978995489188216e-8
    z = r * r
    s = r + r * z * (-1.6666654611e-1 + z * (8.3321608736e-3 + z * -1.9515295891e-4))
    c = 1.0 - 0.5 * z + z * z * (
        4.166664568298827e-2 + z * (-1.388731625493765e-3 + z * 2.443315711809948e-5)
    )
    q = n.astype(jnp.int32)
    odd = (q & 1) == 1
    sin = jnp.where(odd, c, s)
    cos = jnp.where(odd, s, c)
    sin = jnp.where((q & 2) == 2, -sin, sin)
    cos = jnp.where(((q + 1) & 2) == 2, -cos, cos)
    return sin, cos


def dot(a, b):
    return lax.dot_general(
        a,
        b,
        (((1,), (0,)), ((), ())),
        precision=lax.Precision.HIGHEST,
        preferred_element_type=F32,
    )


def cadd(a, b):
    return (a[0] + b[0], a[1] + b[1])


def csub(a, b):
    return (a[0] - b[0], a[1] - b[1])


def radix8(x, sign):
    def turn(v):
        return (-v[1], v[0]) if sign > 0 else (v[1], -v[0])

    def four(p, q, r, s):
        e0, e1, e2, e3 = cadd(p, r), csub(p, r), cadd(q, s), turn(csub(q, s))
        return cadd(e0, e2), cadd(e1, e3), csub(e0, e2), csub(e1, e3)

    e = four(x[0], x[2], x[4], x[6])
    o = four(x[1], x[3], x[5], x[7])
    t1, t3 = turn(o[1]), turn(o[3])
    w1 = ((o[1][0] + t1[0]) * ROOT_HALF, (o[1][1] + t1[1]) * ROOT_HALF)
    w3 = ((t3[0] - o[3][0]) * ROOT_HALF, (t3[1] - o[3][1]) * ROOT_HALF)
    o = (o[0], w1, turn(o[2]), w3)
    return [cadd(e[k], o[k]) for k in range(4)] + [csub(e[k], o[k]) for k in range(4)]


def roll(v, by, axis):
    return pltpu.roll(v, by % v.shape[axis], axis)


def transpose_lanes(blocks, width):
    blocks = list(blocks)
    group = lax.broadcasted_iota(jnp.int32, (8, LANES), 1) // width
    bit = len(blocks) // 2
    while bit:
        clear = lax.rem(group // bit, 2) == 0
        for u in range(len(blocks)):
            if u & bit == 0:
                p, q = blocks[u], blocks[u | bit]
                blocks[u] = jnp.where(clear, p, roll(q, bit * width, 1))
                blocks[u | bit] = jnp.where(clear, roll(p, -bit * width, 1), q)
        bit //= 2
    return blocks


def spread_lanes(v):
    group = lax.broadcasted_iota(jnp.int32, (8, LANES), 1) // 16
    out = [v]
    for bit in (4, 2, 1):
        clear = lax.rem(group // bit, 2) == 0
        nxt = []
        for x in out:
            nxt.append(jnp.where(clear, x, roll(x, 16 * bit, 1)))
            nxt.append(jnp.where(clear, roll(x, -16 * bit, 1), x))
        out = nxt
    return out


def rates(re, im, dens):
    intensity = re * re + im * im
    power = intensity * intensity
    power = power * power
    power = power * power
    rate = RATE_COEF * power
    lost = rate + RECOMB
    decays = jnp.exp(-lost)
    source = (1.0 - decays) * dens * (rate / lost)
    return intensity, decays, source


def kernel(
    field_hbm, dens_hbm, phx_hbm, phy_hbm, tx_hbm, wf_hbm, wb_hbm, tw_hbm, sp_hbm,
    out, ele,
    field, dens1, dens2, phx, phy, tx, wf, wb, tw, sp,
    stage, bmat, mmat, mmix, turns, densx, densy,
    send1, recv1, work, gain, phase0,
    send2, recv2, ent, send4, recv4, fold, dec, src, inten,
    sende, recve, send5, recv5, ent5, send6, recv6,
    in_sems, ready, team_send, team_recv, map_send, map_recv, own_send, own_recv,
):
    tm = lax.axis_index("tm")
    trans = lax.axis_index("trans")
    g = tm // GROUP
    s = lax.rem(tm, GROUP)
    me = GROUP * trans + s

    barrier = pltpu.get_barrier_semaphore()

    def mate(r):
        other = lax.rem(trans + r // GROUP, N)
        slot = lax.rem(s + lax.rem(r, GROUP), GROUP)
        return (GROUP * g + slot, other), GROUP * other + slot

    def greet(r, carry):
        where_to, _ = mate(r)
        pl.semaphore_signal(barrier, inc=1, device_id=where_to, device_id_type=MESH)
        return carry

    row0 = pl.multiple_of(trans * N, N)
    col0 = pl.multiple_of((me // 8) * LANES, LANES)
    loads = [
        pltpu.make_async_copy(a, b, in_sems.at[i])
        for i, (a, b) in enumerate(
            [
                (field_hbm, field),
                (tw_hbm, tw),
                (wf_hbm, wf),
                (phy_hbm, phy),
                (sp_hbm, sp),
                (wb_hbm, wb),
                (phx_hbm, phx),
                (tx_hbm, tx),
                (dens_hbm.at[:, pl.ds(col0, LANES)], dens1),
                (dens_hbm.at[pl.ds(row0, N), :], dens2),
            ]
        )
    ]
    for load in loads:
        load.start()
    lax.fori_loop(1, TEAM, greet, 0)
    for later in range(1, GROUP):

        @pl.when(g + later < GROUP)
        def _():
            pl.semaphore_signal(
                barrier, inc=1, device_id=(tm + GROUP * later, trans), device_id_type=MESH
            )

    def exchange(src_ref, dst_ref, phase):
        def one(r, carry):
            where_to, slot = mate(r)
            pltpu.make_async_remote_copy(
                src_ref=src_ref.at[slot],
                dst_ref=dst_ref.at[me],
                send_sem=team_send.at[phase],
                recv_sem=team_recv.at[phase],
                device_id=where_to,
                device_id_type=MESH,
            ).start()
            return carry

        lax.fori_loop(1, TEAM, one, 0)
        dst_ref[me] = src_ref[me]

    def whole(ref, sem, count):
        part = ref.at[pl.ds(0, count)]
        pltpu.make_async_copy(part, part, sem).wait()

    def send_map(src_ref, dst_ref, phase, chunk):
        for later in range(1, GROUP):

            @pl.when(g + later < GROUP)
            def _():
                pltpu.make_async_remote_copy(
                    src_ref=src_ref.at[chunk],
                    dst_ref=dst_ref.at[g, chunk],
                    send_sem=map_send.at[phase],
                    recv_sem=map_recv.at[phase, g],
                    device_id=(tm + GROUP * later, trans),
                    device_id_type=MESH,
                ).start()

    def enter(dst_ref, phase, total):
        total[...] = jnp.zeros_like(total)
        for k in range(GROUP - 1):

            @pl.when(k < g)
            def _():
                pltpu.make_async_copy(dst_ref.at[k], dst_ref.at[k], map_recv.at[phase, k]).wait()
                for chunk in range(4):
                    total[chunk] = dst_ref[k, chunk, 0] * total[chunk] + dst_ref[k, chunk, 1]

    def send_own(src_ref, dst_ref, phase, i):
        @pl.when(i != s)
        def _():
            pltpu.make_async_remote_copy(
                src_ref=src_ref.at[i],
                dst_ref=dst_ref.at[s],
                send_sem=own_send.at[phase],
                recv_sem=own_recv.at[phase, s],
                device_id=(GROUP * g + i, trans),
                device_id_type=MESH,
            ).start()

    lane = lax.broadcasted_iota(jnp.int32, (8, LANES), 1)
    sub = lax.broadcasted_iota(jnp.int32, (8, LANES), 0)
    group = lane // 16
    top = sub < 4

    def flip(v):
        return roll(v, 4, 0)

    def spectral():
        freq = dot(stage[...], wf[...])
        for k in range(RADIX):
            rows = slice(32 * k, 32 * k + 32)
            re, im = freq[rows, :LANES], freq[rows, LANES:]
            pr, pi = turns[1, k : k + 1, :], turns[0, k : k + 1, :]
            stage[rows, :LANES] = re * pr - im * pi
            stage[rows, LANES:] = re * pi + im * pr
        stage[...] = dot(stage[...], wb[...])

    def forward(blocks, w):
        for k, (re, im) in enumerate(radix8(blocks, -1)):
            rows = slice(32 * k + 8 * w, 32 * k + 8 * w + 8)
            c, d = tw[0, k : k + 1, :], tw[1, k : k + 1, :]
            stage[rows, :LANES] = re * c + im * d
            stage[rows, LANES:] = im * c - re * d

    def back(w):
        parts = []
        for k in range(RADIX):
            rows = slice(32 * k + 8 * w, 32 * k + 8 * w + 8)
            re, im = stage[rows, :LANES], stage[rows, LANES:]
            c, d = tw[0, k : k + 1, :], tw[1, k : k + 1, :]
            parts.append((re * c - im * d, im * c + re * d))
        return radix8(parts, 1)

    loads[0].wait()
    loads[1].wait()
    for xh in range(2):
        for t in range(2):
            forward(
                [
                    tuple(field[c, pl.ds(128 * xh + 2 * a + t, 8, stride=16), :] for c in range(2))
                    for a in range(RADIX)
                ],
                2 * xh + t,
            )
    for load in loads[2:6]:
        load.wait()
    picked = jnp.concatenate(
        [jnp.where(lane % RADIX == sub, phy[r : r + 1, :], 0.0) for r in range(RADIX)], axis=0
    )
    picked = dot(picked, sp[...])
    phase = jnp.zeros((8, LANES), F32)
    for r in range(RADIX):
        phase = jnp.where(group == r, picked[8 * r : 8 * r + 8, :], phase)
    sin, cos = sincos(phase)
    turns[0] = sin * (1.0 / NY)
    turns[1] = cos * (1.0 / NY)
    spectral()
    parts = [back(w) for w in range(4)]
    for a in range(RADIX):
        mixed = transpose_lanes(
            [parts[2 * xh + t][a][c] for xh in range(2) for c in range(2) for t in range(2)], 16
        )
        for j in range(8):
            send1[8 * a + j] = mixed[j]

    pl.semaphore_wait(barrier, TEAM - 1 + g)
    exchange(send1, recv1, 0)
    for k in range(GROUP - 1):

        @pl.when(k < g)
        def _():
            pl.semaphore_signal(
                ready, inc=1, device_id=(GROUP * k + s, trans), device_id_type=MESH
            )

    for load in loads[6:]:
        load.wait()
    sin, cos = sincos(phx[...])
    sin, cos = sin * (1.0 / NX), cos * (1.0 / NX)
    cx, sx = tx[:, :NX], tx[:, NX:]
    bmat[:NX, :] = cx * cos - sx * sin
    bmat[NX:, :] = cx * sin + sx * cos
    both = dot(bmat[...], tx[...])
    mmat[:NX, :] = both[:NX, :NX] + both[NX:, NX:]
    mmat[NX:, :] = both[NX:, :NX] - both[:NX, NX:]
    for m in range(NX // 8):
        for half in range(2):
            cols = slice(LANES * half, LANES * (half + 1))
            re, im = mmat[8 * m : 8 * m + 8, cols], mmat[NX + 8 * m : NX + 8 * m + 8, cols]
            mmix[16 * m : 16 * m + 8, cols] = jnp.where(top, re, flip(im))
            mmix[16 * m + 8 : 16 * m + 16, cols] = jnp.where(top, flip(re), im)
    mine = group == lax.rem(me, 8)
    for m in range(NX // 8):
        rows = slice(8 * m, 8 * m + 8)
        v = jnp.where(mine, dens1[rows, :], 0.0)
        for shift in (16, 32, 64):
            v = v + roll(v, shift, 1)
        densx[rows, :] = v
    for r in range(4):
        line = dens2[pl.ds(4 * s + r, 1), :]
        densy[r : r + 1, :] = line
        densy[r + 4 : r + 5, :] = line

    whole(recv1, team_recv.at[0], TEAM - 1)
    for p in range(N):
        mixed = transpose_lanes([recv1[4 * p + k] for k in range(4)], 32)
        for xh in range(2):
            for c in range(2):
                work[c, 16 * p + 8 * xh : 16 * p + 8 * xh + 8, :] = mixed[2 * xh + c]
    both = dot(mmat[...], jnp.concatenate([work[0], work[1]], axis=1))
    work[0] = both[:NX, :LANES] - both[NX:, LANES:]
    work[1] = both[NX:, :LANES] + both[:NX, LANES:]

    @pl.when(g < GROUP - 1)
    def _():
        pl.semaphore_wait(ready, GROUP - 1 - g)

    for chunk in range(4):
        maps = [jnp.zeros((8, LANES), F32)] * 2
        for i in range(8):
            rows = slice(64 * chunk + 8 * i, 64 * chunk + 8 * i + 8)
            intensity, grow, add = rates(work[0, rows, :], work[1, rows, :], densx[rows, :])
            for bit in (1, 2, 4):
                there = group >= bit
                grow2, add2 = roll(grow, 16 * bit, 1), roll(add, 16 * bit, 1)
                add = jnp.where(there, grow * add2 + add, add)
                grow = jnp.where(there, grow * grow2, grow)
            phase0[rows, :] = KERR_COEF * intensity - PLASMA * add
            gain[rows, :] = PLASMA * grow
            maps = [
                jnp.where(group == i, roll(v, 16 * (i + 1), 1), old)
                for v, old in zip((grow, add), maps)
            ]
        send2[chunk, 0] = maps[0]
        send2[chunk, 1] = maps[1]
        send_map(send2, recv2, 0, chunk)
    enter(recv2, 0, ent)
    for chunk in range(4):
        for i, entering in enumerate(spread_lanes(ent[chunk])):
            rows = slice(64 * chunk + 8 * i, 64 * chunk + 8 * i + 8)
            sin, cos = sincos(phase0[rows, :] - gain[rows, :] * entering)
            re, im = work[0, rows, :], work[1, rows, :]
            work[0, rows, :] = re * cos - im * sin
            work[1, rows, :] = re * sin + im * cos

    both = dot(mmix[...], jnp.concatenate([work[0], work[1]], axis=1))
    for k in range(TEAM):
        rows = slice(8 * k, 8 * k + 8)
        turned = flip(both[rows, LANES:])
        send4[k] = both[rows, :LANES] + jnp.where(top, -turned, turned)
    exchange(send4, recv4, 1)
    whole(recv4, team_recv.at[1], TEAM - 1)

    for a in range(RADIX):
        times = transpose_lanes([recv4[8 * a + j] for j in range(8)], 16)
        for i in range(4):
            u, v = times[2 * i], times[2 * i + 1]
            fold[i, a, 0] = jnp.where(top, u, flip(v))
            fold[i, a, 1] = jnp.where(top, flip(u), v)
    for i in range(4):
        forward([(fold[i, a, 0], fold[i, a, 1]) for a in range(RADIX)], i)
    spectral()
    maps = [None] * 4
    for i in range(4):
        fields = back(i)
        pairs = []
        for a in range(RADIX):
            re, im = fields[a]
            sende[i, a, 0] = re
            sende[i, a, 1] = im
            _, decays, source = rates(re, im, densy[:, LANES * a : LANES * (a + 1)])
            dec[i, a] = decays
            src[i, a] = source
            pairs.append((decays * flip(decays), decays * flip(source) + source))
        for h in range(4):
            even, odd = pairs[2 * h], pairs[2 * h + 1]
            grow = jnp.where(top, even[0], odd[0])
            add = jnp.where(top, flip(even[1]), odd[1])
            if maps[h] is not None:
                grow, add = grow * maps[h][0], grow * maps[h][1] + add
            maps[h] = (grow, add)
    for h in range(4):
        send5[h, 0] = maps[h][0]
        send5[h, 1] = maps[h][1]
        send_map(send5, recv5, 1, h)
    for i in range(GROUP):
        send_own(sende, recve, 0, i)
    recve[s] = sende[s]

    enter(recv5, 1, ent5)
    current = []
    for h in range(4):
        v = ent5[h]
        turned = flip(v)
        current += [jnp.where(top, v, turned), jnp.where(top, turned, v)]
    for i in range(4):
        for a in range(RADIX):
            decays, source = dec[i, a], src[i, a]
            first = decays * current[a] + source
            electrons = decays * jnp.where(top, current[a], flip(first)) + source
            send6[i, a] = electrons
            current[a] = jnp.where(top, flip(electrons), electrons)
        send_own(send6, recv6, 1, i)
    recv6[s] = send6[s]

    for k in range(GROUP):

        @pl.when(k != s)
        def _():
            pltpu.make_async_copy(recve.at[k], recve.at[k], own_recv.at[0, k]).wait()
            pltpu.make_async_copy(recv6.at[k], recv6.at[k], own_recv.at[1, k]).wait()

        for a in range(RADIX):
            re, im, electrons = recve[k, a, 0], recve[k, a, 1], recv6[k, a]
            intensity = re * re + im * im
            sin, cos = sincos(KERR_COEF * intensity - PLASMA * electrons)
            new_re, new_im = re * cos - im * sin, re * sin + im * cos
            for t in range(2):
                rows = pl.ds(64 * k + 2 * a + t, 4, stride=16)
                part = slice(4 * t, 4 * t + 4)
                out[0, rows, :] = new_re[part]
                out[1, rows, :] = new_im[part]
                ele[rows, :] = electrons[part]

    whole(send1, team_send.at[0], TEAM - 1)
    whole(send4, team_send.at[1], TEAM - 1)
    whole(sende, own_send.at[0], GROUP - 1)
    whole(send6, own_send.at[1], GROUP - 1)
    for later in range(1, GROUP):

        @pl.when(g + later < GROUP)
        def _():
            for phase_index, ref in enumerate((send2, send5)):
                whole(ref, map_send.at[phase_index], 4)


def local(light_field, gas_density, phase_x, phase_y):
    consts = tables()
    rows = light_field.reshape(2, 16, 2, RADIX, LANES).transpose(0, 1, 3, 2, 4).reshape(2, NX, LANES)
    vmem = lambda *shape: pltpu.VMEM(shape, F32)
    team = vmem(TEAM, 8, LANES)
    chunks = vmem(4, 2, 8, LANES)
    incoming = vmem(GROUP - 1, 4, 2, 8, LANES)
    tall = vmem(4, RADIX, 8, LANES)
    fields = vmem(4, RADIX, 2, 8, LANES)
    plane = vmem(NX, LANES)
    out, ele = pl.pallas_call(
        kernel,
        out_shape=(
            jax.ShapeDtypeStruct((2, NX, LANES), F32),
            jax.ShapeDtypeStruct((NX, LANES), F32),
        ),
        in_specs=[pl.BlockSpec(memory_space=pltpu.HBM)] * 9,
        out_specs=(pl.BlockSpec(memory_space=pltpu.VMEM),) * 2,
        scratch_shapes=[
            vmem(2, NX, LANES), plane, vmem(16, NY), vmem(1, NX), vmem(8, LANES),
            vmem(NX, 2 * NX), vmem(NX, NX), vmem(NX, NX), vmem(2, 8, LANES), vmem(LANES, LANES),
            vmem(NX, NX), vmem(2 * NX, NX), vmem(2 * NX, NX), vmem(2 * NX, NX),
            vmem(2, 8, LANES), plane, vmem(8, NY),
            team, team, vmem(2, NX, LANES), plane, plane,
            chunks, incoming, vmem(4, 8, LANES), team, team, fields, tall, tall, tall,
            fields, fields, chunks, incoming, vmem(4, 8, LANES), tall, tall,
            pltpu.SemaphoreType.DMA((10,)),
            pltpu.SemaphoreType.REGULAR,
            pltpu.SemaphoreType.DMA((2,)),
            pltpu.SemaphoreType.DMA((2,)),
            pltpu.SemaphoreType.DMA((2,)),
            pltpu.SemaphoreType.DMA((2, GROUP - 1)),
            pltpu.SemaphoreType.DMA((2,)),
            pltpu.SemaphoreType.DMA((2, GROUP)),
        ],
        compiler_params=pltpu.CompilerParams(
            collective_id=0, has_side_effects=True, vmem_limit_bytes=60 * 1024 * 1024
        ),
        name="split_step",
    )(rows, gas_density, phase_x.reshape(1, NX), phase_y.reshape(RADIX, LANES), *consts)
    out = out.reshape(2, 16, RADIX, 2, LANES).transpose(0, 1, 3, 2, 4).reshape(2, 16, 2, NY)
    ele = ele.reshape(16, RADIX, 2, LANES).transpose(0, 2, 1, 3).reshape(16, 2, NY)
    return out, ele


def solution(mesh):
    placed = (P(None, "trans", "tm", None), P(), P(), P())
    return jax.shard_map(
        local,
        mesh=mesh,
        in_specs=placed,
        out_specs=(P(None, "trans", "tm", None), P("trans", "tm", None)),
        check_vma=False,
    )
```

```python
import functools
import math

import jax
import jax.numpy as jnp
import numpy as np
from jax import lax
from jax.experimental import pallas as pl
from jax.experimental.pallas import tpu as pltpu
from jax.sharding import PartitionSpec as P

RATE_COEF = 1.8e-08
RECOMB = 0.02
KERR_COEF = 0.3
PLASMA = 4.0

N = 16
LANES = 128
GROUP = 4
TEAM = N * GROUP
NX = 256
NY = 1024
RADIX = 8

F32 = jnp.float32
MESH = pl.DeviceIdType.MESH
ROOT_HALF = math.sqrt(0.5)


def tables():
    j = np.arange(NX)
    angle = 2.0 * np.pi * ((j[:, None] * j[None, :]) % NX) / NX
    table_x = np.concatenate([np.cos(angle), np.sin(angle)], axis=1)
    b = np.arange(LANES)
    angle = 2.0 * np.pi * ((b[:, None] * b[None, :]) % LANES) / LANES
    c, s = np.cos(angle), np.sin(angle)
    forward = np.block([[c, -s], [s, c]])
    backward = np.block([[c, s], [-s, c]])
    k = np.arange(RADIX)
    angle = 2.0 * np.pi * (k[:, None] * b[None, :]) / NY
    twist = np.stack([np.cos(angle), np.sin(angle)])
    spread = (b[None, :] % 16 == b[:, None] // RADIX).astype(np.float32)
    return [np.asarray(t, np.float32) for t in (table_x, forward, backward, twist, spread)]


def sincos(x):
    n = jnp.floor(x * (2.0 / math.pi) + 0.5)
    r = x - n * 1.5703125
    r = r - n * 4.837512969970703125e-4
    r = r - n * 7.54978995489188216e-8
    z = r * r
    s = r + r * z * (-1.6666654611e-1 + z * (8.3321608736e-3 + z * -1.9515295891e-4))
    c = 1.0 - 0.5 * z + z * z * (
        4.166664568298827e-2 + z * (-1.388731625493765e-3 + z * 2.443315711809948e-5)
    )
    q = n.astype(jnp.int32)
    odd = (q & 1) == 1
    sin = jnp.where(odd, c, s)
    cos = jnp.where(odd, s, c)
    sin = jnp.where((q & 2) == 2, -sin, sin)
    cos = jnp.where(((q + 1) & 2) == 2, -cos, cos)
    return sin, cos


def dot(a, b):
    return lax.dot_general(
        a,
        b,
        (((1,), (0,)), ((), ())),
        precision=lax.Precision.HIGHEST,
        preferred_element_type=F32,
    )


def cadd(a, b):
    return (a[0] + b[0], a[1] + b[1])


def csub(a, b):
    return (a[0] - b[0], a[1] - b[1])


def radix8(x, sign):
    def turn(v):
        return (-v[1], v[0]) if sign > 0 else (v[1], -v[0])

    def four(p, q, r, s):
        e0, e1, e2, e3 = cadd(p, r), csub(p, r), cadd(q, s), turn(csub(q, s))
        return cadd(e0, e2), cadd(e1, e3), csub(e0, e2), csub(e1, e3)

    e = four(x[0], x[2], x[4], x[6])
    o = four(x[1], x[3], x[5], x[7])
    t1, t3 = turn(o[1]), turn(o[3])
    w1 = ((o[1][0] + t1[0]) * ROOT_HALF, (o[1][1] + t1[1]) * ROOT_HALF)
    w3 = ((t3[0] - o[3][0]) * ROOT_HALF, (t3[1] - o[3][1]) * ROOT_HALF)
    o = (o[0], w1, turn(o[2]), w3)
    return [cadd(e[k], o[k]) for k in range(4)] + [csub(e[k], o[k]) for k in range(4)]


def roll(v, by, axis):
    return pltpu.roll(v, by % v.shape[axis], axis)


def transpose_lanes(blocks, width):
    blocks = list(blocks)
    group = lax.broadcasted_iota(jnp.int32, (8, LANES), 1) // width
    bit = len(blocks) // 2
    while bit:
        clear = lax.rem(group // bit, 2) == 0
        for u in range(len(blocks)):
            if u & bit == 0:
                p, q = blocks[u], blocks[u | bit]
                blocks[u] = jnp.where(clear, p, roll(q, bit * width, 1))
                blocks[u | bit] = jnp.where(clear, roll(p, -bit * width, 1), q)
        bit //= 2
    return blocks


def spread_lanes(v):
    group = lax.broadcasted_iota(jnp.int32, (8, LANES), 1) // 16
    out = [v]
    for bit in (4, 2, 1):
        clear = lax.rem(group // bit, 2) == 0
        nxt = []
        for x in out:
            nxt.append(jnp.where(clear, x, roll(x, 16 * bit, 1)))
            nxt.append(jnp.where(clear, roll(x, -16 * bit, 1), x))
        out = nxt
    return out


def rates(re, im, dens):
    intensity = re * re + im * im
    power = intensity * intensity
    power = power * power
    power = power * power
    rate = RATE_COEF * power
    lost = rate + RECOMB
    decays = jnp.exp(-lost)
    source = (1.0 - decays) * dens * (rate / lost)
    return intensity, decays, source


def kernel(
    field_hbm, dens_hbm, phx_hbm, phy_hbm, tx_hbm, wf_hbm, wb_hbm, tw_hbm, sp_hbm,
    out, ele,
    field, dens1, dens2, phx, phy, tx, wf, wb, tw, sp,
    stage, bmat, mmat, mmix, turns, densx, densy,
    send1, recv1, work, gain, phase0,
    send2, recv2, ent, send4, recv4, fold, dec, src, inten,
    sende, recve, send5, recv5, ent5, send6, recv6,
    in_sems, ready, team_send, team_recv, map_send, map_recv, own_send, own_recv,
):
    tm = lax.axis_index("tm")
    trans = lax.axis_index("trans")
    g = tm // GROUP
    s = lax.rem(tm, GROUP)
    me = GROUP * trans + s

    barrier = pltpu.get_barrier_semaphore()

    def mate(r):
        other = lax.rem(trans + r // GROUP, N)
        slot = lax.rem(s + lax.rem(r, GROUP), GROUP)
        return (GROUP * g + slot, other), GROUP * other + slot

    def greet(r, carry):
        where_to, _ = mate(r)
        pl.semaphore_signal(barrier, inc=1, device_id=where_to, device_id_type=MESH)
        return carry

    row0 = pl.multiple_of(trans * N, N)
    col0 = pl.multiple_of((me // 8) * LANES, LANES)
    loads = [
        pltpu.make_async_copy(a, b, in_sems.at[i])
        for i, (a, b) in enumerate(
            [
                (field_hbm, field),
                (tw_hbm, tw),
                (wf_hbm, wf),
                (phy_hbm, phy),
                (sp_hbm, sp),
                (wb_hbm, wb),
                (phx_hbm, phx),
                (tx_hbm, tx),
                (dens_hbm.at[:, pl.ds(col0, LANES)], dens1),
                (dens_hbm.at[pl.ds(row0, N), :], dens2),
            ]
        )
    ]
    for load in loads:
        load.start()
    lax.fori_loop(1, TEAM, greet, 0)
    for later in range(1, GROUP):

        @pl.when(g + later < GROUP)
        def _():
            pl.semaphore_signal(
                barrier, inc=1, device_id=(tm + GROUP * later, trans), device_id_type=MESH
            )

    def exchange(src_ref, dst_ref, phase):
        def one(r, carry):
            where_to, slot = mate(r)
            pltpu.make_async_remote_copy(
                src_ref=src_ref.at[slot],
                dst_ref=dst_ref.at[me],
                send_sem=team_send.at[phase],
                recv_sem=team_recv.at[phase],
                device_id=where_to,
                device_id_type=MESH,
            ).start()
            return carry

        lax.fori_loop(1, TEAM, one, 0)
        dst_ref[me] = src_ref[me]

    def whole(ref, sem, count):
        part = ref.at[pl.ds(0, count)]
        pltpu.make_async_copy(part, part, sem).wait()

    def send_map(src_ref, dst_ref, phase, chunk):
        for later in range(1, GROUP):

            @pl.when(g + later < GROUP)
            def _():
                pltpu.make_async_remote_copy(
                    src_ref=src_ref.at[chunk],
                    dst_ref=dst_ref.at[g, chunk],
                    send_sem=map_send.at[phase],
                    recv_sem=map_recv.at[phase, g],
                    device_id=(tm + GROUP * later, trans),
                    device_id_type=MESH,
                ).start()

    def enter(dst_ref, phase, total):
        total[...] = jnp.zeros_like(total)
        for k in range(GROUP - 1):

            @pl.when(k < g)
            def _():
                pltpu.make_async_copy(dst_ref.at[k], dst_ref.at[k], map_recv.at[phase, k]).wait()
                for chunk in range(4):
                    total[chunk] = dst_ref[k, chunk, 0] * total[chunk] + dst_ref[k, chunk, 1]

    def send_own(src_ref, dst_ref, phase, i):
        @pl.when(i != s)
        def _():
            pltpu.make_async_remote_copy(
                src_ref=src_ref.at[i],
                dst_ref=dst_ref.at[s],
                send_sem=own_send.at[phase],
                recv_sem=own_recv.at[phase, s],
                device_id=(GROUP * g + i, trans),
                device_id_type=MESH,
            ).start()

    lane = lax.broadcasted_iota(jnp.int32, (8, LANES), 1)
    sub = lax.broadcasted_iota(jnp.int32, (8, LANES), 0)
    group = lane // 16
    top = sub < 4

    def flip(v):
        return roll(v, 4, 0)

    def spectral():
        freq = dot(stage[...], wf[...])
        for k in range(RADIX):
            rows = slice(32 * k, 32 * k + 32)
            re, im = freq[rows, :LANES], freq[rows, LANES:]
            pr, pi = turns[1, k : k + 1, :], turns[0, k : k + 1, :]
            stage[rows, :LANES] = re * pr - im * pi
            stage[rows, LANES:] = re * pi + im * pr
        stage[...] = dot(stage[...], wb[...])

    def forward(blocks, w):
        for k, (re, im) in enumerate(radix8(blocks, -1)):
            rows = slice(32 * k + 8 * w, 32 * k + 8 * w + 8)
            c, d = tw[0, k : k + 1, :], tw[1, k : k + 1, :]
            stage[rows, :LANES] = re * c + im * d
            stage[rows, LANES:] = im * c - re * d

    def back(w):
        parts = []
        for k in range(RADIX):
            rows = slice(32 * k + 8 * w, 32 * k + 8 * w + 8)
            re, im = stage[rows, :LANES], stage[rows, LANES:]
            c, d = tw[0, k : k + 1, :], tw[1, k : k + 1, :]
            parts.append((re * c - im * d, im * c + re * d))
        return radix8(parts, 1)

    loads[0].wait()
    loads[1].wait()
    for xh in range(2):
        for t in range(2):
            forward(
                [
                    tuple(field[c, pl.ds(128 * xh + 2 * a + t, 8, stride=16), :] for c in range(2))
                    for a in range(RADIX)
                ],
                2 * xh + t,
            )
    for load in loads[2:6]:
        load.wait()
    picked = jnp.concatenate(
        [jnp.where(lane % RADIX == sub, phy[r : r + 1, :], 0.0) for r in range(RADIX)], axis=0
    )
    picked = dot(picked, sp[...])
    phase = jnp.zeros((8, LANES), F32)
    for r in range(RADIX):
        phase = jnp.where(group == r, picked[8 * r : 8 * r + 8, :], phase)
    sin, cos = sincos(phase)
    turns[0] = sin * (1.0 / NY)
    turns[1] = cos * (1.0 / NY)
    spectral()
    parts = [back(w) for w in range(4)]
    for a in range(RADIX):
        mixed = transpose_lanes(
            [parts[2 * xh + t][a][c] for xh in range(2) for c in range(2) for t in range(2)], 16
        )
        for j in range(8):
            send1[8 * a + j] = mixed[j]

    pl.semaphore_wait(barrier, TEAM - 1 + g)
    exchange(send1, recv1, 0)
    for k in range(GROUP - 1):

        @pl.when(k < g)
        def _():
            pl.semaphore_signal(
                ready, inc=1, device_id=(GROUP * k + s, trans), device_id_type=MESH
            )

    for load in loads[6:]:
        load.wait()
    sin, cos = sincos(phx[...])
    sin, cos = sin * (1.0 / NX), cos * (1.0 / NX)
    cx, sx = tx[:, :NX], tx[:, NX:]
    bmat[:NX, :] = cx * cos - sx * sin
    bmat[NX:, :] = cx * sin + sx * cos
    both = dot(bmat[...], tx[...])
    mmat[:NX, :] = both[:NX, :NX] + both[NX:, NX:]
    mmat[NX:, :] = both[NX:, :NX] - both[:NX, NX:]
    for m in range(NX // 8):
        for half in range(2):
            cols = slice(LANES * half, LANES * (half + 1))
            re, im = mmat[8 * m : 8 * m + 8, cols], mmat[NX + 8 * m : NX + 8 * m + 8, cols]
            mmix[16 * m : 16 * m + 8, cols] = jnp.where(top, re, flip(im))
            mmix[16 * m + 8 : 16 * m + 16, cols] = jnp.where(top, flip(re), im)
    mine = group == lax.rem(me, 8)
    for m in range(NX // 8):
        rows = slice(8 * m, 8 * m + 8)
        v = jnp.where(mine, dens1[rows, :], 0.0)
        for shift in (16, 32, 64):
            v = v + roll(v, shift, 1)
        densx[rows, :] = v
    for r in range(4):
        line = dens2[pl.ds(4 * s + r, 1), :]
        densy[r : r + 1, :] = line
        densy[r + 4 : r + 5, :] = line

    whole(recv1, team_recv.at[0], TEAM - 1)
    for p in range(N):
        mixed = transpose_lanes([recv1[4 * p + k] for k in range(4)], 32)
        for xh in range(2):
            for c in range(2):
                work[c, 16 * p + 8 * xh : 16 * p + 8 * xh + 8, :] = mixed[2 * xh + c]
    both = dot(mmat[...], jnp.concatenate([work[0], work[1]], axis=1))
    work[0] = both[:NX, :LANES] - both[NX:, LANES:]
    work[1] = both[NX:, :LANES] + both[:NX, LANES:]

    @pl.when(g < GROUP - 1)
    def _():
        pl.semaphore_wait(ready, GROUP - 1 - g)

    for chunk in range(4):
        maps = [jnp.zeros((8, LANES), F32)] * 2
        for i in range(8):
            rows = slice(64 * chunk + 8 * i, 64 * chunk + 8 * i + 8)
            intensity, grow, add = rates(work[0, rows, :], work[1, rows, :], densx[rows, :])
            for bit in (1, 2, 4):
                there = group >= bit
                grow2, add2 = roll(grow, 16 * bit, 1), roll(add, 16 * bit, 1)
                add = jnp.where(there, grow * add2 + add, add)
                grow = jnp.where(there, grow * grow2, grow)
            phase0[rows, :] = KERR_COEF * intensity - PLASMA * add
            gain[rows, :] = PLASMA * grow
            maps = [
                jnp.where(group == i, roll(v, 16 * (i + 1), 1), old)
                for v, old in zip((grow, add), maps)
            ]
        send2[chunk, 0] = maps[0]
        send2[chunk, 1] = maps[1]
        send_map(send2, recv2, 0, chunk)
    enter(recv2, 0, ent)
    for chunk in range(4):
        for i, entering in enumerate(spread_lanes(ent[chunk])):
            rows = slice(64 * chunk + 8 * i, 64 * chunk + 8 * i + 8)
            sin, cos = sincos(phase0[rows, :] - gain[rows, :] * entering)
            re, im = work[0, rows, :], work[1, rows, :]
            work[0, rows, :] = re * cos - im * sin
            work[1, rows, :] = re * sin + im * cos

    both = dot(mmix[...], jnp.concatenate([work[0], work[1]], axis=1))
    for k in range(TEAM):
        rows = slice(8 * k, 8 * k + 8)
        turned = flip(both[rows, LANES:])
        send4[k] = both[rows, :LANES] + jnp.where(top, -turned, turned)
    exchange(send4, recv4, 1)
    whole(recv4, team_recv.at[1], TEAM - 1)

    for a in range(RADIX):
        times = transpose_lanes([recv4[8 * a + j] for j in range(8)], 16)
        for i in range(4):
            u, v = times[2 * i], times[2 * i + 1]
            fold[i, a, 0] = jnp.where(top, u, flip(v))
            fold[i, a, 1] = jnp.where(top, flip(u), v)
    for i in range(4):
        forward([(fold[i, a, 0], fold[i, a, 1]) for a in range(RADIX)], i)
    spectral()
    maps = [None] * 4
    for i in range(4):
        fields = back(i)
        pairs = []
        for a in range(RADIX):
            re, im = fields[a]
            sende[i, a, 0] = re
            sende[i, a, 1] = im
            _, decays, source = rates(re, im, densy[:, LANES * a : LANES * (a + 1)])
            dec[i, a] = decays
            src[i, a] = source
            pairs.append((decays * flip(decays), decays * flip(source) + source))
        for h in range(4):
            even, odd = pairs[2 * h], pairs[2 * h + 1]
            grow = jnp.where(top, even[0], odd[0])
            add = jnp.where(top, flip(even[1]), odd[1])
            if maps[h] is not None:
                grow, add = grow * maps[h][0], grow * maps[h][1] + add
            maps[h] = (grow, add)
    for h in range(4):
        send5[h, 0] = maps[h][0]
        send5[h, 1] = maps[h][1]
        send_map(send5, recv5, 1, h)
    for i in range(GROUP):
        send_own(sende, recve, 0, i)
    recve[s] = sende[s]

    enter(recv5, 1, ent5)
    current = []
    for h in range(4):
        v = ent5[h]
        turned = flip(v)
        current += [jnp.where(top, v, turned), jnp.where(top, turned, v)]
    for i in range(4):
        for a in range(RADIX):
            decays, source = dec[i, a], src[i, a]
            first = decays * current[a] + source
            electrons = decays * jnp.where(top, current[a], flip(first)) + source
            send6[i, a] = electrons
            current[a] = jnp.where(top, flip(electrons), electrons)
        send_own(send6, recv6, 1, i)
    recv6[s] = send6[s]

    for k in range(GROUP):

        @pl.when(k != s)
        def _():
            pltpu.make_async_copy(recve.at[k], recve.at[k], own_recv.at[0, k]).wait()
            pltpu.make_async_copy(recv6.at[k], recv6.at[k], own_recv.at[1, k]).wait()

        for a in range(RADIX):
            re, im, electrons = recve[k, a, 0], recve[k, a, 1], recv6[k, a]
            intensity = re * re + im * im
            sin, cos = sincos(KERR_COEF * intensity - PLASMA * electrons)
            new_re, new_im = re * cos - im * sin, re * sin + im * cos
            for t in range(2):
                rows = pl.ds(64 * k + 2 * a + t, 4, stride=16)
                part = slice(4 * t, 4 * t + 4)
                out[0, rows, :] = new_re[part]
                out[1, rows, :] = new_im[part]
                ele[rows, :] = electrons[part]

    whole(send1, team_send.at[0], TEAM - 1)
    whole(send4, team_send.at[1], TEAM - 1)
    whole(sende, own_send.at[0], GROUP - 1)
    whole(send6, own_send.at[1], GROUP - 1)
    for later in range(1, GROUP):

        @pl.when(g + later < GROUP)
        def _():
            for phase_index, ref in enumerate((send2, send5)):
                whole(ref, map_send.at[phase_index], 4)


def local(light_field, gas_density, phase_x, phase_y):
    consts = tables()
    rows = light_field.reshape(2, 16, 2, RADIX, LANES).transpose(0, 1, 3, 2, 4).reshape(2, NX, LANES)
    vmem = lambda *shape: pltpu.VMEM(shape, F32)
    team = vmem(TEAM, 8, LANES)
    chunks = vmem(4, 2, 8, LANES)
    incoming = vmem(GROUP - 1, 4, 2, 8, LANES)
    tall = vmem(4, RADIX, 8, LANES)
    fields = vmem(4, RADIX, 2, 8, LANES)
    plane = vmem(NX, LANES)
    out, ele = pl.pallas_call(
        kernel,
        out_shape=(
            jax.ShapeDtypeStruct((2, NX, LANES), F32),
            jax.ShapeDtypeStruct((NX, LANES), F32),
        ),
        in_specs=[pl.BlockSpec(memory_space=pltpu.HBM)] * 9,
        out_specs=(pl.BlockSpec(memory_space=pltpu.VMEM),) * 2,
        scratch_shapes=[
            vmem(2, NX, LANES), plane, vmem(16, NY), vmem(1, NX), vmem(8, LANES),
            vmem(NX, 2 * NX), vmem(NX, NX), vmem(NX, NX), vmem(2, 8, LANES), vmem(LANES, LANES),
            vmem(NX, NX), vmem(2 * NX, NX), vmem(2 * NX, NX), vmem(2 * NX, NX),
            vmem(2, 8, LANES), plane, vmem(8, NY),
            team, team, vmem(2, NX, LANES), plane, plane,
            chunks, incoming, vmem(4, 8, LANES), team, team, fields, tall, tall, tall,
            fields, fields, chunks, incoming, vmem(4, 8, LANES), tall, tall,
            pltpu.SemaphoreType.DMA((10,)),
            pltpu.SemaphoreType.REGULAR,
            pltpu.SemaphoreType.DMA((2,)),
            pltpu.SemaphoreType.DMA((2,)),
            pltpu.SemaphoreType.DMA((2,)),
            pltpu.SemaphoreType.DMA((2, GROUP - 1)),
            pltpu.SemaphoreType.DMA((2,)),
            pltpu.SemaphoreType.DMA((2, GROUP)),
        ],
        compiler_params=pltpu.CompilerParams(
            collective_id=0, has_side_effects=True, vmem_limit_bytes=24 * 1024 * 1024
        ),
        name="split_step",
    )(
        *(
            pltpu.with_memory_space_constraint(array, pltpu.HBM)
            for array in (
                rows, gas_density, phase_x.reshape(1, NX), phase_y.reshape(RADIX, LANES), *consts
            )
        )
    )
    out = out.reshape(2, 16, RADIX, 2, LANES).transpose(0, 1, 3, 2, 4).reshape(2, 16, 2, NY)
    ele = ele.reshape(16, RADIX, 2, LANES).transpose(0, 2, 1, 3).reshape(16, 2, NY)
    return out, ele


def solution(mesh):
    placed = (P(None, "trans", "tm", None), P(), P(), P())
    return jax.shard_map(
        local,
        mesh=mesh,
        in_specs=placed,
        out_specs=(P(None, "trans", "tm", None), P("trans", "tm", None)),
        check_vma=False,
    )
```

```python
import functools
import math

import jax
import jax.numpy as jnp
import numpy as np
from jax import lax
from jax.experimental import pallas as pl
from jax.experimental.pallas import tpu as pltpu
from jax.sharding import PartitionSpec as P

RATE_COEF = 1.8e-08
RECOMB = 0.02
KERR_COEF = 0.3
PLASMA = 4.0

N = 16
LANES = 128
GROUP = 4
TEAM = N * GROUP
NX = 256
NY = 1024
RADIX = 8

F32 = jnp.float32
MESH = pl.DeviceIdType.MESH
ROOT_HALF = math.sqrt(0.5)


FAR_FIRST = sorted(
    (
        (dy, dx, dz, dc)
        for dy in range(4)
        for dx in range(4)
        for dz in range(2)
        for dc in range(2)
        if dy or dx or dz or dc
    ),
    key=lambda d: -(min(d[0], 4 - d[0]) + min(d[1], 4 - d[1]) + d[2]) - 0.1 * d[3],
)


def tables():
    j = np.arange(NX)
    angle = 2.0 * np.pi * ((j[:, None] * j[None, :]) % NX) / NX
    table_x = np.concatenate([np.cos(angle), np.sin(angle)], axis=1)
    b = np.arange(LANES)
    angle = 2.0 * np.pi * ((b[:, None] * b[None, :]) % LANES) / LANES
    c, s = np.cos(angle), np.sin(angle)
    forward = np.block([[c, -s], [s, c]])
    backward = np.block([[c, s], [-s, c]])
    k = np.arange(RADIX)
    angle = 2.0 * np.pi * (k[:, None] * b[None, :]) / NY
    twist = np.stack([np.cos(angle), np.sin(angle)])
    spread = (b[None, :] % 16 == b[:, None] // RADIX).astype(np.float32)
    return [np.asarray(t, np.float32) for t in (table_x, forward, backward, twist, spread)]


def sincos(x):
    n = jnp.floor(x * (2.0 / math.pi) + 0.5)
    r = x - n * 1.5703125
    r = r - n * 4.837512969970703125e-4
    r = r - n * 7.54978995489188216e-8
    z = r * r
    s = r + r * z * (-1.6666654611e-1 + z * (8.3321608736e-3 + z * -1.9515295891e-4))
    c = 1.0 - 0.5 * z + z * z * (
        4.166664568298827e-2 + z * (-1.388731625493765e-3 + z * 2.443315711809948e-5)
    )
    q = n.astype(jnp.int32)
    odd = (q & 1) == 1
    sin = jnp.where(odd, c, s)
    cos = jnp.where(odd, s, c)
    sin = jnp.where((q & 2) == 2, -sin, sin)
    cos = jnp.where(((q + 1) & 2) == 2, -cos, cos)
    return sin, cos


def dot(a, b):
    return lax.dot_general(
        a,
        b,
        (((1,), (0,)), ((), ())),
        precision=lax.Precision.HIGHEST,
        preferred_element_type=F32,
    )


def cadd(a, b):
    return (a[0] + b[0], a[1] + b[1])


def csub(a, b):
    return (a[0] - b[0], a[1] - b[1])


def radix8(x, sign):
    def turn(v):
        return (-v[1], v[0]) if sign > 0 else (v[1], -v[0])

    def four(p, q, r, s):
        e0, e1, e2, e3 = cadd(p, r), csub(p, r), cadd(q, s), turn(csub(q, s))
        return cadd(e0, e2), cadd(e1, e3), csub(e0, e2), csub(e1, e3)

    e = four(x[0], x[2], x[4], x[6])
    o = four(x[1], x[3], x[5], x[7])
    t1, t3 = turn(o[1]), turn(o[3])
    w1 = ((o[1][0] + t1[0]) * ROOT_HALF, (o[1][1] + t1[1]) * ROOT_HALF)
    w3 = ((t3[0] - o[3][0]) * ROOT_HALF, (t3[1] - o[3][1]) * ROOT_HALF)
    o = (o[0], w1, turn(o[2]), w3)
    return [cadd(e[k], o[k]) for k in range(4)] + [csub(e[k], o[k]) for k in range(4)]


def roll(v, by, axis):
    return pltpu.roll(v, by % v.shape[axis], axis)


def transpose_lanes(blocks, width):
    blocks = list(blocks)
    group = lax.broadcasted_iota(jnp.int32, (8, LANES), 1) // width
    bit = len(blocks) // 2
    while bit:
        clear = lax.rem(group // bit, 2) == 0
        for u in range(len(blocks)):
            if u & bit == 0:
                p, q = blocks[u], blocks[u | bit]
                blocks[u] = jnp.where(clear, p, roll(q, bit * width, 1))
                blocks[u | bit] = jnp.where(clear, roll(p, -bit * width, 1), q)
        bit //= 2
    return blocks


def spread_lanes(v):
    group = lax.broadcasted_iota(jnp.int32, (8, LANES), 1) // 16
    out = [v]
    for bit in (4, 2, 1):
        clear = lax.rem(group // bit, 2) == 0
        nxt = []
        for x in out:
            nxt.append(jnp.where(clear, x, roll(x, 16 * bit, 1)))
            nxt.append(jnp.where(clear, roll(x, -16 * bit, 1), x))
        out = nxt
    return out


def rates(re, im, dens):
    intensity = re * re + im * im
    power = intensity * intensity
    power = power * power
    power = power * power
    rate = RATE_COEF * power
    lost = rate + RECOMB
    decays = jnp.exp(-lost)
    source = (1.0 - decays) * dens * (rate / lost)
    return intensity, decays, source


def kernel(
    field_hbm, dens_hbm, phx_hbm, phy_hbm, tx_hbm, wf_hbm, wb_hbm, tw_hbm, sp_hbm,
    out, ele,
    field, dens1, dens2, phx, phy, tx, wf, wb, tw, sp,
    stage, bmat, mmat, mmix, turns, densx, densy,
    send1, recv1, work, gain, phase0,
    send2, recv2, ent, send4, recv4, fold, dec, src, inten,
    sende, recve, send5, recv5, ent5, send6, recv6,
    in_sems, ready, team_send, team_recv, map_send, map_recv, own_send, own_recv,
):
    tm = lax.axis_index("tm")
    trans = lax.axis_index("trans")
    g = tm // GROUP
    s = lax.rem(tm, GROUP)
    me = GROUP * trans + s

    barrier = pltpu.get_barrier_semaphore()

    ys = [GROUP * lax.rem(trans // 4 + d, 4) for d in range(4)]
    xs = [lax.rem(trans + d, 4) for d in range(4)]
    zs = [2 * lax.rem(s // 2 + d, 2) for d in range(2)]
    cs = [lax.rem(s + d, 2) for d in range(2)]
    mates = []
    for dy, dx, dz, dc in FAR_FIRST:
        other, slot = ys[dy] + xs[dx], zs[dz] + cs[dc]
        mates.append(((GROUP * g + slot, other), GROUP * other + slot))

    row0 = pl.multiple_of(trans * N, N)
    col0 = pl.multiple_of((me // 8) * LANES, LANES)
    loads = [
        pltpu.make_async_copy(a, b, in_sems.at[i])
        for i, (a, b) in enumerate(
            [
                (field_hbm, field),
                (tw_hbm, tw),
                (wf_hbm, wf),
                (phy_hbm, phy),
                (sp_hbm, sp),
                (wb_hbm, wb),
                (phx_hbm, phx),
                (tx_hbm, tx),
                (dens_hbm.at[:, pl.ds(col0, LANES)], dens1),
                (dens_hbm.at[pl.ds(row0, N), :], dens2),
            ]
        )
    ]
    for load in loads[:3]:
        load.start()
    for where_to, _ in mates:
        pl.semaphore_signal(barrier, inc=1, device_id=where_to, device_id_type=MESH)
    for load in loads[3:]:
        load.start()
    for later in range(1, GROUP):

        @pl.when(g + later < GROUP)
        def _():
            pl.semaphore_signal(
                barrier, inc=1, device_id=(tm + GROUP * later, trans), device_id_type=MESH
            )

    def exchange(src_ref, dst_ref, phase):
        for where_to, slot in mates:
            pltpu.make_async_remote_copy(
                src_ref=src_ref.at[slot],
                dst_ref=dst_ref.at[me],
                send_sem=team_send.at[phase],
                recv_sem=team_recv.at[phase],
                device_id=where_to,
                device_id_type=MESH,
            ).start()
        dst_ref[me] = src_ref[me]

    def whole(ref, sem, count):
        part = ref.at[pl.ds(0, count)]
        pltpu.make_async_copy(part, part, sem).wait()

    def send_map(src_ref, dst_ref, phase, chunk):
        for later in range(1, GROUP):

            @pl.when(g + later < GROUP)
            def _():
                pltpu.make_async_remote_copy(
                    src_ref=src_ref.at[chunk],
                    dst_ref=dst_ref.at[g, chunk],
                    send_sem=map_send.at[phase],
                    recv_sem=map_recv.at[phase, g],
                    device_id=(tm + GROUP * later, trans),
                    device_id_type=MESH,
                ).start()

    def enter(dst_ref, phase, total):
        total[...] = jnp.zeros_like(total)
        for k in range(GROUP - 1):

            @pl.when(k < g)
            def _():
                pltpu.make_async_copy(dst_ref.at[k], dst_ref.at[k], map_recv.at[phase, k]).wait()
                for chunk in range(4):
                    total[chunk] = dst_ref[k, chunk, 0] * total[chunk] + dst_ref[k, chunk, 1]

    def send_own(src_ref, dst_ref, phase, i):
        @pl.when(i != s)
        def _():
            pltpu.make_async_remote_copy(
                src_ref=src_ref.at[i],
                dst_ref=dst_ref.at[s],
                send_sem=own_send.at[phase],
                recv_sem=own_recv.at[phase, s],
                device_id=(GROUP * g + i, trans),
                device_id_type=MESH,
            ).start()

    lane = lax.broadcasted_iota(jnp.int32, (8, LANES), 1)
    sub = lax.broadcasted_iota(jnp.int32, (8, LANES), 0)
    group = lane // 16
    top = sub < 4

    def flip(v):
        return roll(v, 4, 0)

    def spectral():
        freq = dot(stage[...], wf[...])
        for k in range(RADIX):
            rows = slice(32 * k, 32 * k + 32)
            re, im = freq[rows, :LANES], freq[rows, LANES:]
            pr, pi = turns[1, k : k + 1, :], turns[0, k : k + 1, :]
            stage[rows, :LANES] = re * pr - im * pi
            stage[rows, LANES:] = re * pi + im * pr
        stage[...] = dot(stage[...], wb[...])

    def forward(blocks, w):
        for k, (re, im) in enumerate(radix8(blocks, -1)):
            rows = slice(32 * k + 8 * w, 32 * k + 8 * w + 8)
            c, d = tw[0, k : k + 1, :], tw[1, k : k + 1, :]
            stage[rows, :LANES] = re * c + im * d
            stage[rows, LANES:] = im * c - re * d

    def back(w):
        parts = []
        for k in range(RADIX):
            rows = slice(32 * k + 8 * w, 32 * k + 8 * w + 8)
            re, im = stage[rows, :LANES], stage[rows, LANES:]
            c, d = tw[0, k : k + 1, :], tw[1, k : k + 1, :]
            parts.append((re * c - im * d, im * c + re * d))
        return radix8(parts, 1)

    loads[0].wait()
    loads[1].wait()
    for xh in range(2):
        for t in range(2):
            forward(
                [
                    tuple(field[c, pl.ds(128 * xh + 2 * a + t, 8, stride=16), :] for c in range(2))
                    for a in range(RADIX)
                ],
                2 * xh + t,
            )
    for load in loads[2:6]:
        load.wait()
    picked = jnp.concatenate(
        [jnp.where(lane % RADIX == sub, phy[r : r + 1, :], 0.0) for r in range(RADIX)], axis=0
    )
    picked = dot(picked, sp[...])
    phase = jnp.zeros((8, LANES), F32)
    for r in range(RADIX):
        phase = jnp.where(group == r, picked[8 * r : 8 * r + 8, :], phase)
    sin, cos = sincos(phase)
    turns[0] = sin * (1.0 / NY)
    turns[1] = cos * (1.0 / NY)
    spectral()
    parts = [back(w) for w in range(4)]
    for a in range(RADIX):
        mixed = transpose_lanes(
            [parts[2 * xh + t][a][c] for xh in range(2) for c in range(2) for t in range(2)], 16
        )
        for j in range(8):
            send1[8 * a + j] = mixed[j]

    pl.semaphore_wait(barrier, TEAM - 1 + g)
    exchange(send1, recv1, 0)
    for k in range(GROUP - 1):

        @pl.when(k < g)
        def _():
            pl.semaphore_signal(
                ready, inc=1, device_id=(GROUP * k + s, trans), device_id_type=MESH
            )

    for load in loads[6:]:
        load.wait()
    sin, cos = sincos(phx[...])
    sin, cos = sin * (1.0 / NX), cos * (1.0 / NX)
    cx, sx = tx[:, :NX], tx[:, NX:]
    bmat[:NX, :] = cx * cos - sx * sin
    bmat[NX:, :] = cx * sin + sx * cos
    both = dot(bmat[...], tx[...])
    mmat[:NX, :] = both[:NX, :NX] + both[NX:, NX:]
    mmat[NX:, :] = both[NX:, :NX] - both[:NX, NX:]
    for m in range(NX // 8):
        for half in range(2):
            cols = slice(LANES * half, LANES * (half + 1))
            re, im = mmat[8 * m : 8 * m + 8, cols], mmat[NX + 8 * m : NX + 8 * m + 8, cols]
            mmix[16 * m : 16 * m + 8, cols] = jnp.where(top, re, flip(im))
            mmix[16 * m + 8 : 16 * m + 16, cols] = jnp.where(top, flip(re), im)
    mine = group == lax.rem(me, 8)
    for m in range(NX // 8):
        rows = slice(8 * m, 8 * m + 8)
        v = jnp.where(mine, dens1[rows, :], 0.0)
        for shift in (16, 32, 64):
            v = v + roll(v, shift, 1)
        densx[rows, :] = v
    for r in range(4):
        line = dens2[pl.ds(4 * s + r, 1), :]
        densy[r : r + 1, :] = line
        densy[r + 4 : r + 5, :] = line

    whole(recv1, team_recv.at[0], TEAM - 1)
    for p in range(N):
        mixed = transpose_lanes([recv1[4 * p + k] for k in range(4)], 32)
        for xh in range(2):
            for c in range(2):
                work[c, 16 * p + 8 * xh : 16 * p + 8 * xh + 8, :] = mixed[2 * xh + c]
    both = dot(mmat[...], jnp.concatenate([work[0], work[1]], axis=1))
    work[0] = both[:NX, :LANES] - both[NX:, LANES:]
    work[1] = both[NX:, :LANES] + both[:NX, LANES:]

    @pl.when(g < GROUP - 1)
    def _():
        pl.semaphore_wait(ready, GROUP - 1 - g)

    for chunk in range(4):
        maps = [jnp.zeros((8, LANES), F32)] * 2
        for i in range(8):
            rows = slice(64 * chunk + 8 * i, 64 * chunk + 8 * i + 8)
            intensity, grow, add = rates(work[0, rows, :], work[1, rows, :], densx[rows, :])
            for bit in (1, 2, 4):
                there = group >= bit
                grow2, add2 = roll(grow, 16 * bit, 1), roll(add, 16 * bit, 1)
                add = jnp.where(there, grow * add2 + add, add)
                grow = jnp.where(there, grow * grow2, grow)
            phase0[rows, :] = KERR_COEF * intensity - PLASMA * add
            gain[rows, :] = PLASMA * grow
            maps = [
                jnp.where(group == i, roll(v, 16 * (i + 1), 1), old)
                for v, old in zip((grow, add), maps)
            ]
        send2[chunk, 0] = maps[0]
        send2[chunk, 1] = maps[1]
        send_map(send2, recv2, 0, chunk)
    enter(recv2, 0, ent)
    for chunk in range(4):
        for i, entering in enumerate(spread_lanes(ent[chunk])):
            rows = slice(64 * chunk + 8 * i, 64 * chunk + 8 * i + 8)
            sin, cos = sincos(phase0[rows, :] - gain[rows, :] * entering)
            re, im = work[0, rows, :], work[1, rows, :]
            work[0, rows, :] = re * cos - im * sin
            work[1, rows, :] = re * sin + im * cos

    both = dot(mmix[...], jnp.concatenate([work[0], work[1]], axis=1))
    for k in range(TEAM):
        rows = slice(8 * k, 8 * k + 8)
        turned = flip(both[rows, LANES:])
        send4[k] = both[rows, :LANES] + jnp.where(top, -turned, turned)
    exchange(send4, recv4, 1)
    whole(recv4, team_recv.at[1], TEAM - 1)

    for a in range(RADIX):
        times = transpose_lanes([recv4[8 * a + j] for j in range(8)], 16)
        for i in range(4):
            u, v = times[2 * i], times[2 * i + 1]
            fold[i, a, 0] = jnp.where(top, u, flip(v))
            fold[i, a, 1] = jnp.where(top, flip(u), v)
    for i in range(4):
        forward([(fold[i, a, 0], fold[i, a, 1]) for a in range(RADIX)], i)
    spectral()
    maps = [None] * 4
    for i in range(4):
        fields = back(i)
        pairs = []
        for a in range(RADIX):
            re, im = fields[a]
            sende[i, a, 0] = re
            sende[i, a, 1] = im
            _, decays, source = rates(re, im, densy[:, LANES * a : LANES * (a + 1)])
            dec[i, a] = decays
            src[i, a] = source
            pairs.append((decays * flip(decays), decays * flip(source) + source))
        for h in range(4):
            even, odd = pairs[2 * h], pairs[2 * h + 1]
            grow = jnp.where(top, even[0], odd[0])
            add = jnp.where(top, flip(even[1]), odd[1])
            if maps[h] is not None:
                grow, add = grow * maps[h][0], grow * maps[h][1] + add
            maps[h] = (grow, add)
    for h in range(4):
        send5[h, 0] = maps[h][0]
        send5[h, 1] = maps[h][1]
        send_map(send5, recv5, 1, h)
    for i in range(GROUP):
        send_own(sende, recve, 0, i)
    recve[s] = sende[s]

    enter(recv5, 1, ent5)
    current = []
    for h in range(4):
        v = ent5[h]
        turned = flip(v)
        current += [jnp.where(top, v, turned), jnp.where(top, turned, v)]
    for i in range(4):
        for a in range(RADIX):
            decays, source = dec[i, a], src[i, a]
            first = decays * current[a] + source
            electrons = decays * jnp.where(top, current[a], flip(first)) + source
            send6[i, a] = electrons
            current[a] = jnp.where(top, flip(electrons), electrons)
        send_own(send6, recv6, 1, i)
    recv6[s] = send6[s]

    for k in range(GROUP):

        @pl.when(k != s)
        def _():
            pltpu.make_async_copy(recve.at[k], recve.at[k], own_recv.at[0, k]).wait()
            pltpu.make_async_copy(recv6.at[k], recv6.at[k], own_recv.at[1, k]).wait()

        for a in range(RADIX):
            re, im, electrons = recve[k, a, 0], recve[k, a, 1], recv6[k, a]
            intensity = re * re + im * im
            sin, cos = sincos(KERR_COEF * intensity - PLASMA * electrons)
            new_re, new_im = re * cos - im * sin, re * sin + im * cos
            for t in range(2):
                rows = pl.ds(64 * k + 2 * a + t, 4, stride=16)
                part = slice(4 * t, 4 * t + 4)
                out[0, rows, :] = new_re[part]
                out[1, rows, :] = new_im[part]
                ele[rows, :] = electrons[part]

    whole(send1, team_send.at[0], TEAM - 1)
    whole(send4, team_send.at[1], TEAM - 1)
    whole(sende, own_send.at[0], GROUP - 1)
    whole(send6, own_send.at[1], GROUP - 1)
    for later in range(1, GROUP):

        @pl.when(g + later < GROUP)
        def _():
            for phase_index, ref in enumerate((send2, send5)):
                whole(ref, map_send.at[phase_index], 4)


def finish(a, b, c, d, sems):
    copies = [
        pltpu.make_async_copy(x, y, sems.at[i]) for i, (x, y) in enumerate([(a, c), (b, d)])
    ]
    for copy in copies:
        copy.start()
    for copy in copies:
        copy.wait()


def local(light_field, gas_density, phase_x, phase_y):
    consts = tables()
    rows = light_field.reshape(2, 16, 2, RADIX, LANES).transpose(0, 1, 3, 2, 4).reshape(2, NX, LANES)
    vmem = lambda *shape: pltpu.VMEM(shape, F32)
    team = vmem(TEAM, 8, LANES)
    chunks = vmem(4, 2, 8, LANES)
    incoming = vmem(GROUP - 1, 4, 2, 8, LANES)
    tall = vmem(4, RADIX, 8, LANES)
    fields = vmem(4, RADIX, 2, 8, LANES)
    plane = vmem(NX, LANES)
    out, ele = pl.pallas_call(
        kernel,
        out_shape=(
            jax.ShapeDtypeStruct((2, NX, LANES), F32),
            jax.ShapeDtypeStruct((NX, LANES), F32),
        ),
        in_specs=[pl.BlockSpec(memory_space=pltpu.HBM)] * 9,
        out_specs=(pl.BlockSpec(memory_space=pltpu.VMEM),) * 2,
        scratch_shapes=[
            vmem(2, NX, LANES), plane, vmem(16, NY), vmem(1, NX), vmem(8, LANES),
            vmem(NX, 2 * NX), vmem(NX, NX), vmem(NX, NX), vmem(2, 8, LANES), vmem(LANES, LANES),
            vmem(NX, NX), vmem(2 * NX, NX), vmem(2 * NX, NX), vmem(2 * NX, NX),
            vmem(2, 8, LANES), plane, vmem(8, NY),
            team, team, vmem(2, NX, LANES), plane, plane,
            chunks, incoming, vmem(4, 8, LANES), team, team, fields, tall, tall, tall,
            fields, fields, chunks, incoming, vmem(4, 8, LANES), tall, tall,
            pltpu.SemaphoreType.DMA((10,)),
            pltpu.SemaphoreType.REGULAR,
            pltpu.SemaphoreType.DMA((2,)),
            pltpu.SemaphoreType.DMA((2,)),
            pltpu.SemaphoreType.DMA((2,)),
            pltpu.SemaphoreType.DMA((2, GROUP - 1)),
            pltpu.SemaphoreType.DMA((2,)),
            pltpu.SemaphoreType.DMA((2, GROUP)),
        ],
        compiler_params=pltpu.CompilerParams(
            collective_id=0, has_side_effects=True, vmem_limit_bytes=24 * 1024 * 1024
        ),
        name="split_step",
    )(
        *(
            pltpu.with_memory_space_constraint(array, pltpu.HBM)
            for array in (
                rows, gas_density, phase_x.reshape(1, NX), phase_y.reshape(RADIX, LANES), *consts
            )
        )
    )
    out, ele = pl.pallas_call(
        finish,
        out_shape=(
            jax.ShapeDtypeStruct((2, NX, LANES), F32),
            jax.ShapeDtypeStruct((NX, LANES), F32),
        ),
        in_specs=[pl.BlockSpec(memory_space=pltpu.VMEM)] * 2,
        out_specs=(pl.BlockSpec(memory_space=pltpu.HBM),) * 2,
        scratch_shapes=[pltpu.SemaphoreType.DMA((2,))],
        compiler_params=pltpu.CompilerParams(vmem_limit_bytes=1024 * 1024),
        name="finish",
    )(out, ele)
    out = out.reshape(2, 16, RADIX, 2, LANES).transpose(0, 1, 3, 2, 4).reshape(2, 16, 2, NY)
    ele = ele.reshape(16, RADIX, 2, LANES).transpose(0, 2, 1, 3).reshape(16, 2, NY)
    return out, ele


def solution(mesh):
    placed = (P(None, "trans", "tm", None), P(), P(), P())
    return jax.shard_map(
        local,
        mesh=mesh,
        in_specs=placed,
        out_specs=(P(None, "trans", "tm", None), P("trans", "tm", None)),
        check_vma=False,
    )
```

```python
import functools
import math

import jax
import jax.numpy as jnp
import numpy as np
from jax import lax
from jax.experimental import pallas as pl
from jax.experimental.pallas import tpu as pltpu
from jax.sharding import PartitionSpec as P

RATE_COEF = 1.8e-08
RECOMB = 0.02
KERR_COEF = 0.3
PLASMA = 4.0

N = 16
LANES = 128
GROUP = 4
TEAM = N * GROUP
NX = 256
NY = 1024
RADIX = 8

F32 = jnp.float32
MESH = pl.DeviceIdType.MESH
ROOT_HALF = math.sqrt(0.5)


FAR_FIRST = sorted(
    (
        (dy, dx, dz, dc)
        for dy in range(4)
        for dx in range(4)
        for dz in range(2)
        for dc in range(2)
        if dy or dx or dz or dc
    ),
    key=lambda d: -(min(d[0], 4 - d[0]) + min(d[1], 4 - d[1]) + d[2]) - 0.1 * d[3],
)

NEARNESS = ((2,), (1,), (3,), (0,))


def tables():
    j = np.arange(NX)
    angle = 2.0 * np.pi * ((j[:, None] * j[None, :]) % NX) / NX
    table_x = np.concatenate([np.cos(angle), np.sin(angle)], axis=1)
    b = np.arange(LANES)
    angle = 2.0 * np.pi * ((b[:, None] * b[None, :]) % LANES) / LANES
    c, s = np.cos(angle), np.sin(angle)
    forward = np.block([[c, -s], [s, c]])
    backward = np.block([[c, s], [-s, c]])
    k = np.arange(RADIX)
    angle = 2.0 * np.pi * (k[:, None] * b[None, :]) / NY
    twist = np.stack([np.cos(angle), np.sin(angle)])
    spread = (b[None, :] % 16 == b[:, None] // RADIX).astype(np.float32)
    return [np.asarray(t, np.float32) for t in (table_x, forward, backward, twist, spread)]


def sincos(x):
    n = jnp.floor(x * (2.0 / math.pi) + 0.5)
    r = x - n * 1.5703125
    r = r - n * 4.837512969970703125e-4
    r = r - n * 7.54978995489188216e-8
    z = r * r
    s = r + r * z * (-1.6666654611e-1 + z * (8.3321608736e-3 + z * -1.9515295891e-4))
    c = 1.0 - 0.5 * z + z * z * (
        4.166664568298827e-2 + z * (-1.388731625493765e-3 + z * 2.443315711809948e-5)
    )
    q = n.astype(jnp.int32)
    odd = (q & 1) == 1
    sin = jnp.where(odd, c, s)
    cos = jnp.where(odd, s, c)
    sin = jnp.where((q & 2) == 2, -sin, sin)
    cos = jnp.where(((q + 1) & 2) == 2, -cos, cos)
    return sin, cos


def dot(a, b):
    return lax.dot_general(
        a,
        b,
        (((1,), (0,)), ((), ())),
        precision=lax.Precision.HIGHEST,
        preferred_element_type=F32,
    )


def split(v, parts):
    out = []
    for _ in range(parts):
        out.append(v.astype(jnp.bfloat16))
        v = v - out[-1].astype(F32)
    return out


def dot_parts(a, b):
    total = None
    for order in range(len(a) - 1, -1, -1):
        for i in range(order + 1):
            term = lax.dot_general(
                a[i], b[order - i], (((1,), (0,)), ((), ())), preferred_element_type=F32
            )
            total = term if total is None else total + term
    return total


def cadd(a, b):
    return (a[0] + b[0], a[1] + b[1])


def csub(a, b):
    return (a[0] - b[0], a[1] - b[1])


def radix8(x, sign):
    def turn(v):
        return (-v[1], v[0]) if sign > 0 else (v[1], -v[0])

    def four(p, q, r, s):
        e0, e1, e2, e3 = cadd(p, r), csub(p, r), cadd(q, s), turn(csub(q, s))
        return cadd(e0, e2), cadd(e1, e3), csub(e0, e2), csub(e1, e3)

    e = four(x[0], x[2], x[4], x[6])
    o = four(x[1], x[3], x[5], x[7])
    t1, t3 = turn(o[1]), turn(o[3])
    w1 = ((o[1][0] + t1[0]) * ROOT_HALF, (o[1][1] + t1[1]) * ROOT_HALF)
    w3 = ((t3[0] - o[3][0]) * ROOT_HALF, (t3[1] - o[3][1]) * ROOT_HALF)
    o = (o[0], w1, turn(o[2]), w3)
    return [cadd(e[k], o[k]) for k in range(4)] + [csub(e[k], o[k]) for k in range(4)]


def roll(v, by, axis):
    return pltpu.roll(v, by % v.shape[axis], axis)


def transpose_lanes(blocks, width):
    blocks = list(blocks)
    group = lax.broadcasted_iota(jnp.int32, (8, LANES), 1) // width
    bit = len(blocks) // 2
    while bit:
        clear = lax.rem(group // bit, 2) == 0
        for u in range(len(blocks)):
            if u & bit == 0:
                p, q = blocks[u], blocks[u | bit]
                blocks[u] = jnp.where(clear, p, roll(q, bit * width, 1))
                blocks[u | bit] = jnp.where(clear, roll(p, -bit * width, 1), q)
        bit //= 2
    return blocks


def spread_lanes(v):
    group = lax.broadcasted_iota(jnp.int32, (8, LANES), 1) // 16
    out = [v]
    for bit in (4, 2, 1):
        clear = lax.rem(group // bit, 2) == 0
        nxt = []
        for x in out:
            nxt.append(jnp.where(clear, x, roll(x, 16 * bit, 1)))
            nxt.append(jnp.where(clear, roll(x, -16 * bit, 1), x))
        out = nxt
    return out


def rates(re, im, dens):
    intensity = re * re + im * im
    power = intensity * intensity
    power = power * power
    power = power * power
    rate = RATE_COEF * power
    lost = rate + RECOMB
    decays = jnp.exp(-lost)
    source = (1.0 - decays) * dens * (rate / lost)
    return intensity, decays, source


def kernel(
    field_hbm, dens_hbm, phx_hbm, phy_hbm, tx_hbm, wf_hbm, wb_hbm, tw_hbm, sp_hbm,
    out, ele,
    field, dens1, dens2, phx, phy, tx, wf, wb, tw, sp,
    stage, bmat, mmat, mmix, turns, densx, densy,
    mparts, xparts, wparts, send1, recv1, work, gain, phase0,
    send2, recv2, ent, send4, recv4, fold, dec, src, inten,
    sende, recve, send5, recv5, ent5, send6, recv6,
    in_sems, ready, team_send, team_recv, map_send, map_recv, own_send, own_recv,
):
    tm = lax.axis_index("tm")
    trans = lax.axis_index("trans")
    g = tm // GROUP
    s = lax.rem(tm, GROUP)
    me = GROUP * trans + s

    barrier = pltpu.get_barrier_semaphore()

    ys = [GROUP * lax.rem(trans // 4 + d, 4) for d in range(4)]
    xs = [lax.rem(trans + d, 4) for d in range(4)]
    zs = [2 * lax.rem(s // 2 + d, 2) for d in range(2)]
    cs = [lax.rem(s + d, 2) for d in range(2)]
    mates = []
    for dy, dx, dz, dc in FAR_FIRST:
        other, slot = ys[dy] + xs[dx], zs[dz] + cs[dc]
        mates.append(((GROUP * g + slot, other), GROUP * other + slot))

    row0 = pl.multiple_of(trans * N, N)
    col0 = pl.multiple_of((me // 8) * LANES, LANES)
    loads = [
        pltpu.make_async_copy(a, b, in_sems.at[i])
        for i, (a, b) in enumerate(
            [
                (field_hbm, field),
                (tw_hbm, tw),
                (wf_hbm, wf),
                (phy_hbm, phy),
                (sp_hbm, sp),
                (wb_hbm, wb),
                (phx_hbm, phx),
                (tx_hbm, tx),
                (dens_hbm.at[:, pl.ds(col0, LANES)], dens1),
                (dens_hbm.at[pl.ds(row0, N), :], dens2),
            ]
        )
    ]
    for load in loads[:3]:
        load.start()
    for where_to, _ in mates:
        pl.semaphore_signal(barrier, inc=1, device_id=where_to, device_id_type=MESH)
    for load in loads[3:]:
        load.start()
    for later in range(1, GROUP):

        @pl.when(g + later < GROUP)
        def _():
            pl.semaphore_signal(
                barrier, inc=1, device_id=(tm + GROUP * later, trans), device_id_type=MESH
            )

    def exchange(src_ref, dst_ref, phase, near):
        for offsets, (where_to, slot) in zip(FAR_FIRST, mates):
            if offsets[0] not in near:
                continue
            pltpu.make_async_remote_copy(
                src_ref=src_ref.at[slot],
                dst_ref=dst_ref.at[me],
                send_sem=team_send.at[phase],
                recv_sem=team_recv.at[phase],
                device_id=where_to,
                device_id_type=MESH,
            ).start()

    def whole(ref, sem, count):
        part = ref.at[pl.ds(0, count)]
        pltpu.make_async_copy(part, part, sem).wait()

    def send_map(src_ref, dst_ref, phase, chunk):
        for later in range(1, GROUP):

            @pl.when(g + later < GROUP)
            def _():
                pltpu.make_async_remote_copy(
                    src_ref=src_ref.at[chunk],
                    dst_ref=dst_ref.at[g, chunk],
                    send_sem=map_send.at[phase],
                    recv_sem=map_recv.at[phase, g],
                    device_id=(tm + GROUP * later, trans),
                    device_id_type=MESH,
                ).start()

    def enter(dst_ref, phase, total):
        total[...] = jnp.zeros_like(total)
        for k in range(GROUP - 1):

            @pl.when(k < g)
            def _():
                pltpu.make_async_copy(dst_ref.at[k], dst_ref.at[k], map_recv.at[phase, k]).wait()
                for chunk in range(4):
                    total[chunk] = dst_ref[k, chunk, 0] * total[chunk] + dst_ref[k, chunk, 1]

    def send_own(src_ref, dst_ref, phase, i):
        @pl.when(i != s)
        def _():
            pltpu.make_async_remote_copy(
                src_ref=src_ref.at[i],
                dst_ref=dst_ref.at[s],
                send_sem=own_send.at[phase],
                recv_sem=own_recv.at[phase, s],
                device_id=(GROUP * g + i, trans),
                device_id_type=MESH,
            ).start()

    lane = lax.broadcasted_iota(jnp.int32, (8, LANES), 1)
    sub = lax.broadcasted_iota(jnp.int32, (8, LANES), 0)
    group = lane // 16
    top = sub < 4

    def flip(v):
        return roll(v, 4, 0)

    def spectral(ahead, behind):
        freq = ahead(stage[...])
        for k in range(RADIX):
            rows = slice(32 * k, 32 * k + 32)
            re, im = freq[rows, :LANES], freq[rows, LANES:]
            pr, pi = turns[1, k : k + 1, :], turns[0, k : k + 1, :]
            stage[rows, :LANES] = re * pr - im * pi
            stage[rows, LANES:] = re * pi + im * pr
        stage[...] = behind(stage[...])

    def forward(blocks, w):
        for k, (re, im) in enumerate(radix8(blocks, -1)):
            rows = slice(32 * k + 8 * w, 32 * k + 8 * w + 8)
            c, d = tw[0, k : k + 1, :], tw[1, k : k + 1, :]
            stage[rows, :LANES] = re * c + im * d
            stage[rows, LANES:] = im * c - re * d

    def back(w):
        parts = []
        for k in range(RADIX):
            rows = slice(32 * k + 8 * w, 32 * k + 8 * w + 8)
            re, im = stage[rows, :LANES], stage[rows, LANES:]
            c, d = tw[0, k : k + 1, :], tw[1, k : k + 1, :]
            parts.append((re * c - im * d, im * c + re * d))
        return radix8(parts, 1)

    loads[0].wait()
    loads[1].wait()
    for xh in range(2):
        for t in range(2):
            forward(
                [
                    tuple(field[c, pl.ds(128 * xh + 2 * a + t, 8, stride=16), :] for c in range(2))
                    for a in range(RADIX)
                ],
                2 * xh + t,
            )
    for load in loads[2:6]:
        load.wait()
    picked = jnp.concatenate(
        [jnp.where(lane % RADIX == sub, phy[r : r + 1, :], 0.0) for r in range(RADIX)], axis=0
    )
    picked = dot(picked, sp[...])
    phase = jnp.zeros((8, LANES), F32)
    for r in range(RADIX):
        phase = jnp.where(group == r, picked[8 * r : 8 * r + 8, :], phase)
    sin, cos = sincos(phase)
    turns[0] = sin * (1.0 / NY)
    turns[1] = cos * (1.0 / NY)
    spectral(lambda v: dot(v, wf[...]), lambda v: dot(v, wb[...]))
    parts = [back(w) for w in range(4)]
    for a in range(RADIX):
        mixed = transpose_lanes(
            [parts[2 * xh + t][a][c] for xh in range(2) for c in range(2) for t in range(2)], 16
        )
        for j in range(8):
            send1[8 * a + j] = mixed[j]

    pl.semaphore_wait(barrier, TEAM - 1 + g)
    exchange(send1, recv1, 0, range(4))
    recv1[me] = send1[me]
    for k in range(GROUP - 1):

        @pl.when(k < g)
        def _():
            pl.semaphore_signal(
                ready, inc=1, device_id=(GROUP * k + s, trans), device_id_type=MESH
            )

    for load in loads[6:]:
        load.wait()
    sin, cos = sincos(phx[...])
    sin, cos = sin * (1.0 / NX), cos * (1.0 / NX)
    cx, sx = tx[:, :NX], tx[:, NX:]
    bmat[:NX, :] = cx * cos - sx * sin
    bmat[NX:, :] = cx * sin + sx * cos
    both = dot(bmat[...], tx[...])
    mmat[:NX, :] = both[:NX, :NX] + both[NX:, NX:]
    mmat[NX:, :] = both[NX:, :NX] - both[:NX, NX:]
    for m in range(NX // 8):
        for half in range(2):
            cols = slice(LANES * half, LANES * (half + 1))
            re, im = mmat[8 * m : 8 * m + 8, cols], mmat[NX + 8 * m : NX + 8 * m + 8, cols]
            mmix[16 * m : 16 * m + 8, cols] = jnp.where(top, re, flip(im))
            mmix[16 * m + 8 : 16 * m + 16, cols] = jnp.where(top, flip(re), im)
    for target, parts in (
        (mparts, split(mmat[...], 3)),
        (xparts, split(mmix[...], 2)),
        (wparts.at[0], split(wf[...], 2)),
        (wparts.at[1], split(wb[...], 2)),
    ):
        for i, part in enumerate(parts):
            target[i] = part
    mine = group == lax.rem(me, 8)
    for m in range(NX // 8):
        rows = slice(8 * m, 8 * m + 8)
        v = jnp.where(mine, dens1[rows, :], 0.0)
        for shift in (16, 32, 64):
            v = v + roll(v, shift, 1)
        densx[rows, :] = v
    for r in range(4):
        line = dens2[pl.ds(4 * s + r, 1), :]
        densy[r : r + 1, :] = line
        densy[r + 4 : r + 5, :] = line

    whole(recv1, team_recv.at[0], TEAM - 1)
    for p in range(N):
        mixed = transpose_lanes([recv1[4 * p + k] for k in range(4)], 32)
        for xh in range(2):
            for c in range(2):
                work[c, 16 * p + 8 * xh : 16 * p + 8 * xh + 8, :] = mixed[2 * xh + c]
    both = dot_parts(
        [mparts[i] for i in range(3)], split(jnp.concatenate([work[0], work[1]], axis=1), 3)
    )
    work[0] = both[:NX, :LANES] - both[NX:, LANES:]
    work[1] = both[NX:, :LANES] + both[:NX, LANES:]

    @pl.when(g < GROUP - 1)
    def _():
        pl.semaphore_wait(ready, GROUP - 1 - g)

    for chunk in range(4):
        maps = [jnp.zeros((8, LANES), F32)] * 2
        for i in range(8):
            rows = slice(64 * chunk + 8 * i, 64 * chunk + 8 * i + 8)
            intensity, grow, add = rates(work[0, rows, :], work[1, rows, :], densx[rows, :])
            for bit in (1, 2, 4):
                there = group >= bit
                grow2, add2 = roll(grow, 16 * bit, 1), roll(add, 16 * bit, 1)
                add = jnp.where(there, grow * add2 + add, add)
                grow = jnp.where(there, grow * grow2, grow)
            phase0[rows, :] = KERR_COEF * intensity - PLASMA * add
            gain[rows, :] = PLASMA * grow
            maps = [
                jnp.where(group == i, roll(v, 16 * (i + 1), 1), old)
                for v, old in zip((grow, add), maps)
            ]
        send2[chunk, 0] = maps[0]
        send2[chunk, 1] = maps[1]
        send_map(send2, recv2, 0, chunk)
    enter(recv2, 0, ent)
    for chunk in range(4):
        for i, entering in enumerate(spread_lanes(ent[chunk])):
            rows = slice(64 * chunk + 8 * i, 64 * chunk + 8 * i + 8)
            sin, cos = sincos(phase0[rows, :] - gain[rows, :] * entering)
            re, im = work[0, rows, :], work[1, rows, :]
            work[0, rows, :] = re * cos - im * sin
            work[1, rows, :] = re * sin + im * cos

    fields = split(jnp.concatenate([work[0], work[1]], axis=1), 2)
    for near in NEARNESS:
        both = dot_parts(
            [
                jnp.concatenate(
                    [
                        xparts[i, pl.ds(pl.multiple_of(32 * ys[dy], 128), 128), :]
                        for dy in near
                    ],
                    axis=0,
                )
                for i in range(2)
            ],
            fields,
        )
        for n, dy in enumerate(near):
            for k in range(16):
                rows = slice(128 * n + 8 * k, 128 * n + 8 * k + 8)
                turned = flip(both[rows, LANES:])
                send4[GROUP * ys[dy] + k] = both[rows, :LANES] + jnp.where(top, -turned, turned)
        exchange(send4, recv4, 1, near)
    recv4[me] = send4[me]
    whole(recv4, team_recv.at[1], TEAM - 1)

    for a in range(RADIX):
        times = transpose_lanes([recv4[8 * a + j] for j in range(8)], 16)
        for i in range(4):
            u, v = times[2 * i], times[2 * i + 1]
            fold[i, a, 0] = jnp.where(top, u, flip(v))
            fold[i, a, 1] = jnp.where(top, flip(u), v)
    for i in range(4):
        forward([(fold[i, a, 0], fold[i, a, 1]) for a in range(RADIX)], i)
    spectral(
        *(lambda v, i=i: dot_parts(split(v, 2), [wparts[i, 0], wparts[i, 1]]) for i in range(2))
    )
    maps = [None] * 4
    for i in range(4):
        fields = back(i)
        pairs = []
        for a in range(RADIX):
            re, im = fields[a]
            sende[i, a, 0] = re
            sende[i, a, 1] = im
            _, decays, source = rates(re, im, densy[:, LANES * a : LANES * (a + 1)])
            dec[i, a] = decays
            src[i, a] = source
            pairs.append((decays * flip(decays), decays * flip(source) + source))
        for h in range(4):
            even, odd = pairs[2 * h], pairs[2 * h + 1]
            grow = jnp.where(top, even[0], odd[0])
            add = jnp.where(top, flip(even[1]), odd[1])
            if maps[h] is not None:
                grow, add = grow * maps[h][0], grow * maps[h][1] + add
            maps[h] = (grow, add)
    for h in range(4):
        send5[h, 0] = maps[h][0]
        send5[h, 1] = maps[h][1]
        send_map(send5, recv5, 1, h)
    for i in range(GROUP):
        send_own(sende, recve, 0, i)
    recve[s] = sende[s]

    enter(recv5, 1, ent5)
    current = []
    for h in range(4):
        v = ent5[h]
        turned = flip(v)
        current += [jnp.where(top, v, turned), jnp.where(top, turned, v)]
    for i in range(4):
        for a in range(RADIX):
            decays, source = dec[i, a], src[i, a]
            first = decays * current[a] + source
            electrons = decays * jnp.where(top, current[a], flip(first)) + source
            send6[i, a] = electrons
            current[a] = jnp.where(top, flip(electrons), electrons)
        send_own(send6, recv6, 1, i)
    recv6[s] = send6[s]

    for k in range(GROUP):

        @pl.when(k != s)
        def _():
            pltpu.make_async_copy(recve.at[k], recve.at[k], own_recv.at[0, k]).wait()
            pltpu.make_async_copy(recv6.at[k], recv6.at[k], own_recv.at[1, k]).wait()

        for a in range(RADIX):
            re, im, electrons = recve[k, a, 0], recve[k, a, 1], recv6[k, a]
            intensity = re * re + im * im
            sin, cos = sincos(KERR_COEF * intensity - PLASMA * electrons)
            new_re, new_im = re * cos - im * sin, re * sin + im * cos
            for t in range(2):
                rows = pl.ds(64 * k + 2 * a + t, 4, stride=16)
                part = slice(4 * t, 4 * t + 4)
                out[0, rows, :] = new_re[part]
                out[1, rows, :] = new_im[part]
                ele[rows, :] = electrons[part]

    whole(send1, team_send.at[0], TEAM - 1)
    whole(send4, team_send.at[1], TEAM - 1)
    whole(sende, own_send.at[0], GROUP - 1)
    whole(send6, own_send.at[1], GROUP - 1)
    for later in range(1, GROUP):

        @pl.when(g + later < GROUP)
        def _():
            for phase_index, ref in enumerate((send2, send5)):
                whole(ref, map_send.at[phase_index], 4)


def finish(a, b, c, d, sems):
    copies = [
        pltpu.make_async_copy(x, y, sems.at[i]) for i, (x, y) in enumerate([(a, c), (b, d)])
    ]
    for copy in copies:
        copy.start()
    for copy in copies:
        copy.wait()


def local(light_field, gas_density, phase_x, phase_y):
    consts = tables()
    rows = light_field.reshape(2, 16, 2, RADIX, LANES).transpose(0, 1, 3, 2, 4).reshape(2, NX, LANES)
    vmem = lambda *shape: pltpu.VMEM(shape, F32)
    team = vmem(TEAM, 8, LANES)
    chunks = vmem(4, 2, 8, LANES)
    incoming = vmem(GROUP - 1, 4, 2, 8, LANES)
    tall = vmem(4, RADIX, 8, LANES)
    fields = vmem(4, RADIX, 2, 8, LANES)
    plane = vmem(NX, LANES)
    out, ele = pl.pallas_call(
        kernel,
        out_shape=(
            jax.ShapeDtypeStruct((2, NX, LANES), F32),
            jax.ShapeDtypeStruct((NX, LANES), F32),
        ),
        in_specs=[pl.BlockSpec(memory_space=pltpu.HBM)] * 9,
        out_specs=(pl.BlockSpec(memory_space=pltpu.VMEM),) * 2,
        scratch_shapes=[
            vmem(2, NX, LANES), plane, vmem(16, NY), vmem(1, NX), vmem(8, LANES),
            vmem(NX, 2 * NX), vmem(NX, NX), vmem(NX, NX), vmem(2, 8, LANES), vmem(LANES, LANES),
            vmem(NX, NX), vmem(2 * NX, NX), vmem(2 * NX, NX), vmem(2 * NX, NX),
            vmem(2, 8, LANES), plane, vmem(8, NY),
            pltpu.VMEM((3, 2 * NX, NX), jnp.bfloat16),
            pltpu.VMEM((2, 2 * NX, NX), jnp.bfloat16),
            pltpu.VMEM((2, 2, NX, NX), jnp.bfloat16),
            team, team, vmem(2, NX, LANES), plane, plane,
            chunks, incoming, vmem(4, 8, LANES), team, team, fields, tall, tall, tall,
            fields, fields, chunks, incoming, vmem(4, 8, LANES), tall, tall,
            pltpu.SemaphoreType.DMA((10,)),
            pltpu.SemaphoreType.REGULAR,
            pltpu.SemaphoreType.DMA((2,)),
            pltpu.SemaphoreType.DMA((2,)),
            pltpu.SemaphoreType.DMA((2,)),
            pltpu.SemaphoreType.DMA((2, GROUP - 1)),
            pltpu.SemaphoreType.DMA((2,)),
            pltpu.SemaphoreType.DMA((2, GROUP)),
        ],
        compiler_params=pltpu.CompilerParams(
            collective_id=0, has_side_effects=True, vmem_limit_bytes=24 * 1024 * 1024
        ),
        name="split_step",
    )(
        *(
            pltpu.with_memory_space_constraint(array, pltpu.HBM)
            for array in (
                rows, gas_density, phase_x.reshape(1, NX), phase_y.reshape(RADIX, LANES), *consts
            )
        )
    )
    out, ele = pl.pallas_call(
        finish,
        out_shape=(
            jax.ShapeDtypeStruct((2, NX, LANES), F32),
            jax.ShapeDtypeStruct((NX, LANES), F32),
        ),
        in_specs=[pl.BlockSpec(memory_space=pltpu.VMEM)] * 2,
        out_specs=(pl.BlockSpec(memory_space=pltpu.HBM),) * 2,
        scratch_shapes=[pltpu.SemaphoreType.DMA((2,))],
        compiler_params=pltpu.CompilerParams(vmem_limit_bytes=1024 * 1024),
        name="finish",
    )(out, ele)
    out = out.reshape(2, 16, RADIX, 2, LANES).transpose(0, 1, 3, 2, 4).reshape(2, 16, 2, NY)
    ele = ele.reshape(16, RADIX, 2, LANES).transpose(0, 2, 1, 3).reshape(16, 2, NY)
    return out, ele


def solution(mesh):
    placed = (P(None, "trans", "tm", None), P(), P(), P())
    return jax.shard_map(
        local,
        mesh=mesh,
        in_specs=placed,
        out_specs=(P(None, "trans", "tm", None), P("trans", "tm", None)),
        check_vma=False,
    )
```

```python
import functools
import math

import jax
import jax.numpy as jnp
import numpy as np
from jax import lax
from jax.experimental import pallas as pl
from jax.experimental.pallas import tpu as pltpu
from jax.sharding import PartitionSpec as P

RATE_COEF = 1.8e-08
RECOMB = 0.02
KERR_COEF = 0.3
PLASMA = 4.0

N = 16
LANES = 128
GROUP = 4
TEAM = N * GROUP
NX = 256
NY = 1024
RADIX = 8

F32 = jnp.float32
MESH = pl.DeviceIdType.MESH
ROOT_HALF = math.sqrt(0.5)


FAR_FIRST = sorted(
    (
        (dy, dx, dz, dc)
        for dy in range(4)
        for dx in range(4)
        for dz in range(2)
        for dc in range(2)
        if dy or dx or dz or dc
    ),
    key=lambda d: -(min(d[0], 4 - d[0]) + min(d[1], 4 - d[1]) + d[2]) - 0.1 * d[3],
)

NEARNESS = ((2,), (1,), (3,), (0,))


def tables():
    j = np.arange(NX)
    angle = 2.0 * np.pi * ((j[:, None] * j[None, :]) % NX) / NX
    table_x = np.concatenate([np.cos(angle), np.sin(angle)], axis=1)
    b = np.arange(LANES)
    angle = 2.0 * np.pi * ((b[:, None] * b[None, :]) % LANES) / LANES
    c, s = np.cos(angle), np.sin(angle)
    forward = np.block([[c, -s], [s, c]])
    backward = np.block([[c, s], [-s, c]])
    k = np.arange(RADIX)
    angle = 2.0 * np.pi * (k[:, None] * b[None, :]) / NY
    twist = np.stack([np.cos(angle), np.sin(angle)])
    spread = (b[None, :] % 16 == b[:, None] // RADIX).astype(np.float32)
    return [np.asarray(t, np.float32) for t in (table_x, forward, backward, twist, spread)]


def sincos(x):
    n = jnp.floor(x * (2.0 / math.pi) + 0.5)
    r = x - n * 1.5703125
    r = r - n * 4.837512969970703125e-4
    r = r - n * 7.54978995489188216e-8
    z = r * r
    s = r + r * z * (-1.6666654611e-1 + z * (8.3321608736e-3 + z * -1.9515295891e-4))
    c = 1.0 - 0.5 * z + z * z * (
        4.166664568298827e-2 + z * (-1.388731625493765e-3 + z * 2.443315711809948e-5)
    )
    q = n.astype(jnp.int32)
    odd = (q & 1) == 1
    sin = jnp.where(odd, c, s)
    cos = jnp.where(odd, s, c)
    sin = jnp.where((q & 2) == 2, -sin, sin)
    cos = jnp.where(((q + 1) & 2) == 2, -cos, cos)
    return sin, cos


def dot(a, b):
    return lax.dot_general(
        a,
        b,
        (((1,), (0,)), ((), ())),
        precision=lax.Precision.HIGHEST,
        preferred_element_type=F32,
    )


def split(v, parts):
    out = []
    for _ in range(parts):
        out.append(v.astype(jnp.bfloat16))
        v = v - out[-1].astype(F32)
    return out


def dot_parts(a, b):
    total = None
    for order in range(len(a) - 1, -1, -1):
        for i in range(order + 1):
            term = lax.dot_general(
                a[i], b[order - i], (((1,), (0,)), ((), ())), preferred_element_type=F32
            )
            total = term if total is None else total + term
    return total


def cadd(a, b):
    return (a[0] + b[0], a[1] + b[1])


def csub(a, b):
    return (a[0] - b[0], a[1] - b[1])


def radix8(x, sign):
    def turn(v):
        return (-v[1], v[0]) if sign > 0 else (v[1], -v[0])

    def four(p, q, r, s):
        e0, e1, e2, e3 = cadd(p, r), csub(p, r), cadd(q, s), turn(csub(q, s))
        return cadd(e0, e2), cadd(e1, e3), csub(e0, e2), csub(e1, e3)

    e = four(x[0], x[2], x[4], x[6])
    o = four(x[1], x[3], x[5], x[7])
    t1, t3 = turn(o[1]), turn(o[3])
    w1 = ((o[1][0] + t1[0]) * ROOT_HALF, (o[1][1] + t1[1]) * ROOT_HALF)
    w3 = ((t3[0] - o[3][0]) * ROOT_HALF, (t3[1] - o[3][1]) * ROOT_HALF)
    o = (o[0], w1, turn(o[2]), w3)
    return [cadd(e[k], o[k]) for k in range(4)] + [csub(e[k], o[k]) for k in range(4)]


def roll(v, by, axis):
    return pltpu.roll(v, by % v.shape[axis], axis)


def transpose_lanes(blocks, width):
    blocks = list(blocks)
    group = lax.broadcasted_iota(jnp.int32, (8, LANES), 1) // width
    bit = len(blocks) // 2
    while bit:
        clear = lax.rem(group // bit, 2) == 0
        for u in range(len(blocks)):
            if u & bit == 0:
                p, q = blocks[u], blocks[u | bit]
                blocks[u] = jnp.where(clear, p, roll(q, bit * width, 1))
                blocks[u | bit] = jnp.where(clear, roll(p, -bit * width, 1), q)
        bit //= 2
    return blocks


def spread_lanes(v):
    group = lax.broadcasted_iota(jnp.int32, (8, LANES), 1) // 16
    out = [v]
    for bit in (4, 2, 1):
        clear = lax.rem(group // bit, 2) == 0
        nxt = []
        for x in out:
            nxt.append(jnp.where(clear, x, roll(x, 16 * bit, 1)))
            nxt.append(jnp.where(clear, roll(x, -16 * bit, 1), x))
        out = nxt
    return out


def rates(re, im, dens):
    intensity = re * re + im * im
    power = intensity * intensity
    power = power * power
    power = power * power
    rate = RATE_COEF * power
    lost = rate + RECOMB
    decays = jnp.exp(-lost)
    source = (1.0 - decays) * dens * (rate / lost)
    return intensity, decays, source


def kernel(
    field_hbm, dens_hbm, phx_hbm, phy_hbm, tx_hbm, wf_hbm, wb_hbm, tw_hbm, sp_hbm,
    out, ele,
    field, dens1, dens2, phx, phy, tx, wf, wb, tw, sp,
    stage, bmat, mmat, mmix, turns, densx, densy,
    mparts, xparts, wparts, send1, recv1, work, gain, phase0,
    send2, recv2, ent, send4, recv4, fold, dec, src, inten,
    sende, recve, send5, recv5, ent5, send6, recv6, pairmap,
    in_sems, ready, team_send, team_recv, map_send, map_recv, own_send, own_recv,
):
    tm = lax.axis_index("tm")
    trans = lax.axis_index("trans")
    g = tm // GROUP
    s = lax.rem(tm, GROUP)
    me = GROUP * trans + s

    barrier = pltpu.get_barrier_semaphore()

    ys = [GROUP * lax.rem(trans // 4 + d, 4) for d in range(4)]
    xs = [lax.rem(trans + d, 4) for d in range(4)]
    zs = [2 * lax.rem(s // 2 + d, 2) for d in range(2)]
    cs = [lax.rem(s + d, 2) for d in range(2)]
    mates = []
    for dy, dx, dz, dc in FAR_FIRST:
        other, slot = ys[dy] + xs[dx], zs[dz] + cs[dc]
        mates.append(((GROUP * g + slot, other), GROUP * other + slot))

    row0 = pl.multiple_of(trans * N, N)
    col0 = pl.multiple_of((me // 8) * LANES, LANES)
    loads = [
        pltpu.make_async_copy(a, b, in_sems.at[i])
        for i, (a, b) in enumerate(
            [
                (field_hbm, field),
                (tw_hbm, tw),
                (wf_hbm, wf),
                (phy_hbm, phy),
                (sp_hbm, sp),
                (wb_hbm, wb),
                (phx_hbm, phx),
                (tx_hbm, tx),
                (dens_hbm.at[:, pl.ds(col0, LANES)], dens1),
                (dens_hbm.at[pl.ds(row0, N), :], dens2),
            ]
        )
    ]
    for load in loads[:3]:
        load.start()
    for where_to, _ in mates:
        pl.semaphore_signal(barrier, inc=1, device_id=where_to, device_id_type=MESH)
    for load in loads[3:]:
        load.start()
    for later in range(1, GROUP):

        @pl.when(g + later < GROUP)
        def _():
            pl.semaphore_signal(
                barrier, inc=1, device_id=(tm + GROUP * later, trans), device_id_type=MESH
            )

    def exchange(src_ref, dst_ref, phase, near):
        for offsets, (where_to, slot) in zip(FAR_FIRST, mates):
            if offsets[0] not in near:
                continue
            pltpu.make_async_remote_copy(
                src_ref=src_ref.at[slot],
                dst_ref=dst_ref.at[me],
                send_sem=team_send.at[phase],
                recv_sem=team_recv.at[phase],
                device_id=where_to,
                device_id_type=MESH,
            ).start()

    def whole(ref, sem, count):
        part = ref.at[pl.ds(0, count)]
        pltpu.make_async_copy(part, part, sem).wait()

    def send_map(src_ref, dst_ref, phase, chunk):
        for later in range(1, GROUP):

            @pl.when(g + later < GROUP)
            def _():
                pltpu.make_async_remote_copy(
                    src_ref=src_ref.at[chunk],
                    dst_ref=dst_ref.at[g, chunk],
                    send_sem=map_send.at[phase],
                    recv_sem=map_recv.at[phase, g],
                    device_id=(tm + GROUP * later, trans),
                    device_id_type=MESH,
                ).start()

    def enter(dst_ref, phase, total):
        total[...] = jnp.zeros_like(total)
        for k in range(GROUP - 1):

            @pl.when(k < g)
            def _():
                pltpu.make_async_copy(dst_ref.at[k], dst_ref.at[k], map_recv.at[phase, k]).wait()
                for chunk in range(4):
                    total[chunk] = dst_ref[k, chunk, 0] * total[chunk] + dst_ref[k, chunk, 1]

    def send_own(src_ref, dst_ref, phase, i):
        @pl.when(i != s)
        def _():
            pltpu.make_async_remote_copy(
                src_ref=src_ref.at[i],
                dst_ref=dst_ref.at[s],
                send_sem=own_send.at[phase],
                recv_sem=own_recv.at[phase, s],
                device_id=(GROUP * g + i, trans),
                device_id_type=MESH,
            ).start()

    lane = lax.broadcasted_iota(jnp.int32, (8, LANES), 1)
    sub = lax.broadcasted_iota(jnp.int32, (8, LANES), 0)
    group = lane // 16
    top = sub < 4

    def flip(v):
        return roll(v, 4, 0)

    def spectral(ahead, behind):
        freq = ahead(stage[...])
        for k in range(RADIX):
            rows = slice(32 * k, 32 * k + 32)
            re, im = freq[rows, :LANES], freq[rows, LANES:]
            pr, pi = turns[1, k : k + 1, :], turns[0, k : k + 1, :]
            stage[rows, :LANES] = re * pr - im * pi
            stage[rows, LANES:] = re * pi + im * pr
        stage[...] = behind(stage[...])

    def forward(blocks, w):
        for k, (re, im) in enumerate(radix8(blocks, -1)):
            rows = slice(32 * k + 8 * w, 32 * k + 8 * w + 8)
            c, d = tw[0, k : k + 1, :], tw[1, k : k + 1, :]
            stage[rows, :LANES] = re * c + im * d
            stage[rows, LANES:] = im * c - re * d

    def back(w):
        parts = []
        for k in range(RADIX):
            rows = slice(32 * k + 8 * w, 32 * k + 8 * w + 8)
            re, im = stage[rows, :LANES], stage[rows, LANES:]
            c, d = tw[0, k : k + 1, :], tw[1, k : k + 1, :]
            parts.append((re * c - im * d, im * c + re * d))
        return radix8(parts, 1)

    loads[0].wait()
    loads[1].wait()
    for xh in range(2):
        for t in range(2):
            forward(
                [
                    tuple(field[c, pl.ds(128 * xh + 2 * a + t, 8, stride=16), :] for c in range(2))
                    for a in range(RADIX)
                ],
                2 * xh + t,
            )
    for load in loads[2:6]:
        load.wait()
    picked = jnp.concatenate(
        [jnp.where(lane % RADIX == sub, phy[r : r + 1, :], 0.0) for r in range(RADIX)], axis=0
    )
    picked = dot(picked, sp[...])
    phase = jnp.zeros((8, LANES), F32)
    for r in range(RADIX):
        phase = jnp.where(group == r, picked[8 * r : 8 * r + 8, :], phase)
    sin, cos = sincos(phase)
    turns[0] = sin * (1.0 / NY)
    turns[1] = cos * (1.0 / NY)
    spectral(lambda v: dot(v, wf[...]), lambda v: dot(v, wb[...]))
    parts = [back(w) for w in range(4)]
    for a in range(RADIX):
        mixed = transpose_lanes(
            [parts[2 * xh + t][a][c] for xh in range(2) for c in range(2) for t in range(2)], 16
        )
        for j in range(8):
            send1[8 * a + j] = mixed[j]

    pl.semaphore_wait(barrier, TEAM - 1 + g)
    exchange(send1, recv1, 0, range(4))
    recv1[me] = send1[me]
    for k in range(GROUP - 1):

        @pl.when(k < g)
        def _():
            pl.semaphore_signal(
                ready, inc=1, device_id=(GROUP * k + s, trans), device_id_type=MESH
            )

    for load in loads[6:]:
        load.wait()
    sin, cos = sincos(phx[...])
    sin, cos = sin * (1.0 / NX), cos * (1.0 / NX)
    cx, sx = tx[:, :NX], tx[:, NX:]
    bmat[:NX, :] = cx * cos - sx * sin
    bmat[NX:, :] = cx * sin + sx * cos
    both = dot(bmat[...], tx[...])
    mmat[:NX, :] = both[:NX, :NX] + both[NX:, NX:]
    mmat[NX:, :] = both[NX:, :NX] - both[:NX, NX:]
    for m in range(NX // 8):
        for half in range(2):
            cols = slice(LANES * half, LANES * (half + 1))
            re, im = mmat[8 * m : 8 * m + 8, cols], mmat[NX + 8 * m : NX + 8 * m + 8, cols]
            mmix[16 * m : 16 * m + 8, cols] = jnp.where(top, re, flip(im))
            mmix[16 * m + 8 : 16 * m + 16, cols] = jnp.where(top, flip(re), im)
    for target, parts in (
        (mparts, split(mmat[...], 3)),
        (xparts, split(mmix[...], 2)),
        (wparts.at[0], split(wf[...], 2)),
        (wparts.at[1], split(wb[...], 2)),
    ):
        for i, part in enumerate(parts):
            target[i] = part
    mine = group == lax.rem(me, 8)
    for m in range(NX // 8):
        rows = slice(8 * m, 8 * m + 8)
        v = jnp.where(mine, dens1[rows, :], 0.0)
        for shift in (16, 32, 64):
            v = v + roll(v, shift, 1)
        densx[rows, :] = v
    for k in range(GROUP):
        for r in range(4):
            line = dens2[4 * k + r : 4 * k + r + 1, :]
            densy[k, r : r + 1, :] = line
            densy[k, r + 4 : r + 5, :] = line

    whole(recv1, team_recv.at[0], TEAM - 1)
    for p in range(N):
        mixed = transpose_lanes([recv1[4 * p + k] for k in range(4)], 32)
        for xh in range(2):
            for c in range(2):
                work[c, 16 * p + 8 * xh : 16 * p + 8 * xh + 8, :] = mixed[2 * xh + c]
    fields = split(jnp.concatenate([work[0], work[1]], axis=1), 3)

    def along_x(chunk):
        both = dot_parts(
            [
                jnp.concatenate(
                    [mparts[i, n + 64 * chunk : n + 64 * chunk + 64, :] for n in (0, NX)], axis=0
                )
                for i in range(3)
            ],
            fields,
        )
        return both[:64, :LANES] - both[64:, LANES:], both[64:, :LANES] + both[:64, LANES:]

    ahead = along_x(0)
    for chunk in range(4):
        maps = [jnp.zeros((8, LANES), F32)] * 2
        re, im = ahead
        if chunk < 3:
            ahead = along_x(chunk + 1)
        for i in range(8):
            part = slice(8 * i, 8 * i + 8)
            rows = slice(64 * chunk + 8 * i, 64 * chunk + 8 * i + 8)
            work[0, rows, :] = re[part]
            work[1, rows, :] = im[part]
            intensity, grow, add = rates(re[part], im[part], densx[rows, :])
            for bit in (1, 2, 4):
                there = group >= bit
                grow2, add2 = roll(grow, 16 * bit, 1), roll(add, 16 * bit, 1)
                add = jnp.where(there, grow * add2 + add, add)
                grow = jnp.where(there, grow * grow2, grow)
            phase0[rows, :] = KERR_COEF * intensity - PLASMA * add
            gain[rows, :] = PLASMA * grow
            maps = [
                jnp.where(group == i, roll(v, 16 * (i + 1), 1), old)
                for v, old in zip((grow, add), maps)
            ]
        if chunk == 0:

            @pl.when(g < GROUP - 1)
            def _():
                pl.semaphore_wait(ready, GROUP - 1 - g)

        send2[chunk, 0] = maps[0]
        send2[chunk, 1] = maps[1]
        send_map(send2, recv2, 0, chunk)
    enter(recv2, 0, ent)
    for chunk in range(4):
        for i, entering in enumerate(spread_lanes(ent[chunk])):
            rows = slice(64 * chunk + 8 * i, 64 * chunk + 8 * i + 8)
            sin, cos = sincos(phase0[rows, :] - gain[rows, :] * entering)
            re, im = work[0, rows, :], work[1, rows, :]
            work[0, rows, :] = re * cos - im * sin
            work[1, rows, :] = re * sin + im * cos

    fields = split(jnp.concatenate([work[0], work[1]], axis=1), 2)
    for near in NEARNESS:
        both = dot_parts(
            [
                jnp.concatenate(
                    [
                        xparts[i, pl.ds(pl.multiple_of(32 * ys[dy], 128), 128), :]
                        for dy in near
                    ],
                    axis=0,
                )
                for i in range(2)
            ],
            fields,
        )
        for n, dy in enumerate(near):
            for k in range(16):
                rows = slice(128 * n + 8 * k, 128 * n + 8 * k + 8)
                turned = flip(both[rows, LANES:])
                send4[GROUP * ys[dy] + k] = both[rows, :LANES] + jnp.where(top, -turned, turned)
        exchange(send4, recv4, 1, near)
    recv4[me] = send4[me]
    whole(recv4, team_recv.at[1], TEAM - 1)

    for a in range(RADIX):
        times = transpose_lanes([recv4[8 * a + j] for j in range(8)], 16)
        for i in range(4):
            u, v = times[2 * i], times[2 * i + 1]
            fold[i, a, 0] = jnp.where(top, u, flip(v))
            fold[i, a, 1] = jnp.where(top, flip(u), v)
    for i in range(4):
        forward([(fold[i, a, 0], fold[i, a, 1]) for a in range(RADIX)], i)
    spectral(
        *(lambda v, i=i: dot_parts(split(v, 2), [wparts[i, 0], wparts[i, 1]]) for i in range(2))
    )
    maps = [None] * 4
    for i in range(4):
        fields = back(i)
        pairs = []
        for a in range(RADIX):
            re, im = fields[a]
            sende[i, a, 0] = re
            sende[i, a, 1] = im
            _, decays, source = rates(re, im, densy[s, :, LANES * a : LANES * (a + 1)])
            pairs.append((decays * flip(decays), decays * flip(source) + source))
        for h in range(4):
            even, odd = pairs[2 * h], pairs[2 * h + 1]
            grow = jnp.where(top, even[0], odd[0])
            add = jnp.where(top, flip(even[1]), odd[1])
            pairmap[i, h, 0] = grow
            pairmap[i, h, 1] = add
            if maps[h] is not None:
                grow, add = grow * maps[h][0], grow * maps[h][1] + add
            maps[h] = (grow, add)
    for h in range(4):
        send5[h, 0] = maps[h][0]
        send5[h, 1] = maps[h][1]
        send_map(send5, recv5, 1, h)
    for i in range(GROUP):
        send_own(sende, recve, 0, i)
    recve[s] = sende[s]

    enter(recv5, 1, ent5)
    for i in range(GROUP):
        for h in range(4):
            if i == 0:
                send6[0, h] = ent5[h]
            else:
                send6[i, h] = pairmap[i - 1, h, 0] * send6[i - 1, h] + pairmap[i - 1, h, 1]
        send_own(send6, recv6, 1, i)
    recv6[s] = send6[s]

    for step in range(GROUP):
        k = lax.rem(s + step, GROUP)
        if step:
            pltpu.make_async_copy(recve.at[k], recve.at[k], own_recv.at[0, k]).wait()
        for a in range(RADIX):
            intensity, decays, source = rates(
                recve[k, a, 0], recve[k, a, 1], densy[k, :, LANES * a : LANES * (a + 1)]
            )
            inten[step, a] = KERR_COEF * intensity
            dec[step, a] = jnp.where(top, decays, decays * flip(decays))
            src[step, a] = jnp.where(top, source, decays * flip(source) + source)
    for step in range(GROUP):
        k = lax.rem(s + step, GROUP)
        if step:
            pltpu.make_async_copy(recv6.at[k], recv6.at[k], own_recv.at[1, k]).wait()
        for a in range(RADIX):
            packed = recv6[k, a // 2]
            turned = flip(packed)
            pair = (packed, turned) if a % 2 == 0 else (turned, packed)
            electrons = dec[step, a] * jnp.where(top, *pair) + src[step, a]
            sin, cos = sincos(inten[step, a] - PLASMA * electrons)
            re, im = recve[k, a, 0], recve[k, a, 1]
            new_re, new_im = re * cos - im * sin, re * sin + im * cos
            for t in range(2):
                rows = pl.ds(64 * k + 2 * a + t, 4, stride=16)
                part = slice(4 * t, 4 * t + 4)
                out[0, rows, :] = new_re[part]
                out[1, rows, :] = new_im[part]
                ele[rows, :] = electrons[part]

    whole(send1, team_send.at[0], TEAM - 1)
    whole(send4, team_send.at[1], TEAM - 1)
    whole(sende, own_send.at[0], GROUP - 1)
    whole(send6, own_send.at[1], GROUP - 1)
    for later in range(1, GROUP):

        @pl.when(g + later < GROUP)
        def _():
            for phase_index, ref in enumerate((send2, send5)):
                whole(ref, map_send.at[phase_index], 4)


def finish(a, b, c, d, sems):
    copies = [
        pltpu.make_async_copy(x, y, sems.at[i]) for i, (x, y) in enumerate([(a, c), (b, d)])
    ]
    for copy in copies:
        copy.start()
    for copy in copies:
        copy.wait()


def local(light_field, gas_density, phase_x, phase_y):
    consts = tables()
    rows = light_field.reshape(2, 16, 2, RADIX, LANES).transpose(0, 1, 3, 2, 4).reshape(2, NX, LANES)
    vmem = lambda *shape: pltpu.VMEM(shape, F32)
    team = vmem(TEAM, 8, LANES)
    chunks = vmem(4, 2, 8, LANES)
    incoming = vmem(GROUP - 1, 4, 2, 8, LANES)
    tall = vmem(4, RADIX, 8, LANES)
    short = vmem(4, 4, 8, LANES)
    fields = vmem(4, RADIX, 2, 8, LANES)
    plane = vmem(NX, LANES)
    out, ele = pl.pallas_call(
        kernel,
        out_shape=(
            jax.ShapeDtypeStruct((2, NX, LANES), F32),
            jax.ShapeDtypeStruct((NX, LANES), F32),
        ),
        in_specs=[pl.BlockSpec(memory_space=pltpu.HBM)] * 9,
        out_specs=(pl.BlockSpec(memory_space=pltpu.VMEM),) * 2,
        scratch_shapes=[
            vmem(2, NX, LANES), plane, vmem(16, NY), vmem(1, NX), vmem(8, LANES),
            vmem(NX, 2 * NX), vmem(NX, NX), vmem(NX, NX), vmem(2, 8, LANES), vmem(LANES, LANES),
            vmem(NX, NX), vmem(2 * NX, NX), vmem(2 * NX, NX), vmem(2 * NX, NX),
            vmem(2, 8, LANES), plane, vmem(GROUP, 8, NY),
            pltpu.VMEM((3, 2 * NX, NX), jnp.bfloat16),
            pltpu.VMEM((2, 2 * NX, NX), jnp.bfloat16),
            pltpu.VMEM((2, 2, NX, NX), jnp.bfloat16),
            team, team, vmem(2, NX, LANES), plane, plane,
            chunks, incoming, vmem(4, 8, LANES), team, team, fields, tall, tall, tall,
            fields, fields, chunks, incoming, vmem(4, 8, LANES), short, short,
            vmem(4, 4, 2, 8, LANES),
            pltpu.SemaphoreType.DMA((10,)),
            pltpu.SemaphoreType.REGULAR,
            pltpu.SemaphoreType.DMA((2,)),
            pltpu.SemaphoreType.DMA((2,)),
            pltpu.SemaphoreType.DMA((2,)),
            pltpu.SemaphoreType.DMA((2, GROUP - 1)),
            pltpu.SemaphoreType.DMA((2,)),
            pltpu.SemaphoreType.DMA((2, GROUP)),
        ],
        compiler_params=pltpu.CompilerParams(
            collective_id=0, has_side_effects=True, vmem_limit_bytes=24 * 1024 * 1024
        ),
        name="split_step",
    )(
        *(
            pltpu.with_memory_space_constraint(array, pltpu.HBM)
            for array in (
                rows, gas_density, phase_x.reshape(1, NX), phase_y.reshape(RADIX, LANES), *consts
            )
        )
    )
    out, ele = pl.pallas_call(
        finish,
        out_shape=(
            jax.ShapeDtypeStruct((2, NX, LANES), F32),
            jax.ShapeDtypeStruct((NX, LANES), F32),
        ),
        in_specs=[pl.BlockSpec(memory_space=pltpu.VMEM)] * 2,
        out_specs=(pl.BlockSpec(memory_space=pltpu.HBM),) * 2,
        scratch_shapes=[pltpu.SemaphoreType.DMA((2,))],
        compiler_params=pltpu.CompilerParams(vmem_limit_bytes=1024 * 1024),
        name="finish",
    )(out, ele)
    out = out.reshape(2, 16, RADIX, 2, LANES).transpose(0, 1, 3, 2, 4).reshape(2, 16, 2, NY)
    ele = ele.reshape(16, RADIX, 2, LANES).transpose(0, 2, 1, 3).reshape(16, 2, NY)
    return out, ele


def solution(mesh):
    placed = (P(None, "trans", "tm", None), P(), P(), P())
    return jax.shard_map(
        local,
        mesh=mesh,
        in_specs=placed,
        out_specs=(P(None, "trans", "tm", None), P("trans", "tm", None)),
        check_vma=False,
    )
```

```python
import functools
import math

import jax
import jax.numpy as jnp
import numpy as np
from jax import lax
from jax.experimental import pallas as pl
from jax.experimental.pallas import tpu as pltpu
from jax.sharding import PartitionSpec as P

RATE_COEF = 1.8e-08
RECOMB = 0.02
KERR_COEF = 0.3
PLASMA = 4.0

N = 16
LANES = 128
GROUP = 4
TEAM = N * GROUP
NX = 256
NY = 1024
RADIX = 8

F32 = jnp.float32
MESH = pl.DeviceIdType.MESH
ROOT_HALF = math.sqrt(0.5)


FAR_FIRST = sorted(
    (
        (dy, dx, dz, dc)
        for dy in range(4)
        for dx in range(4)
        for dz in range(2)
        for dc in range(2)
        if dy or dx or dz or dc
    ),
    key=lambda d: -(min(d[0], 4 - d[0]) + min(d[1], 4 - d[1]) + d[2]) - 0.1 * d[3],
)

NEARNESS = ((2,), (1,), (3,), (0,))


def tables():
    j = np.arange(NX)
    angle = 2.0 * np.pi * ((j[:, None] * j[None, :]) % NX) / NX
    table_x = np.concatenate([np.cos(angle), np.sin(angle)], axis=1)
    b = np.arange(LANES)
    angle = 2.0 * np.pi * ((b[:, None] * b[None, :]) % LANES) / LANES
    c, s = np.cos(angle), np.sin(angle)
    forward = np.block([[c, -s], [s, c]])
    backward = np.block([[c, s], [-s, c]])
    k = np.arange(RADIX)
    angle = 2.0 * np.pi * (k[:, None] * b[None, :]) / NY
    twist = np.stack([np.cos(angle), np.sin(angle)])
    spread = (b[None, :] % 16 == b[:, None] // RADIX).astype(np.float32)
    return [np.asarray(t, np.float32) for t in (table_x, forward, backward, twist, spread)]


def sincos(x):
    n = jnp.floor(x * (2.0 / math.pi) + 0.5)
    r = x - n * 1.5703125
    r = r - n * 4.837512969970703125e-4
    r = r - n * 7.54978995489188216e-8
    z = r * r
    s = r + r * z * (-1.6666654611e-1 + z * (8.3321608736e-3 + z * -1.9515295891e-4))
    c = 1.0 - 0.5 * z + z * z * (
        4.166664568298827e-2 + z * (-1.388731625493765e-3 + z * 2.443315711809948e-5)
    )
    q = n.astype(jnp.int32)
    odd = (q & 1) == 1
    sin = jnp.where(odd, c, s)
    cos = jnp.where(odd, s, c)
    sin = jnp.where((q & 2) == 2, -sin, sin)
    cos = jnp.where(((q + 1) & 2) == 2, -cos, cos)
    return sin, cos


def dot(a, b):
    return lax.dot_general(
        a,
        b,
        (((1,), (0,)), ((), ())),
        precision=lax.Precision.HIGHEST,
        preferred_element_type=F32,
    )


def split(v, parts):
    out = []
    for _ in range(parts):
        out.append(v.astype(jnp.bfloat16))
        v = v - out[-1].astype(F32)
    return out


def dot_parts(a, b):
    total = None
    for order in range(len(a) - 1, -1, -1):
        for i in range(order + 1):
            term = lax.dot_general(
                a[i], b[order - i], (((1,), (0,)), ((), ())), preferred_element_type=F32
            )
            total = term if total is None else total + term
    return total


def cadd(a, b):
    return (a[0] + b[0], a[1] + b[1])


def csub(a, b):
    return (a[0] - b[0], a[1] - b[1])


def radix8(x, sign):
    def turn(v):
        return (-v[1], v[0]) if sign > 0 else (v[1], -v[0])

    def four(p, q, r, s):
        e0, e1, e2, e3 = cadd(p, r), csub(p, r), cadd(q, s), turn(csub(q, s))
        return cadd(e0, e2), cadd(e1, e3), csub(e0, e2), csub(e1, e3)

    e = four(x[0], x[2], x[4], x[6])
    o = four(x[1], x[3], x[5], x[7])
    t1, t3 = turn(o[1]), turn(o[3])
    w1 = ((o[1][0] + t1[0]) * ROOT_HALF, (o[1][1] + t1[1]) * ROOT_HALF)
    w3 = ((t3[0] - o[3][0]) * ROOT_HALF, (t3[1] - o[3][1]) * ROOT_HALF)
    o = (o[0], w1, turn(o[2]), w3)
    return [cadd(e[k], o[k]) for k in range(4)] + [csub(e[k], o[k]) for k in range(4)]


def roll(v, by, axis):
    return pltpu.roll(v, by % v.shape[axis], axis)


def transpose_lanes(blocks, width):
    blocks = list(blocks)
    group = lax.broadcasted_iota(jnp.int32, (8, LANES), 1) // width
    bit = len(blocks) // 2
    while bit:
        clear = lax.rem(group // bit, 2) == 0
        for u in range(len(blocks)):
            if u & bit == 0:
                p, q = blocks[u], blocks[u | bit]
                blocks[u] = jnp.where(clear, p, roll(q, bit * width, 1))
                blocks[u | bit] = jnp.where(clear, roll(p, -bit * width, 1), q)
        bit //= 2
    return blocks


def spread_lanes(v):
    group = lax.broadcasted_iota(jnp.int32, (8, LANES), 1) // 16
    out = [v]
    for bit in (4, 2, 1):
        clear = lax.rem(group // bit, 2) == 0
        nxt = []
        for x in out:
            nxt.append(jnp.where(clear, x, roll(x, 16 * bit, 1)))
            nxt.append(jnp.where(clear, roll(x, -16 * bit, 1), x))
        out = nxt
    return out


def rates(re, im, dens):
    intensity = re * re + im * im
    power = intensity * intensity
    power = power * power
    power = power * power
    rate = RATE_COEF * power
    lost = rate + RECOMB
    decays = jnp.exp(-lost)
    source = (1.0 - decays) * dens * (rate / lost)
    return intensity, decays, source


def kernel(
    field_hbm, dens_hbm, phx_hbm, phy_hbm, tx_hbm, wf_hbm, wb_hbm, tw_hbm, sp_hbm,
    out, ele,
    field, dens1, dens2, phx, phy, tx, wf, wb, tw, sp,
    stage, bmat, mmat, mmix, turns, densx, densy,
    mparts, xparts, wparts, send1, recv1, work, gain, phase0,
    send2, recv2, ent, send4, recv4, fold, dec, src, inten,
    sende, recve, send5, recv5, ent5, send6, recv6, pairmap,
    in_sems, ready, team_send, team_recv, map_send, map_recv, own_send, own_recv,
):
    tm = lax.axis_index("tm")
    trans = lax.axis_index("trans")
    g = tm // GROUP
    s = lax.rem(tm, GROUP)
    me = GROUP * trans + s

    barrier = pltpu.get_barrier_semaphore()

    ys = [GROUP * lax.rem(trans // 4 + d, 4) for d in range(4)]
    xs = [lax.rem(trans + d, 4) for d in range(4)]
    zs = [2 * lax.rem(s // 2 + d, 2) for d in range(2)]
    cs = [lax.rem(s + d, 2) for d in range(2)]
    mates = []
    for dy, dx, dz, dc in FAR_FIRST:
        other, slot = ys[dy] + xs[dx], zs[dz] + cs[dc]
        mates.append(((GROUP * g + slot, other), GROUP * other + slot))

    row0 = pl.multiple_of(trans * N, N)
    col0 = pl.multiple_of((me // 8) * LANES, LANES)
    loads = [
        pltpu.make_async_copy(a, b, in_sems.at[i])
        for i, (a, b) in enumerate(
            [
                (field_hbm, field),
                (tw_hbm, tw),
                (wf_hbm, wf),
                (phy_hbm, phy),
                (sp_hbm, sp),
                (wb_hbm, wb),
                (phx_hbm, phx),
                (tx_hbm, tx),
                (dens_hbm.at[:, pl.ds(col0, LANES)], dens1),
                (dens_hbm.at[pl.ds(row0, N), :], dens2),
            ]
        )
    ]
    for load in loads[:3]:
        load.start()
    for where_to, _ in mates:
        pl.semaphore_signal(barrier, inc=1, device_id=where_to, device_id_type=MESH)
    for load in loads[3:]:
        load.start()
    for later in range(1, GROUP):

        @pl.when(g + later < GROUP)
        def _():
            pl.semaphore_signal(
                barrier, inc=1, device_id=(tm + GROUP * later, trans), device_id_type=MESH
            )

    def exchange(src_ref, dst_ref, phase, near):
        for offsets, (where_to, slot) in zip(FAR_FIRST, mates):
            if offsets[0] not in near:
                continue
            pltpu.make_async_remote_copy(
                src_ref=src_ref.at[slot],
                dst_ref=dst_ref.at[me],
                send_sem=team_send.at[phase],
                recv_sem=team_recv.at[phase],
                device_id=where_to,
                device_id_type=MESH,
            ).start()

    def whole(ref, sem, count):
        part = ref.at[pl.ds(0, count)]
        pltpu.make_async_copy(part, part, sem).wait()

    def send_map(src_ref, dst_ref, phase, chunk):
        for later in range(1, GROUP):

            @pl.when(g + later < GROUP)
            def _():
                pltpu.make_async_remote_copy(
                    src_ref=src_ref.at[chunk],
                    dst_ref=dst_ref.at[g, chunk],
                    send_sem=map_send.at[phase],
                    recv_sem=map_recv.at[phase, g],
                    device_id=(tm + GROUP * later, trans),
                    device_id_type=MESH,
                ).start()

    def enter(dst_ref, phase, total):
        total[...] = jnp.zeros_like(total)
        for k in range(GROUP - 1):

            @pl.when(k < g)
            def _():
                pltpu.make_async_copy(dst_ref.at[k], dst_ref.at[k], map_recv.at[phase, k]).wait()
                for chunk in range(4):
                    total[chunk] = dst_ref[k, chunk, 0] * total[chunk] + dst_ref[k, chunk, 1]

    def send_own(src_ref, dst_ref, phase):
        for dz, dc in ((1, 1), (1, 0), (0, 1)):
            i = zs[dz] + cs[dc]
            pltpu.make_async_remote_copy(
                src_ref=src_ref.at[i],
                dst_ref=dst_ref.at[s],
                send_sem=own_send.at[phase],
                recv_sem=own_recv.at[phase, s],
                device_id=(GROUP * g + i, trans),
                device_id_type=MESH,
            ).start()

    lane = lax.broadcasted_iota(jnp.int32, (8, LANES), 1)
    sub = lax.broadcasted_iota(jnp.int32, (8, LANES), 0)
    group = lane // 16
    top = sub < 4

    def flip(v):
        return roll(v, 4, 0)

    def spectral(ahead, behind):
        freq = ahead(stage[...])
        for k in range(RADIX):
            rows = slice(32 * k, 32 * k + 32)
            re, im = freq[rows, :LANES], freq[rows, LANES:]
            pr, pi = turns[1, k : k + 1, :], turns[0, k : k + 1, :]
            stage[rows, :LANES] = re * pr - im * pi
            stage[rows, LANES:] = re * pi + im * pr
        stage[...] = behind(stage[...])

    def forward(blocks, w):
        for k, (re, im) in enumerate(radix8(blocks, -1)):
            rows = slice(32 * k + 8 * w, 32 * k + 8 * w + 8)
            c, d = tw[0, k : k + 1, :], tw[1, k : k + 1, :]
            stage[rows, :LANES] = re * c + im * d
            stage[rows, LANES:] = im * c - re * d

    def back(w):
        parts = []
        for k in range(RADIX):
            rows = slice(32 * k + 8 * w, 32 * k + 8 * w + 8)
            re, im = stage[rows, :LANES], stage[rows, LANES:]
            c, d = tw[0, k : k + 1, :], tw[1, k : k + 1, :]
            parts.append((re * c - im * d, im * c + re * d))
        return radix8(parts, 1)

    loads[0].wait()
    loads[1].wait()
    for xh in range(2):
        for t in range(2):
            forward(
                [
                    tuple(field[c, pl.ds(128 * xh + 2 * a + t, 8, stride=16), :] for c in range(2))
                    for a in range(RADIX)
                ],
                2 * xh + t,
            )
    for load in loads[2:6]:
        load.wait()
    picked = jnp.concatenate(
        [jnp.where(lane % RADIX == sub, phy[r : r + 1, :], 0.0) for r in range(RADIX)], axis=0
    )
    picked = dot(picked, sp[...])
    phase = jnp.zeros((8, LANES), F32)
    for r in range(RADIX):
        phase = jnp.where(group == r, picked[8 * r : 8 * r + 8, :], phase)
    sin, cos = sincos(phase)
    turns[0] = sin * (1.0 / NY)
    turns[1] = cos * (1.0 / NY)
    spectral(lambda v: dot(v, wf[...]), lambda v: dot(v, wb[...]))
    parts = [back(w) for w in range(4)]
    for a in range(RADIX):
        mixed = transpose_lanes(
            [parts[2 * xh + t][a][c] for xh in range(2) for c in range(2) for t in range(2)], 16
        )
        for j in range(8):
            send1[8 * a + j] = mixed[j]

    pl.semaphore_wait(barrier, TEAM - 1 + g)
    exchange(send1, recv1, 0, range(4))
    recv1[me] = send1[me]
    for k in range(GROUP - 1):

        @pl.when(k < g)
        def _():
            pl.semaphore_signal(
                ready, inc=1, device_id=(GROUP * k + s, trans), device_id_type=MESH
            )

    for load in loads[6:]:
        load.wait()
    sin, cos = sincos(phx[...])
    sin, cos = sin * (1.0 / NX), cos * (1.0 / NX)
    cx, sx = tx[:, :NX], tx[:, NX:]
    bmat[:NX, :] = cx * cos - sx * sin
    bmat[NX:, :] = cx * sin + sx * cos
    both = dot(bmat[...], tx[...])
    mmat[:NX, :] = both[:NX, :NX] + both[NX:, NX:]
    mmat[NX:, :] = both[NX:, :NX] - both[:NX, NX:]
    for m in range(NX // 8):
        for half in range(2):
            cols = slice(LANES * half, LANES * (half + 1))
            re, im = mmat[8 * m : 8 * m + 8, cols], mmat[NX + 8 * m : NX + 8 * m + 8, cols]
            mmix[16 * m : 16 * m + 8, cols] = jnp.where(top, re, flip(im))
            mmix[16 * m + 8 : 16 * m + 16, cols] = jnp.where(top, flip(re), im)
    for target, parts in (
        (mparts, split(mmat[...], 3)),
        (xparts, split(mmix[...], 2)),
        (wparts.at[0], split(wf[...], 2)),
        (wparts.at[1], split(wb[...], 2)),
    ):
        for i, part in enumerate(parts):
            target[i] = part
    mine = group == lax.rem(me, 8)
    for m in range(NX // 8):
        rows = slice(8 * m, 8 * m + 8)
        v = jnp.where(mine, dens1[rows, :], 0.0)
        for shift in (16, 32, 64):
            v = v + roll(v, shift, 1)
        densx[rows, :] = v
    for k in range(GROUP):
        for r in range(4):
            line = dens2[4 * k + r : 4 * k + r + 1, :]
            densy[k, r : r + 1, :] = line
            densy[k, r + 4 : r + 5, :] = line

    whole(recv1, team_recv.at[0], TEAM - 1)
    for p in range(N):
        mixed = transpose_lanes([recv1[4 * p + k] for k in range(4)], 32)
        for xh in range(2):
            for c in range(2):
                work[c, 16 * p + 8 * xh : 16 * p + 8 * xh + 8, :] = mixed[2 * xh + c]
    fields = split(jnp.concatenate([work[0], work[1]], axis=1), 3)

    def along_x(chunk):
        both = dot_parts(
            [
                jnp.concatenate(
                    [mparts[i, n + 64 * chunk : n + 64 * chunk + 64, :] for n in (0, NX)], axis=0
                )
                for i in range(3)
            ],
            fields,
        )
        return both[:64, :LANES] - both[64:, LANES:], both[64:, :LANES] + both[:64, LANES:]

    ahead = along_x(0)
    for chunk in range(4):
        maps = [jnp.zeros((8, LANES), F32)] * 2
        re, im = ahead
        if chunk < 3:
            ahead = along_x(chunk + 1)
        for i in range(8):
            part = slice(8 * i, 8 * i + 8)
            rows = slice(64 * chunk + 8 * i, 64 * chunk + 8 * i + 8)
            work[0, rows, :] = re[part]
            work[1, rows, :] = im[part]
            intensity, grow, add = rates(re[part], im[part], densx[rows, :])
            for bit in (1, 2, 4):
                there = group >= bit
                grow2, add2 = roll(grow, 16 * bit, 1), roll(add, 16 * bit, 1)
                add = jnp.where(there, grow * add2 + add, add)
                grow = jnp.where(there, grow * grow2, grow)
            phase0[rows, :] = KERR_COEF * intensity - PLASMA * add
            gain[rows, :] = PLASMA * grow
            maps = [
                jnp.where(group == i, roll(v, 16 * (i + 1), 1), old)
                for v, old in zip((grow, add), maps)
            ]
        if chunk == 0:

            @pl.when(g < GROUP - 1)
            def _():
                pl.semaphore_wait(ready, GROUP - 1 - g)

        send2[chunk, 0] = maps[0]
        send2[chunk, 1] = maps[1]
        send_map(send2, recv2, 0, chunk)
    enter(recv2, 0, ent)
    for chunk in range(4):
        for i, entering in enumerate(spread_lanes(ent[chunk])):
            rows = slice(64 * chunk + 8 * i, 64 * chunk + 8 * i + 8)
            sin, cos = sincos(phase0[rows, :] - gain[rows, :] * entering)
            re, im = work[0, rows, :], work[1, rows, :]
            work[0, rows, :] = re * cos - im * sin
            work[1, rows, :] = re * sin + im * cos

    fields = split(jnp.concatenate([work[0], work[1]], axis=1), 2)
    for near in NEARNESS:
        both = dot_parts(
            [
                jnp.concatenate(
                    [
                        xparts[i, pl.ds(pl.multiple_of(32 * ys[dy], 128), 128), :]
                        for dy in near
                    ],
                    axis=0,
                )
                for i in range(2)
            ],
            fields,
        )
        for n, dy in enumerate(near):
            for k in range(16):
                rows = slice(128 * n + 8 * k, 128 * n + 8 * k + 8)
                turned = flip(both[rows, LANES:])
                send4[GROUP * ys[dy] + k] = both[rows, :LANES] + jnp.where(top, -turned, turned)
        exchange(send4, recv4, 1, near)
    recv4[me] = send4[me]
    whole(recv4, team_recv.at[1], TEAM - 1)

    for a in range(RADIX):
        times = transpose_lanes([recv4[8 * a + j] for j in range(8)], 16)
        for i in range(4):
            u, v = times[2 * i], times[2 * i + 1]
            fold[i, a, 0] = jnp.where(top, u, flip(v))
            fold[i, a, 1] = jnp.where(top, flip(u), v)
    for i in range(4):
        forward([(fold[i, a, 0], fold[i, a, 1]) for a in range(RADIX)], i)
    spectral(
        *(lambda v, i=i: dot_parts(split(v, 2), [wparts[i, 0], wparts[i, 1]]) for i in range(2))
    )
    maps = [None] * 4
    for i in range(4):
        fields = back(i)
        pairs = []
        for a in range(RADIX):
            re, im = fields[a]
            sende[i, a, 0] = re
            sende[i, a, 1] = im
            _, decays, source = rates(re, im, densy[s, :, LANES * a : LANES * (a + 1)])
            pairs.append((decays * flip(decays), decays * flip(source) + source))
        for h in range(4):
            even, odd = pairs[2 * h], pairs[2 * h + 1]
            grow = jnp.where(top, even[0], odd[0])
            add = jnp.where(top, flip(even[1]), odd[1])
            pairmap[i, h, 0] = grow
            pairmap[i, h, 1] = add
            if maps[h] is not None:
                grow, add = grow * maps[h][0], grow * maps[h][1] + add
            maps[h] = (grow, add)
    for h in range(4):
        send5[h, 0] = maps[h][0]
        send5[h, 1] = maps[h][1]
        send_map(send5, recv5, 1, h)
    send_own(sende, recve, 0)
    recve[s] = sende[s]

    enter(recv5, 1, ent5)
    for i in range(GROUP):
        for h in range(4):
            if i == 0:
                send6[0, h] = ent5[h]
            else:
                send6[i, h] = pairmap[i - 1, h, 0] * send6[i - 1, h] + pairmap[i - 1, h, 1]
    send_own(send6, recv6, 1)
    recv6[s] = send6[s]

    for step in range(GROUP):
        k = lax.rem(s + step, GROUP)
        if step:
            pltpu.make_async_copy(recve.at[k], recve.at[k], own_recv.at[0, k]).wait()
        for a in range(RADIX):
            intensity, decays, source = rates(
                recve[k, a, 0], recve[k, a, 1], densy[k, :, LANES * a : LANES * (a + 1)]
            )
            inten[step, a] = KERR_COEF * intensity
            dec[step, a] = jnp.where(top, decays, decays * flip(decays))
            src[step, a] = jnp.where(top, source, decays * flip(source) + source)
    for step in range(GROUP):
        k = lax.rem(s + step, GROUP)
        if step:
            pltpu.make_async_copy(recv6.at[k], recv6.at[k], own_recv.at[1, k]).wait()
        for a in range(RADIX):
            packed = recv6[k, a // 2]
            turned = flip(packed)
            pair = (packed, turned) if a % 2 == 0 else (turned, packed)
            electrons = dec[step, a] * jnp.where(top, *pair) + src[step, a]
            sin, cos = sincos(inten[step, a] - PLASMA * electrons)
            re, im = recve[k, a, 0], recve[k, a, 1]
            new_re, new_im = re * cos - im * sin, re * sin + im * cos
            for t in range(2):
                rows = pl.ds(64 * k + 2 * a + t, 4, stride=16)
                part = slice(4 * t, 4 * t + 4)
                out[0, rows, :] = new_re[part]
                out[1, rows, :] = new_im[part]
                ele[rows, :] = electrons[part]

    whole(send1, team_send.at[0], TEAM - 1)
    whole(send4, team_send.at[1], TEAM - 1)
    whole(sende, own_send.at[0], GROUP - 1)
    whole(send6, own_send.at[1], GROUP - 1)
    for later in range(1, GROUP):

        @pl.when(g + later < GROUP)
        def _():
            for phase_index, ref in enumerate((send2, send5)):
                whole(ref, map_send.at[phase_index], 4)


def finish(a, b, c, d, sems):
    copies = [
        pltpu.make_async_copy(x, y, sems.at[i]) for i, (x, y) in enumerate([(a, c), (b, d)])
    ]
    for copy in copies:
        copy.start()
    for copy in copies:
        copy.wait()


def local(light_field, gas_density, phase_x, phase_y):
    consts = tables()
    rows = light_field.reshape(2, 16, 2, RADIX, LANES).transpose(0, 1, 3, 2, 4).reshape(2, NX, LANES)
    vmem = lambda *shape: pltpu.VMEM(shape, F32)
    team = vmem(TEAM, 8, LANES)
    chunks = vmem(4, 2, 8, LANES)
    incoming = vmem(GROUP - 1, 4, 2, 8, LANES)
    tall = vmem(4, RADIX, 8, LANES)
    short = vmem(4, 4, 8, LANES)
    fields = vmem(4, RADIX, 2, 8, LANES)
    plane = vmem(NX, LANES)
    out, ele = pl.pallas_call(
        kernel,
        out_shape=(
            jax.ShapeDtypeStruct((2, NX, LANES), F32),
            jax.ShapeDtypeStruct((NX, LANES), F32),
        ),
        in_specs=[pl.BlockSpec(memory_space=pltpu.HBM)] * 9,
        out_specs=(pl.BlockSpec(memory_space=pltpu.VMEM),) * 2,
        scratch_shapes=[
            vmem(2, NX, LANES), plane, vmem(16, NY), vmem(1, NX), vmem(8, LANES),
            vmem(NX, 2 * NX), vmem(NX, NX), vmem(NX, NX), vmem(2, 8, LANES), vmem(LANES, LANES),
            vmem(NX, NX), vmem(2 * NX, NX), vmem(2 * NX, NX), vmem(2 * NX, NX),
            vmem(2, 8, LANES), plane, vmem(GROUP, 8, NY),
            pltpu.VMEM((3, 2 * NX, NX), jnp.bfloat16),
            pltpu.VMEM((2, 2 * NX, NX), jnp.bfloat16),
            pltpu.VMEM((2, 2, NX, NX), jnp.bfloat16),
            team, team, vmem(2, NX, LANES), plane, plane,
            chunks, incoming, vmem(4, 8, LANES), team, team, fields, tall, tall, tall,
            fields, fields, chunks, incoming, vmem(4, 8, LANES), short, short,
            vmem(4, 4, 2, 8, LANES),
            pltpu.SemaphoreType.DMA((10,)),
            pltpu.SemaphoreType.REGULAR,
            pltpu.SemaphoreType.DMA((2,)),
            pltpu.SemaphoreType.DMA((2,)),
            pltpu.SemaphoreType.DMA((2,)),
            pltpu.SemaphoreType.DMA((2, GROUP - 1)),
            pltpu.SemaphoreType.DMA((2,)),
            pltpu.SemaphoreType.DMA((2, GROUP)),
        ],
        compiler_params=pltpu.CompilerParams(
            collective_id=0, has_side_effects=True, vmem_limit_bytes=24 * 1024 * 1024
        ),
        name="split_step",
    )(
        *(
            pltpu.with_memory_space_constraint(array, pltpu.HBM)
            for array in (
                rows, gas_density, phase_x.reshape(1, NX), phase_y.reshape(RADIX, LANES), *consts
            )
        )
    )
    out, ele = pl.pallas_call(
        finish,
        out_shape=(
            jax.ShapeDtypeStruct((2, NX, LANES), F32),
            jax.ShapeDtypeStruct((NX, LANES), F32),
        ),
        in_specs=[pl.BlockSpec(memory_space=pltpu.VMEM)] * 2,
        out_specs=(pl.BlockSpec(memory_space=pltpu.HBM),) * 2,
        scratch_shapes=[pltpu.SemaphoreType.DMA((2,))],
        compiler_params=pltpu.CompilerParams(vmem_limit_bytes=1024 * 1024),
        name="finish",
    )(out, ele)
    out = out.reshape(2, 16, RADIX, 2, LANES).transpose(0, 1, 3, 2, 4).reshape(2, 16, 2, NY)
    ele = ele.reshape(16, RADIX, 2, LANES).transpose(0, 2, 1, 3).reshape(16, 2, NY)
    return out, ele


def solution(mesh):
    placed = (P(None, "trans", "tm", None), P(), P(), P())
    return jax.shard_map(
        local,
        mesh=mesh,
        in_specs=placed,
        out_specs=(P(None, "trans", "tm", None), P("trans", "tm", None)),
        check_vma=False,
    )
```

```python
import functools
import math

import jax
import jax.numpy as jnp
import numpy as np
from jax import lax
from jax.experimental import pallas as pl
from jax.experimental.pallas import tpu as pltpu
from jax.sharding import PartitionSpec as P

RATE_COEF = 1.8e-08
RECOMB = 0.02
KERR_COEF = 0.3
PLASMA = 4.0

N = 16
LANES = 128
GROUP = 4
TEAM = N * GROUP
NX = 256
NY = 1024
RADIX = 8

F32 = jnp.float32
MESH = pl.DeviceIdType.MESH
ROOT_HALF = math.sqrt(0.5)


FAR_FIRST = sorted(
    (
        (dy, dx, dz, dc)
        for dy in range(4)
        for dx in range(4)
        for dz in range(2)
        for dc in range(2)
        if dy or dx or dz or dc
    ),
    key=lambda d: -(min(d[0], 4 - d[0]) + min(d[1], 4 - d[1]) + d[2]) - 0.1 * d[3],
)

NEARNESS = ((2,), (1,), (3,), (0,))


def tables():
    j = np.arange(NX)
    angle = 2.0 * np.pi * ((j[:, None] * j[None, :]) % NX) / NX
    table_x = np.concatenate([np.cos(angle), np.sin(angle)], axis=1)
    b = np.arange(LANES)
    angle = 2.0 * np.pi * ((b[:, None] * b[None, :]) % LANES) / LANES
    c, s = np.cos(angle), np.sin(angle)
    forward = np.block([[c, -s], [s, c]])
    backward = np.block([[c, s], [-s, c]])
    k = np.arange(RADIX)
    angle = 2.0 * np.pi * (k[:, None] * b[None, :]) / NY
    twist = np.stack([np.cos(angle), np.sin(angle)])
    spread = (b[None, :] % 16 == b[:, None] // RADIX).astype(np.float32)
    return [np.asarray(t, np.float32) for t in (table_x, forward, backward, twist, spread)]


def sincos(x):
    n = jnp.floor(x * (2.0 / math.pi) + 0.5)
    r = x - n * 1.5703125
    r = r - n * 4.837512969970703125e-4
    r = r - n * 7.54978995489188216e-8
    z = r * r
    s = r + r * z * (-1.6666654611e-1 + z * (8.3321608736e-3 + z * -1.9515295891e-4))
    c = 1.0 - 0.5 * z + z * z * (
        4.166664568298827e-2 + z * (-1.388731625493765e-3 + z * 2.443315711809948e-5)
    )
    q = n.astype(jnp.int32)
    odd = (q & 1) == 1
    sin = jnp.where(odd, c, s)
    cos = jnp.where(odd, s, c)
    sin = jnp.where((q & 2) == 2, -sin, sin)
    cos = jnp.where(((q + 1) & 2) == 2, -cos, cos)
    return sin, cos


def dot(a, b):
    return lax.dot_general(
        a,
        b,
        (((1,), (0,)), ((), ())),
        precision=lax.Precision.HIGHEST,
        preferred_element_type=F32,
    )


def split(v, parts):
    out = []
    for _ in range(parts):
        out.append(v.astype(jnp.bfloat16))
        v = v - out[-1].astype(F32)
    return out


def dot_parts(a, b):
    total = None
    for order in range(len(a) - 1, -1, -1):
        for i in range(order + 1):
            term = lax.dot_general(
                a[i], b[order - i], (((1,), (0,)), ((), ())), preferred_element_type=F32
            )
            total = term if total is None else total + term
    return total


def cadd(a, b):
    return (a[0] + b[0], a[1] + b[1])


def csub(a, b):
    return (a[0] - b[0], a[1] - b[1])


def radix8(x, sign):
    def turn(v):
        return (-v[1], v[0]) if sign > 0 else (v[1], -v[0])

    def four(p, q, r, s):
        e0, e1, e2, e3 = cadd(p, r), csub(p, r), cadd(q, s), turn(csub(q, s))
        return cadd(e0, e2), cadd(e1, e3), csub(e0, e2), csub(e1, e3)

    e = four(x[0], x[2], x[4], x[6])
    o = four(x[1], x[3], x[5], x[7])
    t1, t3 = turn(o[1]), turn(o[3])
    w1 = ((o[1][0] + t1[0]) * ROOT_HALF, (o[1][1] + t1[1]) * ROOT_HALF)
    w3 = ((t3[0] - o[3][0]) * ROOT_HALF, (t3[1] - o[3][1]) * ROOT_HALF)
    o = (o[0], w1, turn(o[2]), w3)
    return [cadd(e[k], o[k]) for k in range(4)] + [csub(e[k], o[k]) for k in range(4)]


def roll(v, by, axis):
    return pltpu.roll(v, by % v.shape[axis], axis)


def transpose_lanes(blocks, width):
    blocks = list(blocks)
    group = lax.broadcasted_iota(jnp.int32, (8, LANES), 1) // width
    bit = len(blocks) // 2
    while bit:
        clear = lax.rem(group // bit, 2) == 0
        for u in range(len(blocks)):
            if u & bit == 0:
                p, q = blocks[u], blocks[u | bit]
                blocks[u] = jnp.where(clear, p, roll(q, bit * width, 1))
                blocks[u | bit] = jnp.where(clear, roll(p, -bit * width, 1), q)
        bit //= 2
    return blocks


def spread_lanes(v):
    group = lax.broadcasted_iota(jnp.int32, (8, LANES), 1) // 16
    out = [v]
    for bit in (4, 2, 1):
        clear = lax.rem(group // bit, 2) == 0
        nxt = []
        for x in out:
            nxt.append(jnp.where(clear, x, roll(x, 16 * bit, 1)))
            nxt.append(jnp.where(clear, roll(x, -16 * bit, 1), x))
        out = nxt
    return out


def rates(re, im, dens):
    intensity = re * re + im * im
    power = intensity * intensity
    power = power * power
    power = power * power
    rate = RATE_COEF * power
    lost = rate + RECOMB
    decays = jnp.exp(-lost)
    source = (1.0 - decays) * dens * (rate / lost)
    return intensity, decays, source


def kernel(
    field_hbm, dens_hbm, phx_hbm, phy_hbm, tx_hbm, wf_hbm, wb_hbm, tw_hbm, sp_hbm,
    out, ele,
    field, dens1, dens2, phx, phy, tx, wf, wb, tw, sp,
    stage, bmat, mmat, mmix, turns, densx, densy,
    mparts, xparts, wparts, send1, recv1, work, gain, phase0,
    send2, recv2, ent, send4, recv4, fold, dec, src, inten,
    sende, recve, send5, recv5, ent5, send6, recv6, pairmap,
    in_sems, ready, team_send, team_recv, map_send, map_recv, own_send, own_recv,
):
    tm = lax.axis_index("tm")
    trans = lax.axis_index("trans")
    g = tm // GROUP
    s = lax.rem(tm, GROUP)
    me = GROUP * trans + s

    barrier = pltpu.get_barrier_semaphore()

    ys = [GROUP * lax.rem(trans // 4 + d, 4) for d in range(4)]
    xs = [lax.rem(trans + d, 4) for d in range(4)]
    zs = [2 * lax.rem(s // 2 + d, 2) for d in range(2)]
    cs = [lax.rem(s + d, 2) for d in range(2)]
    mates = []
    for dy, dx, dz, dc in FAR_FIRST:
        other, slot = ys[dy] + xs[dx], zs[dz] + cs[dc]
        mates.append(((GROUP * g + slot, other), GROUP * other + slot))

    row0 = pl.multiple_of(trans * N, N)
    col0 = pl.multiple_of((me // 8) * LANES, LANES)
    loads = [
        pltpu.make_async_copy(a, b, in_sems.at[i])
        for i, (a, b) in enumerate(
            [
                (field_hbm, field),
                (tw_hbm, tw),
                (wf_hbm, wf),
                (phy_hbm, phy),
                (sp_hbm, sp),
                (wb_hbm, wb),
                (phx_hbm, phx),
                (tx_hbm, tx),
                (dens_hbm.at[:, pl.ds(col0, LANES)], dens1),
                (dens_hbm.at[pl.ds(row0, N), :], dens2),
            ]
        )
    ]
    for load in loads[:3]:
        load.start()
    for where_to, _ in mates:
        pl.semaphore_signal(barrier, inc=1, device_id=where_to, device_id_type=MESH)
    for load in loads[3:]:
        load.start()
    for later in range(1, GROUP):

        @pl.when(g + later < GROUP)
        def _():
            pl.semaphore_signal(
                barrier, inc=1, device_id=(tm + GROUP * later, trans), device_id_type=MESH
            )

    def exchange(src_ref, dst_ref, phase, near):
        for offsets, (where_to, slot) in zip(FAR_FIRST, mates):
            if offsets[0] not in near:
                continue
            pltpu.make_async_remote_copy(
                src_ref=src_ref.at[slot],
                dst_ref=dst_ref.at[me],
                send_sem=team_send.at[phase],
                recv_sem=team_recv.at[phase],
                device_id=where_to,
                device_id_type=MESH,
            ).start()

    def whole(ref, sem, count):
        part = ref.at[pl.ds(0, count)]
        pltpu.make_async_copy(part, part, sem).wait()

    def send_map(src_ref, dst_ref, phase, chunk):
        for later in range(1, GROUP):

            @pl.when(g + later < GROUP)
            def _():
                pltpu.make_async_remote_copy(
                    src_ref=src_ref.at[chunk],
                    dst_ref=dst_ref.at[g, chunk],
                    send_sem=map_send.at[phase],
                    recv_sem=map_recv.at[phase, g],
                    device_id=(tm + GROUP * later, trans),
                    device_id_type=MESH,
                ).start()

    def enter(dst_ref, phase, total):
        total[...] = jnp.zeros_like(total)
        for k in range(GROUP - 1):

            @pl.when(k < g)
            def _():
                pltpu.make_async_copy(dst_ref.at[k], dst_ref.at[k], map_recv.at[phase, k]).wait()
                for chunk in range(4):
                    total[chunk] = dst_ref[k, chunk, 0] * total[chunk] + dst_ref[k, chunk, 1]

    def send_own(src_ref, dst_ref, phase):
        for dz, dc in ((1, 1), (1, 0), (0, 1)):
            i = zs[dz] + cs[dc]
            pltpu.make_async_remote_copy(
                src_ref=src_ref.at[i],
                dst_ref=dst_ref.at[s],
                send_sem=own_send.at[phase],
                recv_sem=own_recv.at[phase, s],
                device_id=(GROUP * g + i, trans),
                device_id_type=MESH,
            ).start()

    lane = lax.broadcasted_iota(jnp.int32, (8, LANES), 1)
    sub = lax.broadcasted_iota(jnp.int32, (8, LANES), 0)
    group = lane // 16
    top = sub < 4

    def flip(v):
        return roll(v, 4, 0)

    def spectral(ahead, behind):
        freq = ahead(stage[...])
        for k in range(RADIX):
            rows = slice(32 * k, 32 * k + 32)
            re, im = freq[rows, :LANES], freq[rows, LANES:]
            pr, pi = turns[1, k : k + 1, :], turns[0, k : k + 1, :]
            stage[rows, :LANES] = re * pr - im * pi
            stage[rows, LANES:] = re * pi + im * pr
        stage[...] = behind(stage[...])

    def forward(blocks, w):
        for k, (re, im) in enumerate(radix8(blocks, -1)):
            rows = slice(32 * k + 8 * w, 32 * k + 8 * w + 8)
            c, d = tw[0, k : k + 1, :], tw[1, k : k + 1, :]
            stage[rows, :LANES] = re * c + im * d
            stage[rows, LANES:] = im * c - re * d

    def back(w):
        parts = []
        for k in range(RADIX):
            rows = slice(32 * k + 8 * w, 32 * k + 8 * w + 8)
            re, im = stage[rows, :LANES], stage[rows, LANES:]
            c, d = tw[0, k : k + 1, :], tw[1, k : k + 1, :]
            parts.append((re * c - im * d, im * c + re * d))
        return radix8(parts, 1)

    loads[0].wait()
    loads[1].wait()
    for xh in range(2):
        for t in range(2):
            forward(
                [
                    tuple(field[c, pl.ds(128 * xh + 2 * a + t, 8, stride=16), :] for c in range(2))
                    for a in range(RADIX)
                ],
                2 * xh + t,
            )
    for load in loads[2:6]:
        load.wait()
    picked = jnp.concatenate(
        [jnp.where(lane % RADIX == sub, phy[r : r + 1, :], 0.0) for r in range(RADIX)], axis=0
    )
    picked = dot(picked, sp[...])
    phase = jnp.zeros((8, LANES), F32)
    for r in range(RADIX):
        phase = jnp.where(group == r, picked[8 * r : 8 * r + 8, :], phase)
    sin, cos = sincos(phase)
    turns[0] = sin * (1.0 / NY)
    turns[1] = cos * (1.0 / NY)
    spectral(lambda v: dot(v, wf[...]), lambda v: dot(v, wb[...]))
    parts = [back(w) for w in range(4)]
    for a in range(RADIX):
        mixed = transpose_lanes(
            [parts[2 * xh + t][a][c] for xh in range(2) for c in range(2) for t in range(2)], 16
        )
        for j in range(8):
            send1[8 * a + j] = mixed[j]

    pl.semaphore_wait(barrier, TEAM - 1 + g)
    exchange(send1, recv1, 0, range(4))
    recv1[me] = send1[me]
    for k in range(GROUP - 1):

        @pl.when(k < g)
        def _():
            pl.semaphore_signal(
                ready, inc=1, device_id=(GROUP * k + s, trans), device_id_type=MESH
            )

    for load in loads[6:]:
        load.wait()
    sin, cos = sincos(phx[...])
    sin, cos = sin * (1.0 / NX), cos * (1.0 / NX)
    cx, sx = tx[:, :NX], tx[:, NX:]
    bmat[:NX, :] = cx * cos - sx * sin
    bmat[NX:, :] = cx * sin + sx * cos
    both = dot(bmat[...], tx[...])
    mmat[:NX, :] = both[:NX, :NX] + both[NX:, NX:]
    mmat[NX:, :] = both[NX:, :NX] - both[:NX, NX:]
    for m in range(NX // 8):
        for half in range(2):
            cols = slice(LANES * half, LANES * (half + 1))
            re, im = mmat[8 * m : 8 * m + 8, cols], mmat[NX + 8 * m : NX + 8 * m + 8, cols]
            mmix[16 * m : 16 * m + 8, cols] = jnp.where(top, re, flip(im))
            mmix[16 * m + 8 : 16 * m + 16, cols] = jnp.where(top, flip(re), im)
    for target, parts in (
        (mparts, split(mmat[...], 3)),
        (xparts, split(mmix[...], 2)),
        (wparts.at[0], split(wf[...], 2)),
        (wparts.at[1], split(wb[...], 2)),
    ):
        for i, part in enumerate(parts):
            target[i] = part
    mine = group == lax.rem(me, 8)
    for m in range(NX // 8):
        rows = slice(8 * m, 8 * m + 8)
        v = jnp.where(mine, dens1[rows, :], 0.0)
        for shift in (16, 32, 64):
            v = v + roll(v, shift, 1)
        densx[rows, :] = v
    for k in range(GROUP):
        for r in range(4):
            line = dens2[4 * k + r : 4 * k + r + 1, :]
            densy[k, r : r + 1, :] = line
            densy[k, r + 4 : r + 5, :] = line

    whole(recv1, team_recv.at[0], TEAM - 1)
    for p in range(N):
        mixed = transpose_lanes([recv1[4 * p + k] for k in range(4)], 32)
        for xh in range(2):
            for c in range(2):
                work[c, 16 * p + 8 * xh : 16 * p + 8 * xh + 8, :] = mixed[2 * xh + c]
    fields = split(jnp.concatenate([work[0], work[1]], axis=1), 3)

    def along_x(chunk):
        both = dot_parts(
            [
                jnp.concatenate(
                    [mparts[i, n + 64 * chunk : n + 64 * chunk + 64, :] for n in (0, NX)], axis=0
                )
                for i in range(3)
            ],
            fields,
        )
        return both[:64, :LANES] - both[64:, LANES:], both[64:, :LANES] + both[:64, LANES:]

    ahead = along_x(0)
    for chunk in range(4):
        maps = [jnp.zeros((8, LANES), F32)] * 2
        re, im = ahead
        if chunk < 3:
            ahead = along_x(chunk + 1)
        for i in range(8):
            part = slice(8 * i, 8 * i + 8)
            rows = slice(64 * chunk + 8 * i, 64 * chunk + 8 * i + 8)
            work[0, rows, :] = re[part]
            work[1, rows, :] = im[part]
            intensity, grow, add = rates(re[part], im[part], densx[rows, :])
            for bit in (1, 2, 4):
                there = group >= bit
                grow2, add2 = roll(grow, 16 * bit, 1), roll(add, 16 * bit, 1)
                add = jnp.where(there, grow * add2 + add, add)
                grow = jnp.where(there, grow * grow2, grow)
            phase0[rows, :] = KERR_COEF * intensity - PLASMA * add
            gain[rows, :] = PLASMA * grow
            maps = [
                jnp.where(group == i, roll(v, 16 * (i + 1), 1), old)
                for v, old in zip((grow, add), maps)
            ]
        if chunk == 0:

            @pl.when(g < GROUP - 1)
            def _():
                pl.semaphore_wait(ready, GROUP - 1 - g)

        send2[chunk, 0] = maps[0]
        send2[chunk, 1] = maps[1]
        send_map(send2, recv2, 0, chunk)
    enter(recv2, 0, ent)
    for chunk in range(4):
        for i, entering in enumerate(spread_lanes(ent[chunk])):
            rows = slice(64 * chunk + 8 * i, 64 * chunk + 8 * i + 8)
            sin, cos = sincos(phase0[rows, :] - gain[rows, :] * entering)
            re, im = work[0, rows, :], work[1, rows, :]
            work[0, rows, :] = re * cos - im * sin
            work[1, rows, :] = re * sin + im * cos

    fields = split(jnp.concatenate([work[0], work[1]], axis=1), 2)
    for near in NEARNESS:
        both = dot_parts(
            [
                jnp.concatenate(
                    [
                        xparts[i, pl.ds(pl.multiple_of(32 * ys[dy], 128), 128), :]
                        for dy in near
                    ],
                    axis=0,
                )
                for i in range(2)
            ],
            fields,
        )
        for n, dy in enumerate(near):
            for k in range(16):
                rows = slice(128 * n + 8 * k, 128 * n + 8 * k + 8)
                turned = flip(both[rows, LANES:])
                send4[GROUP * ys[dy] + k] = both[rows, :LANES] + jnp.where(top, -turned, turned)
        exchange(send4, recv4, 1, near)
    recv4[me] = send4[me]
    whole(recv4, team_recv.at[1], TEAM - 1)

    for a in range(RADIX):
        times = transpose_lanes([recv4[8 * a + j] for j in range(8)], 16)
        for i in range(4):
            u, v = times[2 * i], times[2 * i + 1]
            fold[i, a, 0] = jnp.where(top, u, flip(v))
            fold[i, a, 1] = jnp.where(top, flip(u), v)
    for i in range(4):
        forward([(fold[i, a, 0], fold[i, a, 1]) for a in range(RADIX)], i)
    spectral(
        *(lambda v, i=i: dot_parts(split(v, 2), [wparts[i, 0], wparts[i, 1]]) for i in range(2))
    )
    maps = [None] * 4
    for i in range(4):
        fields = back(i)
        pairs = []
        for a in range(RADIX):
            re, im = fields[a]
            sende[i, a, 0] = re
            sende[i, a, 1] = im
            _, decays, source = rates(re, im, densy[s, :, LANES * a : LANES * (a + 1)])
            pairs.append((decays * flip(decays), decays * flip(source) + source))
        for h in range(4):
            even, odd = pairs[2 * h], pairs[2 * h + 1]
            grow = jnp.where(top, even[0], odd[0])
            add = jnp.where(top, flip(even[1]), odd[1])
            pairmap[i, h, 0] = grow
            pairmap[i, h, 1] = add
            if maps[h] is not None:
                grow, add = grow * maps[h][0], grow * maps[h][1] + add
            maps[h] = (grow, add)
    for h in range(4):
        send5[h, 0] = maps[h][0]
        send5[h, 1] = maps[h][1]
        send_map(send5, recv5, 1, h)
    send_own(sende, recve, 0)
    recve[s] = sende[s]

    def own_rates(step):
        k = lax.rem(s + step, GROUP)
        if step:
            pltpu.make_async_copy(recve.at[k], recve.at[k], own_recv.at[0, k]).wait()
        for a in range(RADIX):
            intensity, decays, source = rates(
                recve[k, a, 0], recve[k, a, 1], densy[k, :, LANES * a : LANES * (a + 1)]
            )
            inten[step, a] = KERR_COEF * intensity
            dec[step, a] = jnp.where(top, decays, decays * flip(decays))
            src[step, a] = jnp.where(top, source, decays * flip(source) + source)

    own_rates(0)
    enter(recv5, 1, ent5)
    for i in range(GROUP):
        for h in range(4):
            if i == 0:
                send6[0, h] = ent5[h]
            else:
                send6[i, h] = pairmap[i - 1, h, 0] * send6[i - 1, h] + pairmap[i - 1, h, 1]
    send_own(send6, recv6, 1)
    recv6[s] = send6[s]

    for step in range(1, GROUP):
        own_rates(step)
    for step in range(GROUP):
        k = lax.rem(s + step, GROUP)
        if step:
            pltpu.make_async_copy(recv6.at[k], recv6.at[k], own_recv.at[1, k]).wait()
        for a in range(RADIX):
            packed = recv6[k, a // 2]
            turned = flip(packed)
            pair = (packed, turned) if a % 2 == 0 else (turned, packed)
            electrons = dec[step, a] * jnp.where(top, *pair) + src[step, a]
            sin, cos = sincos(inten[step, a] - PLASMA * electrons)
            re, im = recve[k, a, 0], recve[k, a, 1]
            new_re, new_im = re * cos - im * sin, re * sin + im * cos
            for t in range(2):
                rows = pl.ds(64 * k + 2 * a + t, 4, stride=16)
                part = slice(4 * t, 4 * t + 4)
                out[0, rows, :] = new_re[part]
                out[1, rows, :] = new_im[part]
                ele[rows, :] = electrons[part]

    whole(send1, team_send.at[0], TEAM - 1)
    whole(send4, team_send.at[1], TEAM - 1)
    whole(sende, own_send.at[0], GROUP - 1)
    whole(send6, own_send.at[1], GROUP - 1)
    for later in range(1, GROUP):

        @pl.when(g + later < GROUP)
        def _():
            for phase_index, ref in enumerate((send2, send5)):
                whole(ref, map_send.at[phase_index], 4)


def finish(a, b, c, d, sems):
    copies = [
        pltpu.make_async_copy(x, y, sems.at[i]) for i, (x, y) in enumerate([(a, c), (b, d)])
    ]
    for copy in copies:
        copy.start()
    for copy in copies:
        copy.wait()


def local(light_field, gas_density, phase_x, phase_y):
    consts = tables()
    rows = light_field.reshape(2, 16, 2, RADIX, LANES).transpose(0, 1, 3, 2, 4).reshape(2, NX, LANES)
    vmem = lambda *shape: pltpu.VMEM(shape, F32)
    team = vmem(TEAM, 8, LANES)
    chunks = vmem(4, 2, 8, LANES)
    incoming = vmem(GROUP - 1, 4, 2, 8, LANES)
    tall = vmem(4, RADIX, 8, LANES)
    short = vmem(4, 4, 8, LANES)
    fields = vmem(4, RADIX, 2, 8, LANES)
    plane = vmem(NX, LANES)
    out, ele = pl.pallas_call(
        kernel,
        out_shape=(
            jax.ShapeDtypeStruct((2, NX, LANES), F32),
            jax.ShapeDtypeStruct((NX, LANES), F32),
        ),
        in_specs=[pl.BlockSpec(memory_space=pltpu.HBM)] * 9,
        out_specs=(pl.BlockSpec(memory_space=pltpu.VMEM),) * 2,
        scratch_shapes=[
            vmem(2, NX, LANES), plane, vmem(16, NY), vmem(1, NX), vmem(8, LANES),
            vmem(NX, 2 * NX), vmem(NX, NX), vmem(NX, NX), vmem(2, 8, LANES), vmem(LANES, LANES),
            vmem(NX, NX), vmem(2 * NX, NX), vmem(2 * NX, NX), vmem(2 * NX, NX),
            vmem(2, 8, LANES), plane, vmem(GROUP, 8, NY),
            pltpu.VMEM((3, 2 * NX, NX), jnp.bfloat16),
            pltpu.VMEM((2, 2 * NX, NX), jnp.bfloat16),
            pltpu.VMEM((2, 2, NX, NX), jnp.bfloat16),
            team, team, vmem(2, NX, LANES), plane, plane,
            chunks, incoming, vmem(4, 8, LANES), team, team, fields, tall, tall, tall,
            fields, fields, chunks, incoming, vmem(4, 8, LANES), short, short,
            vmem(4, 4, 2, 8, LANES),
            pltpu.SemaphoreType.DMA((10,)),
            pltpu.SemaphoreType.REGULAR,
            pltpu.SemaphoreType.DMA((2,)),
            pltpu.SemaphoreType.DMA((2,)),
            pltpu.SemaphoreType.DMA((2,)),
            pltpu.SemaphoreType.DMA((2, GROUP - 1)),
            pltpu.SemaphoreType.DMA((2,)),
            pltpu.SemaphoreType.DMA((2, GROUP)),
        ],
        compiler_params=pltpu.CompilerParams(
            collective_id=0, has_side_effects=True, vmem_limit_bytes=24 * 1024 * 1024
        ),
        name="split_step",
    )(
        *(
            pltpu.with_memory_space_constraint(array, pltpu.HBM)
            for array in (
                rows, gas_density, phase_x.reshape(1, NX), phase_y.reshape(RADIX, LANES), *consts
            )
        )
    )
    out, ele = pl.pallas_call(
        finish,
        out_shape=(
            jax.ShapeDtypeStruct((2, NX, LANES), F32),
            jax.ShapeDtypeStruct((NX, LANES), F32),
        ),
        in_specs=[pl.BlockSpec(memory_space=pltpu.VMEM)] * 2,
        out_specs=(pl.BlockSpec(memory_space=pltpu.HBM),) * 2,
        scratch_shapes=[pltpu.SemaphoreType.DMA((2,))],
        compiler_params=pltpu.CompilerParams(vmem_limit_bytes=1024 * 1024),
        name="finish",
    )(out, ele)
    out = out.reshape(2, 16, RADIX, 2, LANES).transpose(0, 1, 3, 2, 4).reshape(2, 16, 2, NY)
    ele = ele.reshape(16, RADIX, 2, LANES).transpose(0, 2, 1, 3).reshape(16, 2, NY)
    return out, ele


def solution(mesh):
    placed = (P(None, "trans", "tm", None), P(), P(), P())
    return jax.shard_map(
        local,
        mesh=mesh,
        in_specs=placed,
        out_specs=(P(None, "trans", "tm", None), P("trans", "tm", None)),
        check_vma=False,
    )
```
